256 devices in a mesh: sta: 32 (over z, y), seg: 8 (over x, core).
Axes of the slice: x: 4, y: 4, z: 8, core: 2. Of those that a mesh axis runs over, the one named last changes fastest.
Arguments:
- records: bfloat16 [512, 16384], P('sta', 'seg'), may hold values from -300 to 300, as said below
- owners: int32 [256, 4], P('sta'), may hold values from 0 to 31, all different within a row; in each aligned block of 8 rows (0 to 7, 8 to 15, ...) at most 2 rows name the same one
Outputs:
- whitened: bfloat16 [512, 16384], P('sta', 'seg')
- correlations: bfloat16 [128, 512, 512], P('seg', 'sta')
The draws below stay inside these ranges and needn't reach their ends.
Inputs may be any that keep to these rules, and one draw needn't show every extreme that they name: Each row names 4 different owners; among the 8 blocks of one index of sta no owner is named more than 2 times, some owner is named exactly 2 times, and every owner is named by some block. Real-valued records.
All inputs are finite; a program needn't handle non-finite values.
Results may differ from the reference program's by a relative error of at most 0.017.
Values may be sent and summed in bfloat16 or wider, within the bound.
No kernel may reach another device: no remote copies, remote signals or barrier semaphores. Data moves between devices by JAX's collectives and lax.ppermute only.
A program may use at most 128 MiB of HBM per device.

```python
import math
import jax
import jax.numpy as jnp
import numpy as np
from jax import lax

STA_DEV = 16
SEG = 2048
LAGS = 512
BS = 2
DESTS = 4
BPD = 8
CAP = 2
R = 128
S = 512
NBLK = 256
WINDOW = 16384
N_STA = 32
N_SEG = 8


def draw_records(key, part):
    key_list = jax.random.split(key, 4)
    array_shape = (S, WINDOW)
    noise_base = jnp.clip(jax.random.normal(key_list[0], array_shape, jnp.float32), -5.0, 5.0)
    station_gain = jnp.exp(jax.random.uniform(key_list[2], (S, 1), jnp.float32, 0.0, math.log(10.0)))
    piece_gain = jnp.exp(jax.random.uniform(key_list[3], (S, WINDOW // 64), jnp.float32, math.log(0.5), math.log(2.0)))
    piece_gain = jnp.repeat(piece_gain, 64, axis=1)
    time_ramp = jnp.exp(math.log(3.0) * jnp.arange(WINDOW, dtype=jnp.float32) / WINDOW)
    return (noise_base * station_gain * piece_gain * time_ramp[None, :]).astype(jnp.bfloat16)


def assign_block(own_key, own, number, rows, amount, top, limit, lean):
    order = jax.random.permutation(own_key, amount)
    crowded, ordinary = portions_of(amount, rows * top, limit, lean, True), portions_of(amount, rows * top, limit, lean, False)
    places = jnp.arange(amount)

    def named(tallies, offset_by):
        used = int((tallies > 0).sum())
        fixed = max(1, used // 4)
        shifted = fixed + (places - fixed + offset_by * (used - fixed)) % max(1, amount - fixed)
        return jnp.zeros((amount,), jnp.int32).at[order[jnp.where(places < fixed, places, shifted)]].set(jnp.asarray(tallies, jnp.int32))

    tallies = jnp.where(number % 4 == 0, named(crowded, number // 4), named(ordinary, number - number // 4 - 1))
    mixed = jax.random.permutation(jax.random.fold_in(own, 3), amount)
    source_of, taker = mixed[0:amount // 2 * 2:2], mixed[1:amount // 2 * 2:2]
    slack = jnp.minimum(tallies[source_of] - 1, limit - tallies[taker]) // 2
    slack = jnp.where((source_of == order[0]) | (taker == order[0]) | (tallies[taker] == 0), 0, jnp.maximum(slack, 0))
    shifted = jax.random.randint(jax.random.fold_in(own, 4), (amount // 2,), 0, 1 << 20) % (slack + 1)
    tallies = tallies.at[source_of].add(-shifted).at[taker].add(shifted)
    items = jnp.searchsorted(jnp.cumsum(tallies), jnp.arange(rows * top), side="right").astype(jnp.int32)
    grid = items.reshape(top, rows).T
    grid = grid[jax.random.permutation(jax.random.fold_in(own, 1), rows)]
    offset_by = jax.random.randint(jax.random.fold_in(own, 2), (rows, 1), 0, top)
    return jnp.take_along_axis(grid, (jnp.arange(top)[None, :] + offset_by) % top, axis=1)


def portions_of(count, total, limit, skew, full):
    weights = [(1 << 20) // math.isqrt(rank ** skew) + 1 for rank in range(1, count + 1)]
    largest = limit if full else min(limit, max(-(-total // count), total * weights[0] // sum(weights)))
    least = 1 if total - largest >= count - 1 else 0
    holding, spare = [largest] + [least] * (count - 1), total - largest - least * (count - 1)
    while spare > 0:
        movable = [i for i in range(1, count) if holding[i] < largest] or [i for i in range(1, count) if holding[i] < limit]
        pool, budget = sum([weights[i] for i in movable]), spare
        for i in movable:
            addition = min(limit - holding[i], max(1, budget * weights[i] // pool), spare)
            holding[i] = holding[i] + addition
            spare = spare - addition
    return np.array(holding)


def setup_inputs(seed: int = 0) -> dict:
    streams_of = jax.random.split(jax.random.key(seed), 3)
    records = draw_records(jax.random.fold_in(streams_of[2], 71), 0)
    owners_keys = jax.random.split(jax.random.fold_in(streams_of[1], 1), NBLK // BPD)
    owners_turns = jax.random.permutation(jax.random.fold_in(streams_of[1], 3), NBLK // BPD)
    owners = jax.vmap(lambda own, number: assign_block(jax.random.fold_in(streams_of[1], 2), own, number, BPD, N_STA, DESTS, CAP, 2))(owners_keys, owners_turns).reshape((NBLK, DESTS))
    return {"records": records, "owners": owners}


WATER = 0.5
EPSILON = 1e-06

def make_table(length):
    sample_ids = jnp.arange(length, dtype=jnp.int32)
    product = sample_ids[:, None] * sample_ids[None, :] % length
    angles = product.astype(jnp.float32) * (2.0 * math.pi / length)
    return jnp.concatenate([jnp.cos(angles), jnp.sin(angles)], axis=1).astype(jnp.bfloat16)

def reference(records, owners):
    dft_table = make_table(SEG)
    seg_rows = records.reshape(S * N_SEG, SEG)
    spectrum = jnp.dot(seg_rows, dft_table, preferred_element_type=jnp.float32)
    real_part = spectrum[:, :SEG]
    imag_part = spectrum[:, SEG:]
    magnitude = jnp.sqrt(real_part * real_part + imag_part * imag_part)
    amp_total = lax.optimization_barrier(jnp.sum(magnitude.reshape(S, N_SEG * SEG), axis=1))
    water_level = WATER * amp_total / WINDOW + EPSILON
    level_rows = jnp.repeat(water_level, N_SEG)[:, None]
    flattened = (spectrum / (jnp.concatenate([magnitude, magnitude], axis=1) + level_rows)).astype(jnp.bfloat16)
    white_trace = lax.dot_general(flattened, dft_table, (((1,), (1,)), ((), ())), preferred_element_type=jnp.float32) * (1.0 / SEG)
    white_trace = white_trace.reshape(S, WINDOW)
    energy = lax.optimization_barrier(jnp.sum(white_trace * white_trace, axis=1))
    whitened = (white_trace * lax.rsqrt(energy / WINDOW + EPSILON)[:, None]).astype(jnp.bfloat16)
    series = whitened.astype(jnp.float32)
    half_lags = LAGS // 2
    fft_len = 1 << (SEG + LAGS - 1).bit_length()
    padded_series = jnp.pad(series, ((0, 0), (half_lags, half_lags)))
    window_index = (np.arange(N_SEG) * SEG)[:, None] + np.arange(SEG + LAGS)[None, :]
    own_windows = padded_series[:, window_index]
    own_spectra = jnp.fft.rfft(own_windows, n=fft_len, axis=-1)
    seg_spectra = jnp.fft.rfft(series.reshape(S, N_SEG, SEG), n=fft_len, axis=-1)
    spec_real = jnp.real(seg_spectra).reshape(N_STA, BPD, BS, N_SEG, -1)
    spec_imag = jnp.imag(seg_spectra).reshape(N_STA, BPD, BS, N_SEG, -1)
    owner_ids = jnp.arange(N_STA, dtype=jnp.int32)
    wanted = jnp.any(owners[:, :, None] == owner_ids[None, None, :], axis=1).reshape(N_STA, BPD, N_STA)
    wanted_count = wanted.astype(jnp.int32)
    slot_rank = jnp.cumsum(wanted_count, axis=1) - wanted_count
    slot_ids = jnp.arange(CAP, dtype=jnp.int32)
    lag_index = np.arange(LAGS, 0, -1)
    corr_scale = 1.0 / math.sqrt(WINDOW)

    def one_owner(owner):
        chosen = wanted[:, :, owner]
        ranks = slot_rank[:, :, owner]
        selector = (chosen[:, None, :] & (ranks[:, None, :] == slot_ids[None, :, None])).astype(jnp.float32)
        recv_real = jnp.einsum('sqj,sjbgf->sqbgf', selector, spec_real, precision=lax.Precision.HIGHEST).reshape(R, N_SEG, -1)
        recv_imag = jnp.einsum('sqj,sjbgf->sqbgf', selector, spec_imag, precision=lax.Precision.HIGHEST).reshape(R, N_SEG, -1)
        own_part = lax.dynamic_slice_in_dim(own_spectra, owner * STA_DEV, STA_DEV, 0)

        def one_segment(carry, seg_id):
            real_seg = lax.dynamic_index_in_dim(recv_real, seg_id, 1, False)
            imag_seg = lax.dynamic_index_in_dim(recv_imag, seg_id, 1, False)
            conj_recv = real_seg - 1j * imag_seg
            own_seg = lax.dynamic_index_in_dim(own_part, seg_id, 1, False)
            cross = conj_recv[:, None, :] * own_seg[None, :, :]
            lagged = jnp.fft.irfft(cross, n=fft_len, axis=-1)[:, :, lag_index] * corr_scale
            rounded = lax.optimization_barrier(lagged.astype(jnp.bfloat16)).astype(jnp.float32)
            return (carry + rounded, None)
        summed, unused = lax.scan(one_segment, jnp.zeros((R, STA_DEV, LAGS), jnp.float32), jnp.arange(N_SEG, dtype=jnp.int32))
        return summed.astype(jnp.bfloat16)
    per_owner = lax.map(one_owner, owner_ids)
    correlations = jnp.transpose(per_owner, (1, 0, 2, 3)).reshape(R, S, LAGS)
    return (whitened, correlations)
```

```python
import math

import jax
import jax.numpy as jnp
from jax import lax
from jax.experimental import pallas as pl
from jax.experimental.pallas import tpu as pltpu
from jax.sharding import PartitionSpec as P

LAGS = 512
BS = 2
SLOTS = 2
WATER = 0.5
EPSILON = 1e-06

PH = 16
STEP = 16
F32 = jnp.float32
BF16 = jnp.bfloat16
MIB = 1 << 20


def dot(a, b):
    return lax.dot_general(a, b, (((1,), (0,)), ((), ())), preferred_element_type=F32)


def dot_t(a, b):
    return lax.dot_general(a, b, (((1,), (1,)), ((), ())), preferred_element_type=F32)


def cos_sin(phase, period):
    phase = phase & (period - 1)
    phase = jnp.where(phase >= period // 2, phase - period, phase)
    theta = phase.astype(F32) * (2.0 * math.pi / period)
    square = theta * theta
    cosine = jnp.full(theta.shape, 1.0 / math.factorial(20), F32)
    sine = jnp.full(theta.shape, 1.0 / math.factorial(21), F32)
    for n in range(9, -1, -1):
        cosine = (1.0 if n % 2 == 0 else -1.0) / math.factorial(2 * n) + square * cosine
        sine = (1.0 if n % 2 == 0 else -1.0) / math.factorial(2 * n + 1) + square * sine
    return cosine, sine * theta


def table_kernel(length, forward_ref, inverse_ref):
    half = length // 2
    per_phase = length // PH
    wide = 256

    def columns(ref, col, freq_in_rows, rows, cos_at, sin_at, transform):
        lane = lax.broadcasted_iota(jnp.int32, (STEP, wide), 1) + col
        row = lax.broadcasted_iota(jnp.int32, (STEP, wide), 0)
        other = transform(lane)
        cosine, sine = cos_sin(row * other, length)
        turn_cos, turn_sin = cos_sin(STEP * other, length)
        if freq_in_rows:
            special = row == 0
            alternate = jnp.where(other & 1 == 0, 1.0, -1.0)
        else:
            special = other == 0
            alternate = jnp.where(row & 1 == 0, 1.0, -1.0)

        def body(k, carry):
            cosine, sine = carry
            at = pl.multiple_of(k * STEP, STEP)
            ref_cos, ref_sin = cos_at(at), sin_at(at)
            patch = special & (k == 0) if freq_in_rows else special
            ref[ref_cos] = cosine.astype(BF16)
            ref[ref_sin] = jnp.where(patch, alternate, sine).astype(BF16)
            return (
                cosine * turn_cos - sine * turn_sin,
                sine * turn_cos + cosine * turn_sin,
            )

        lax.fori_loop(0, rows // STEP, body, (cosine, sine), unroll=4)

    for c in range(half // wide):
        columns(
            forward_ref,
            c * wide,
            False,
            length,
            lambda at, c=c: (pl.ds(at, STEP), pl.ds(c * wide, wide)),
            lambda at, c=c: (pl.ds(at, STEP), pl.ds(half + c * wide, wide)),
            lambda lane: lane,
        )
    for c in range(length // wide):
        columns(
            inverse_ref,
            c * wide,
            True,
            half,
            lambda at, c=c: (pl.ds(at, STEP), pl.ds(c * wide, wide)),
            lambda at, c=c: (pl.ds(pl.multiple_of(half + at, STEP), STEP), pl.ds(c * wide, wide)),
            lambda lane: PH * (lane & (per_phase - 1)) + lane // per_phase,
        )


def make_tables(length):
    shape = jax.ShapeDtypeStruct((length, length), BF16)
    return pl.pallas_call(
        lambda *refs: table_kernel(length, *refs),
        out_shape=(shape, shape),
        in_specs=[],
        out_specs=[pl.BlockSpec(memory_space=pltpu.VMEM)] * 2,
        compiler_params=pltpu.CompilerParams(vmem_limit_bytes=24 * MIB),
        cost_estimate=pl.CostEstimate(
            flops=16 * length * length, bytes_accessed=4 * length * length, transcendentals=0
        ),
        name="tables",
    )()


def slots_kernel(owner_count, records_ref, owners_ref, out_ref):
    stations = records_ref.shape[0]
    blocks, dests = owners_ref.shape
    per_owner = SLOTS * BS
    rows = owner_count * per_owner
    k_of = lax.broadcasted_iota(jnp.int32, (blocks, stations), 0)
    station = lax.broadcasted_iota(jnp.int32, (blocks, stations), 1)
    expand = jnp.where(station // BS == k_of, 1.0, 0.0)
    named = lax.dot_general(
        owners_ref[...].astype(F32), expand, (((0,), (0,)), ((), ())), preferred_element_type=F32
    )
    row = lax.broadcasted_iota(jnp.int32, (rows, stations), 0)
    col = lax.broadcasted_iota(jnp.int32, (rows, stations), 1)
    owner = (row // per_owner).astype(F32)
    wanted = jnp.zeros((rows, stations), F32)
    for d in range(dests):
        wanted = jnp.maximum(wanted, jnp.where(named[d : d + 1, :] == owner, 1.0, 0.0))
    lower = lax.broadcasted_iota(jnp.int32, (stations, stations), 0)
    upper = lax.broadcasted_iota(jnp.int32, (stations, stations), 1)
    earlier = jnp.where((lower // BS < upper // BS) & (lower % BS == 0), 1.0, 0.0)
    rank = dot(wanted.astype(BF16), earlier.astype(BF16))
    slot = (row // BS % SLOTS).astype(F32)
    select = jnp.where((rank == slot) & (row % BS == col % BS), wanted, 0.0).astype(BF16)
    out_ref[...] = dot(select, records_ref[...]).astype(BF16)


def fill_slots(records, owners, owner_count):
    stations, length = records.shape
    rows = owner_count * SLOTS * BS
    return pl.pallas_call(
        lambda *refs: slots_kernel(owner_count, *refs),
        out_shape=jax.ShapeDtypeStruct((rows, length), BF16),
        in_specs=[pl.BlockSpec(memory_space=pltpu.VMEM)] * 2,
        out_specs=pl.BlockSpec(memory_space=pltpu.VMEM),
        compiler_params=pltpu.CompilerParams(vmem_limit_bytes=8 * MIB),
        cost_estimate=pl.CostEstimate(
            flops=2 * rows * stations * length, bytes_accessed=2 * rows * length, transcendentals=0
        ),
        name="slots",
    )(records, owners)


def seg_total(column, segs):
    rows = column.shape[0] // segs
    total = column[:rows]
    for s in range(1, segs):
        total = total + column[s * rows : (s + 1) * rows]
    return jnp.concatenate([total] * segs, axis=0)


def flatten(x_ref, forward_ref, re_ref, im_ref, mag_ref, flat_ref, segs):
    rows, length = x_ref.shape
    half = length // 2
    window = length * segs
    wide = 256
    lane = lax.broadcasted_iota(jnp.int32, (rows, wide), 1)

    total = jnp.zeros((rows, wide), F32)
    for c in range(half // wide):
        cols = pl.ds(c * wide, wide)
        re = dot(x_ref[...], forward_ref[:, c * wide : (c + 1) * wide])
        im = dot(x_ref[...], forward_ref[:, half + c * wide : half + (c + 1) * wide])
        if c == 0:
            mag = jnp.where(lane == 0, jnp.abs(re), jnp.sqrt(re * re + im * im))
            total = total + jnp.where(lane == 0, 0.5 * (jnp.abs(re) + jnp.abs(im)), mag)
        else:
            mag = jnp.sqrt(re * re + im * im)
            total = total + mag
        re_ref[:, cols] = re
        im_ref[:, cols] = im
        mag_ref[:, cols] = mag
    amp = seg_total(2.0 * jnp.sum(total, axis=1, keepdims=True), segs)
    level = WATER * amp / window + EPSILON
    for c in range(half // wide):
        cols = pl.ds(c * wide, wide)
        re, im, mag = re_ref[:, cols], im_ref[:, cols], mag_ref[:, cols]
        flat_re = re / (mag + level)
        if c == 0:
            im_mag = jnp.where(lane == 0, jnp.abs(im), mag)
            flat_im = im / (im_mag + level)
            weight = jnp.where(lane == 0, 1.0, 2.0)
        else:
            flat_im = im / (mag + level)
            weight = 2.0
        flat_ref[:, cols] = (flat_re * weight).astype(BF16)
        flat_ref[:, pl.ds(half + c * wide, wide)] = (flat_im * weight).astype(BF16)


def traces(flat_ref, inverse_ref, trace_ref, segs):
    rows, length = trace_ref.shape
    window = length * segs
    wide = 256
    total = jnp.zeros((rows, wide), F32)
    for c in range(length // wide):
        tr = dot(flat_ref[...], inverse_ref[:, c * wide : (c + 1) * wide]) * (1.0 / length)
        total = total + tr * tr
        trace_ref[:, pl.ds(c * wide, wide)] = tr
    energy = seg_total(jnp.sum(total, axis=1, keepdims=True), segs)
    return lax.rsqrt(energy / window + EPSILON)


def own_kernel(
    segs, x_ref, forward_ref, inverse_ref,
    white_ref, shifted_ref, extra_ref,
    re_ref, im_ref, mag_ref, flat_ref, trace_ref, phase_ref,
):
    rows, length = x_ref.shape
    stations = rows // segs
    per_phase = length // PH
    wide = 256
    flatten(x_ref, forward_ref, re_ref, im_ref, mag_ref, flat_ref, segs)
    scale = traces(flat_ref, inverse_ref, trace_ref, segs)
    mine = pl.multiple_of(lax.axis_index("seg") * stations, stations)
    my_flat = flat_ref[pl.ds(mine, stations), :]
    my_scale = scale[:stations]
    for c in range(length // wide):
        tr = dot_t(my_flat, forward_ref[c * wide : (c + 1) * wide, :]) * (1.0 / length)
        white_ref[:, pl.ds(c * wide, wide)] = (tr * my_scale).astype(BF16)
    for p in range(PH):
        for s in range(segs):
            tile = trace_ref[s * stations : (s + 1) * stations, p * per_phase : (p + 1) * per_phase]
            phase_ref[s, (PH - 1 - p) * stations : (PH - p) * stations, :] = (
                (tile * my_scale).astype(BF16).astype(F32)
            )
    count = LAGS // PH
    total = segs * per_phase
    lane = lax.broadcasted_iota(jnp.int32, (PH, total), 1)

    def body(a, _):
        block = jnp.concatenate(
            [phase_ref[s, pl.ds(a, PH, stride=stations), :] for s in range(segs)], axis=1
        )
        for i in range(-1, count):
            m = i + 1 - count // 2
            moved = pltpu.roll(block, m % total, 1) if m % total else block
            if m > 0:
                moved = jnp.where(lane >= m, moved, 0.0)
            elif m < 0:
                moved = jnp.where(lane < total + m, moved, 0.0)
            moved = moved.astype(BF16)
            if i < 0:
                extra_ref[pl.ds(pl.multiple_of(a * PH, PH), PH), :] = moved
            else:
                shifted_ref[pl.ds(pl.multiple_of(a * LAGS + i * PH, PH), PH), :] = moved
        return 0

    lax.fori_loop(0, stations, body, 0)


def own_part(x, forward, inverse, segs):
    rows, length = x.shape
    stations = rows // segs
    total = segs * length // PH
    half = length // 2
    return pl.pallas_call(
        lambda *refs: own_kernel(segs, *refs),
        out_shape=(
            jax.ShapeDtypeStruct((stations, length), BF16),
            jax.ShapeDtypeStruct((stations * LAGS, total), BF16),
            jax.ShapeDtypeStruct((stations * PH, total), BF16),
        ),
        in_specs=[pl.BlockSpec(memory_space=pltpu.VMEM)] * 3,
        out_specs=[pl.BlockSpec(memory_space=pltpu.VMEM)] * 3,
        scratch_shapes=[
            pltpu.VMEM((rows, half), F32),
            pltpu.VMEM((rows, half), F32),
            pltpu.VMEM((rows, half), F32),
            pltpu.VMEM((rows, length), BF16),
            pltpu.VMEM((rows, length), F32),
            pltpu.VMEM((segs, stations * PH, length // PH), F32),
        ],
        compiler_params=pltpu.CompilerParams(vmem_limit_bytes=48 * MIB),
        cost_estimate=pl.CostEstimate(
            flops=8 * rows * length * length, bytes_accessed=40 * MIB, transcendentals=0
        ),
        name="own",
    )(x, forward, inverse)


def correlate_kernel(
    segs, x_ref, forward_ref, inverse_ref, shifted_ref, extra_ref,
    out_ref,
    re_ref, im_ref, mag_ref, flat_ref, trace_ref, phase_ref, edge_ref, total_ref,
):
    rows, length = x_ref.shape
    received = rows // segs
    stations = shifted_ref.shape[0] // LAGS
    per_phase = length // PH
    flatten(x_ref, forward_ref, re_ref, im_ref, mag_ref, flat_ref, segs)
    scale = traces(flat_ref, inverse_ref, trace_ref, segs)[:received]
    for p in range(PH):
        for s in range(segs):
            tile = trace_ref[s * received : (s + 1) * received, p * per_phase : (p + 1) * per_phase]
            phase_ref[
                p * received : (p + 1) * received, s * per_phase : (s + 1) * per_phase
            ] = (tile * scale).astype(BF16)
    edge = dot_t(phase_ref[...], extra_ref[...])
    width = stations * PH
    lag = lax.broadcasted_iota(jnp.int32, (received, width), 1) % PH
    sums = jnp.zeros((received, width), F32)
    for p in range(PH):
        block = edge[p * received : (p + 1) * received]
        turn = (p + 1 - PH) % width
        if turn:
            block = pltpu.roll(block, turn, 1)
        sums = sums + jnp.where(lag <= p, block, 0.0)
    edge_ref[...] = sums
    lane = lax.broadcasted_iota(jnp.int32, (received, LAGS), 1)
    norm = 1.0 / math.sqrt(segs * length)

    def body(a, _):
        at = pl.multiple_of(a * LAGS, LAGS)
        product = dot_t(phase_ref[...], shifted_ref[pl.ds(at, LAGS), :])
        first = pltpu.roll(edge_ref[...], (stations - a) * PH, 1)
        if width < LAGS:
            first = jnp.concatenate([first, jnp.zeros((received, LAGS - width), F32)], axis=1)
        sums = jnp.where(lane < PH, first, 0.0)
        for p in range(PH):
            block = pltpu.roll(product[p * received : (p + 1) * received], p + 1, 1)
            sums = sums + jnp.where(lane > p, block, 0.0)
        sums = sums * norm
        for c in range(LAGS // 128):
            total_ref[c, pl.ds(a, received, stride=stations), :] = sums[:, c * 128 : (c + 1) * 128]
        return 0

    lax.fori_loop(0, stations, body, 0)
    for c in range(LAGS // 128):
        out_ref[:, c * 128 : (c + 1) * 128] = total_ref[c].astype(BF16)


def correlate(x, forward, inverse, shifted, extra, segs):
    rows, length = x.shape
    received = rows // segs
    stations = shifted.shape[0] // LAGS
    total = segs * length // PH
    half = length // 2
    return pl.pallas_call(
        lambda *refs: correlate_kernel(segs, *refs),
        out_shape=jax.ShapeDtypeStruct((received * stations, LAGS), BF16),
        in_specs=[pl.BlockSpec(memory_space=pltpu.VMEM)] * 5,
        out_specs=pl.BlockSpec(memory_space=pltpu.VMEM),
        scratch_shapes=[
            pltpu.VMEM((rows, half), F32),
            pltpu.VMEM((rows, half), F32),
            pltpu.VMEM((rows, half), F32),
            pltpu.VMEM((rows, length), BF16),
            pltpu.VMEM((rows, length), F32),
            pltpu.VMEM((received * PH, total), BF16),
            pltpu.VMEM((received, stations * PH), F32),
            pltpu.VMEM((LAGS // 128, received * stations, 128), F32),
        ],
        compiler_params=pltpu.CompilerParams(vmem_limit_bytes=48 * MIB),
        cost_estimate=pl.CostEstimate(
            flops=8 * rows * length * length, bytes_accessed=40 * MIB, transcendentals=0
        ),
        name="correlate",
    )(x, forward, inverse, shifted, extra)


def on_device(records, owners):
    stations, length = records.shape
    segs, sources = lax.axis_size("seg"), lax.axis_size("sta")
    rows_of = sources // segs
    route = [
        ((z * rows_of + y) * segs + g, (g * rows_of + y) * segs + z)
        for z in range(segs)
        for y in range(rows_of)
        for g in range(segs)
    ]
    routed = lax.ppermute(records, ("sta", "seg"), route)
    routed_owners = lax.ppermute(owners, ("sta", "seg"), route)
    whole = jnp.broadcast_to(records[None], (segs, stations, length))
    own = lax.all_to_all(whole, "seg", 0, 0, tiled=True).reshape(segs * stations, length)
    forward, inverse = make_tables(length)
    slots = fill_slots(routed, routed_owners, sources)
    slots = slots.reshape(sources, SLOTS * BS, length)
    received = lax.all_to_all(slots, "sta", 0, 0, tiled=True)
    received = received.reshape(segs * rows_of * SLOTS * BS, length)
    whitened, shifted, extra = own_part(own, forward, inverse, segs)
    result = correlate(received, forward, inverse, shifted, extra, segs)
    return whitened, result.reshape(-1, stations, LAGS)


def solution(mesh):
    return jax.shard_map(
        on_device,
        mesh=mesh,
        in_specs=(P("sta", "seg"), P("sta", None)),
        out_specs=(P("sta", "seg"), P("seg", "sta", None)),
        check_vma=False,
    )
```

```python
import math

import jax
import jax.numpy as jnp
from jax import lax
from jax.experimental import pallas as pl
from jax.experimental.pallas import tpu as pltpu
from jax.sharding import PartitionSpec as P

LAGS = 512
BS = 2
SLOTS = 2
WATER = 0.5
EPSILON = 1e-06

PH = 16
LANES = 128
CORES = 2
GROUP = 4
F32 = jnp.float32
BF16 = jnp.bfloat16
MIB = 1 << 20


def dot(a, b):
    return lax.dot_general(a, b, (((1,), (0,)), ((), ())), preferred_element_type=F32)


def dot_t(a, b):
    return lax.dot_general(a, b, (((1,), (1,)), ((), ())), preferred_element_type=F32)


def iota(shape, axis):
    return lax.broadcasted_iota(jnp.int32, shape, axis)


def cos_sin(phase, period):
    phase = phase & (period - 1)
    phase = jnp.where(phase >= period // 2, phase - period, phase)
    theta = phase.astype(F32) * (2.0 * math.pi / period)
    square = theta * theta
    cosine = jnp.full(theta.shape, 1.0 / math.factorial(20), F32)
    sine = jnp.full(theta.shape, 1.0 / math.factorial(21), F32)
    for n in range(9, -1, -1):
        cosine = (1.0 if n % 2 == 0 else -1.0) / math.factorial(2 * n) + square * cosine
        sine = (1.0 if n % 2 == 0 else -1.0) / math.factorial(2 * n + 1) + square * sine
    return cosine, sine * theta


def spread():
    shape = (LANES, PH * LANES)
    source, target = iota(shape, 0), iota(shape, 1)
    hit = (target // LANES == source % PH) & (target % LANES == source // PH)
    return jnp.where(hit, 1.0, 0.0).astype(BF16)


def prepare_kernel(owner_count, records_ref, owners_ref, phased_ref, slots_ref):
    stations, length = records_ref.shape
    blocks, dests = owners_ref.shape
    per_tile = LANES // PH
    tiles = jnp.concatenate(
        [records_ref[:, t * LANES : (t + 1) * LANES] for t in range(length // LANES)], axis=0
    )
    parts = dot(tiles, spread())
    phases = []
    for p in range(PH):
        total = None
        for t in range(length // LANES):
            part = parts[t * stations : (t + 1) * stations, p * LANES : (p + 1) * LANES]
            part = pltpu.roll(part, per_tile * t, 1) if t else part
            total = part if total is None else total + part
        phases.append(total.astype(BF16))
    for p in range(PH):
        phased_ref[:, p * LANES : (p + 1) * LANES] = phases[p]
    high = PH // GROUP
    stacked = jnp.concatenate(
        [jnp.concatenate(phases[h * GROUP : (h + 1) * GROUP], axis=1) for h in range(high)], axis=0
    )
    rows, width = owner_count * high * SLOTS * BS, high * stations
    k_of, column = iota((blocks, width), 0), iota((blocks, width), 1)
    expand = jnp.where(column % stations // BS == k_of, 1.0, 0.0)
    named = lax.dot_general(
        owners_ref[...].astype(F32), expand, (((0,), (0,)), ((), ())), preferred_element_type=F32
    )
    row, col = iota((rows, width), 0), iota((rows, width), 1)
    owner = (row // (high * SLOTS * BS)).astype(F32)
    wanted = jnp.zeros((rows, width), F32)
    for d in range(dests):
        wanted = jnp.maximum(wanted, jnp.where(named[d : d + 1, :] == owner, 1.0, 0.0))
    first, second = iota((width, width), 0), iota((width, width), 1)
    earlier = (
        (first // stations == second // stations)
        & (first % stations // BS < second % stations // BS)
        & (first % BS == 0)
    )
    rank = dot(wanted.astype(BF16), jnp.where(earlier, 1.0, 0.0).astype(BF16))
    slot = (row // BS % SLOTS).astype(F32)
    right = (
        (rank == slot)
        & (row % BS == col % BS)
        & (row // (SLOTS * BS) % high == col // stations)
    )
    select = jnp.where(right, wanted, 0.0).astype(BF16)
    slots_ref[...] = dot(select, stacked).astype(BF16)


def prepare(records, owners, owner_count):
    stations, length = records.shape
    rows = owner_count * SLOTS * BS * PH // GROUP
    return pl.pallas_call(
        lambda *refs: prepare_kernel(owner_count, *refs),
        out_shape=(
            jax.ShapeDtypeStruct((stations, length), BF16),
            jax.ShapeDtypeStruct((rows, GROUP * LANES), BF16),
        ),
        in_specs=[pl.BlockSpec(memory_space=pltpu.VMEM)] * 2,
        out_specs=[pl.BlockSpec(memory_space=pltpu.VMEM)] * 2,
        compiler_params=pltpu.CompilerParams(vmem_limit_bytes=16 * MIB),
        cost_estimate=pl.CostEstimate(
            flops=100 * MIB, bytes_accessed=2 * MIB, transcendentals=0
        ),
        name="prepare",
    )(records, owners)


def add(a, b):
    return a[0] + b[0], a[1] + b[1]


def sub(a, b):
    return a[0] - b[0], a[1] - b[1]


def times_i(a, sign):
    return (-a[1], a[0]) if sign > 0 else (a[1], -a[0])


def times(a, b):
    return a[0] * b[0] - a[1] * b[1], a[0] * b[1] + a[1] * b[0]


def unit(a, k, sign):
    k %= 16
    if k == 0:
        return a
    if k == 4:
        return times_i(a, sign)
    if k == 8:
        return -a[0], -a[1]
    if k == 12:
        return times_i(a, -sign)
    angle = 2.0 * math.pi * k / 16
    return times(a, (math.cos(angle), sign * math.sin(angle)))


def four(a, sign):
    s, d = add(a[0], a[2]), sub(a[0], a[2])
    t, e = add(a[1], a[3]), times_i(sub(a[1], a[3]), sign)
    return [add(s, t), add(d, e), sub(s, t), sub(d, e)]


def forward_sixteen(v):
    inner = [four([v[4 * p1 + p0] for p1 in range(4)], 1) for p0 in range(4)]
    out = [None] * 8
    for fa in range(4):
        u = [unit(inner[p0][fa], p0 * fa, 1) for p0 in range(4)]
        s, t = add(u[0], u[2]), add(u[1], u[3])
        out[fa] = add(s, t)
        out[fa + 4] = add(sub(u[0], u[2]), times_i(sub(u[1], u[3]), 1))
        if fa == 0:
            last = s[0] - t[0]
    return out, last


def inverse_sixteen(f):
    out = [None] * 16
    for p0 in range(4):
        inner = []
        for fa in range(4):
            turned = unit(f[fa + 4], 4 * p0, -1)
            inner.append(unit(add(f[fa], turned), p0 * fa, -1))
        for p1, value in enumerate(four(inner, -1)):
            out[4 * p1 + p0] = value
    return out


def seg_total(values, segs):
    rows = values.shape[0] // segs
    total = values[:rows]
    for s in range(1, segs):
        total = total + values[s * rows : (s + 1) * rows]
    return total


def whiten(x_ref, y_ref, f_ref, sum_ref, trace_ref, segs):
    rows = x_ref.shape[1]
    length = PH * LANES
    window = length * segs
    half = PH // 2
    n, k = iota((LANES, LANES), 0), iota((LANES, LANES), 1)
    cosine, sine = cos_sin(n * k, LANES)
    table = jnp.concatenate([cosine, sine], axis=1).astype(BF16)
    back = jnp.concatenate([cosine, sine], axis=0).astype(BF16)
    turn_cos, turn_sin = cos_sin(iota((PH, LANES), 0) * iota((PH, LANES), 1), length)
    for p in range(PH):
        y_ref[p] = dot(x_ref[p], table)
    lane = iota((8, LANES), 1)

    def forward(i, _):
        at = pl.ds(pl.multiple_of(i * 8, 8), 8)
        v = []
        for p in range(PH):
            y = y_ref[p, at, :LANES], y_ref[p, at, LANES:]
            v.append(times(y, (turn_cos[p : p + 1], turn_sin[p : p + 1])) if p else y)
        out, last = forward_sixteen(v)
        total = None
        for j, (re, im) in enumerate(out):
            if j == 0:
                mag = jnp.where(lane == 0, jnp.abs(re), jnp.sqrt(re * re + im * im))
                im = jnp.where(lane == 0, last, im)
                total = jnp.where(lane == 0, 0.5 * (jnp.abs(re) + jnp.abs(im)), mag)
            else:
                mag = jnp.sqrt(re * re + im * im)
                total = total + mag
            f_ref[j, at, :] = re
            f_ref[half + j, at, :] = im
            f_ref[2 * half + j, at, :] = mag
        sum_ref[at, :] = total
        return 0

    lax.fori_loop(0, rows // 8, forward, 0)
    amp = 2.0 * jnp.sum(seg_total(sum_ref[...], segs), axis=1, keepdims=True)
    level = WATER * amp / window + EPSILON
    sum_ref[...] = jnp.concatenate(
        [jnp.broadcast_to(level, (rows // segs, LANES))] * segs, axis=0
    )

    def inverse(i, _):
        at = pl.ds(pl.multiple_of(i * 8, 8), 8)
        level = sum_ref[at, :]
        f = []
        for j in range(half):
            re, im, mag = f_ref[j, at, :], f_ref[half + j, at, :], f_ref[2 * half + j, at, :]
            if j == 0:
                edge = im / (jnp.abs(im) + level)
                share = 2.0 / (mag + level)
                f.append(
                    (
                        jnp.where(lane == 0, 0.5, 1.0) * (re * share),
                        jnp.where(lane == 0, 0.0, im * share),
                    )
                )
                edge = jnp.where(lane == 0, edge, 0.0)
            else:
                share = 2.0 / (mag + level)
                f.append((re * share, im * share))
        for p, z in enumerate(inverse_sixteen(f)):
            if p:
                z = times(z, (turn_cos[p : p + 1], -turn_sin[p : p + 1]))
            y_ref[p, at, :LANES] = z[0] - edge if p % 2 else z[0] + edge
            y_ref[p, at, LANES:] = z[1]
        return 0

    lax.fori_loop(0, rows // 8, inverse, 0)
    energy = jnp.zeros((rows, LANES), F32)
    for p in range(PH):
        trace = dot(y_ref[p].astype(BF16), back) * (1.0 / length)
        energy = energy + trace * trace
        trace_ref[p] = trace
    energy = jnp.sum(seg_total(energy, segs), axis=1, keepdims=True)
    return lax.rsqrt(energy / window + EPSILON)


def whiten_scratch(rows):
    return [
        pltpu.VMEM((PH, rows, LANES), BF16),
        pltpu.VMEM((PH, rows, 2 * LANES), F32),
        pltpu.VMEM((3 * PH // 2, rows, LANES), F32),
        pltpu.VMEM((rows, LANES), F32),
        pltpu.VMEM((PH, rows, LANES), F32),
    ]


def own_kernel(
    segs, me_ref, near_ref, far_ref, white_ref, phase_ref, x_ref, y_ref, f_ref, sum_ref, trace_ref
):
    rows, length = x_ref.shape[1], PH * LANES
    stations = rows // segs
    per_tile = LANES // PH
    me, chips = me_ref[0], segs // CORES
    for i in range(chips):
        chip = (me // CORES + chips - i) % chips
        for ref, core in ((near_ref, me % CORES), (far_ref, 1 - me % CORES)):
            at = pl.ds(pl.multiple_of((chip * CORES + core) * stations, stations), stations)
            for p in range(PH):
                x_ref[p, at, :] = ref[
                    i * stations : (i + 1) * stations, p * LANES : (p + 1) * LANES
                ]
    scale = whiten(x_ref, y_ref, f_ref, sum_ref, trace_ref, segs)
    for p in range(PH):
        for s in range(segs):
            tile = trace_ref[p, s * stations : (s + 1) * stations, :]
            phase_ref[s, (PH - 1 - p) * stations : (PH - p) * stations, :] = (
                (tile * scale).astype(BF16).astype(F32)
            )
    mine = pl.ds(pl.multiple_of(me_ref[0] * stations, stations), stations)
    tiles = [trace_ref[p, mine, :] * scale for p in range(PH)]
    moved = []
    for t in range(length // LANES):
        turn = (LANES - per_tile * t) % LANES
        moved.append(
            jnp.concatenate(
                [(pltpu.roll(x, turn, 1) if turn else x).astype(BF16) for x in tiles], axis=1
            )
        )
    natural = dot_t(jnp.concatenate(moved, axis=0), spread()).astype(BF16)
    for t in range(length // LANES):
        white_ref[:, t * LANES : (t + 1) * LANES] = natural[t * stations : (t + 1) * stations]


def own_part(me, near, far, segs):
    rows, length = 2 * near.shape[0], near.shape[1]
    stations = rows // segs
    return pl.pallas_call(
        lambda *refs: own_kernel(segs, *refs),
        out_shape=(
            jax.ShapeDtypeStruct((stations, length), BF16),
            jax.ShapeDtypeStruct((segs, PH * stations, LANES), F32),
        ),
        in_specs=[
            pl.BlockSpec(memory_space=pltpu.SMEM),
            pl.BlockSpec(memory_space=pltpu.VMEM),
            pl.BlockSpec(memory_space=pltpu.VMEM),
        ],
        out_specs=[pl.BlockSpec(memory_space=pltpu.VMEM)] * 2,
        scratch_shapes=whiten_scratch(rows),
        compiler_params=pltpu.CompilerParams(vmem_limit_bytes=32 * MIB),
        cost_estimate=pl.CostEstimate(
            flops=2000 * MIB, bytes_accessed=4 * MIB, transcendentals=0
        ),
        name="own",
    )(me, near, far)


def shift_kernel(segs, stations, phase_ref, shifted_ref, extra_ref):
    count = LAGS // PH
    total = segs * LANES
    lane = iota((PH, total), 1)
    mine = pl.ds(pl.program_id(0), PH, stride=stations)
    block = jnp.concatenate([phase_ref[s, mine, :] for s in range(segs)], axis=1)
    for i in range(-1, count):
        m = i + 1 - count // 2
        moved = pltpu.roll(block, m % total, 1) if m else block
        if m > 0:
            moved = jnp.where(lane >= m, moved, 0.0)
        elif m < 0:
            moved = jnp.where(lane < total + m, moved, 0.0)
        moved = moved.astype(BF16)
        if i < 0:
            extra_ref[...] = moved
        else:
            shifted_ref[i * PH : (i + 1) * PH, :] = moved


def shift(phases, segs):
    stations = phases.shape[1] // PH
    total = segs * LANES
    return pl.pallas_call(
        lambda *refs: shift_kernel(segs, stations, *refs),
        out_shape=(
            jax.ShapeDtypeStruct((stations * LAGS, total), BF16),
            jax.ShapeDtypeStruct((stations * PH, total), BF16),
        ),
        grid=(stations,),
        in_specs=[pl.BlockSpec(phases.shape, lambda a: (0, 0, 0))],
        out_specs=[
            pl.BlockSpec((LAGS, total), lambda a: (a, 0)),
            pl.BlockSpec((PH, total), lambda a: (a, 0)),
        ],
        compiler_params=pltpu.CompilerParams(vmem_limit_bytes=16 * MIB),
        cost_estimate=pl.CostEstimate(
            flops=2000 * MIB, bytes_accessed=18 * MIB, transcendentals=0
        ),
        name="shift",
    )(phases)


def correlate_kernel(
    segs, received_ref, shifted_hbm, extra_hbm,
    out_ref,
    x_ref, y_ref, f_ref, sum_ref, trace_ref, phase_ref, edge_ref, total_ref,
    shifted_ref, extra_ref, sems,
):
    rows = x_ref.shape[1]
    received = rows // segs
    stations = shifted_ref.shape[0]
    copies = [pltpu.make_async_copy(extra_hbm, extra_ref, sems.at[stations])]
    for a in range(stations):
        block = shifted_hbm.at[pl.ds(a * LAGS, LAGS), :]
        copies.append(pltpu.make_async_copy(block, shifted_ref.at[a], sems.at[a]))
    for copy in copies:
        copy.start()
    high, unit_rows = PH // GROUP, SLOTS * BS
    per_seg = high * received
    to, source = iota((per_seg, per_seg), 0), iota((per_seg, per_seg), 1)
    wanted = (
        to % received // unit_rows * (high * unit_rows) + to // received * unit_rows
    ) + to % unit_rows
    order = jnp.where(source == wanted, 1.0, 0.0).astype(BF16)
    for s in range(segs):
        block = dot(order, received_ref[s * per_seg : (s + 1) * per_seg, :]).astype(BF16)
        for p in range(PH):
            x_ref[p, s * received : (s + 1) * received, :] = block[
                p // GROUP * received : (p // GROUP + 1) * received,
                p % GROUP * LANES : (p % GROUP + 1) * LANES,
            ]
    scale = whiten(x_ref, y_ref, f_ref, sum_ref, trace_ref, segs)
    for p in range(PH):
        for s in range(segs):
            tile = trace_ref[p, s * received : (s + 1) * received, :]
            phase_ref[
                p * received : (p + 1) * received, s * LANES : (s + 1) * LANES
            ] = (tile * scale).astype(BF16)
    copies[0].wait()
    edge = dot_t(phase_ref[...], extra_ref[...])
    width = stations * PH
    lag = iota((received, width), 1) % PH
    sums = jnp.zeros((received, width), F32)
    for p in range(PH):
        block = edge[p * received : (p + 1) * received]
        turn = (p + 1 - PH) % width
        block = pltpu.roll(block, turn, 1) if turn else block
        sums = sums + jnp.where(lag <= p, block, 0.0)
    edge_ref[...] = sums
    lane = iota((received, LAGS), 1)
    norm = 1.0 / math.sqrt(segs * PH * LANES)

    def body(a, _):
        block = shifted_hbm.at[pl.ds(pl.multiple_of(a * LAGS, LAGS), LAGS), :]
        pltpu.make_async_copy(block, shifted_ref.at[a], sems.at[a]).wait()
        product = dot_t(phase_ref[...], shifted_ref[a])
        first = pltpu.roll(edge_ref[...], (stations - a) * PH, 1)
        if width < LAGS:
            first = jnp.concatenate([first, jnp.zeros((received, LAGS - width), F32)], axis=1)
        sums = jnp.where(lane < PH, first, 0.0)
        for p in range(PH):
            block = pltpu.roll(product[p * received : (p + 1) * received], p + 1, 1)
            sums = sums + jnp.where(lane > p, block, 0.0)
        sums = sums * norm
        for c in range(LAGS // LANES):
            total_ref[c, pl.ds(a, received, stride=stations), :] = sums[
                :, c * LANES : (c + 1) * LANES
            ]
        return 0

    lax.fori_loop(0, stations, body, 0)
    for c in range(LAGS // LANES):
        out_ref[:, c * LANES : (c + 1) * LANES] = total_ref[c].astype(BF16)


def correlate(received, shifted, extra, segs):
    rows = received.shape[0] // (PH // GROUP)
    count = rows // segs
    stations = shifted.shape[0] // LAGS
    total = segs * LANES
    return pl.pallas_call(
        lambda *refs: correlate_kernel(segs, *refs),
        out_shape=jax.ShapeDtypeStruct((count * stations, LAGS), BF16),
        in_specs=[
            pl.BlockSpec(memory_space=pltpu.VMEM),
            pl.BlockSpec(memory_space=pl.ANY),
            pl.BlockSpec(memory_space=pl.ANY),
        ],
        out_specs=pl.BlockSpec(memory_space=pltpu.VMEM),
        scratch_shapes=[
            *whiten_scratch(rows),
            pltpu.VMEM((count * PH, total), BF16),
            pltpu.VMEM((count, stations * PH), F32),
            pltpu.VMEM((LAGS // LANES, count * stations, LANES), F32),
            pltpu.VMEM((stations, LAGS, total), BF16),
            pltpu.VMEM((stations * PH, total), BF16),
            pltpu.SemaphoreType.DMA((stations + 1,)),
        ],
        compiler_params=pltpu.CompilerParams(vmem_limit_bytes=48 * MIB),
        cost_estimate=pl.CostEstimate(
            flops=6000 * MIB, bytes_accessed=20 * MIB, transcendentals=0
        ),
        name="correlate",
    )(received, shifted, extra)


def on_device(records, owners):
    stations, length = records.shape
    segs, sources = lax.axis_size("seg"), lax.axis_size("sta")
    phased, slots = prepare(records, owners, sources)
    slots = slots.reshape(sources, -1, GROUP * LANES)
    passing = lax.all_to_all(slots, "sta", 0, 0, tiled=True)
    passing = passing.reshape(segs, -1, GROUP * LANES)
    received = lax.all_to_all(passing, "seg", 0, 0, tiled=True).reshape(-1, GROUP * LANES)
    near = [phased]
    for k in range(1, segs // CORES):
        near.append(lax.ppermute(phased, "seg", [(i, (i + k * CORES) % segs) for i in range(segs)]))
    near = jnp.concatenate(near, axis=0)
    far = lax.ppermute(near, "seg", [(i, i ^ 1) for i in range(segs)])
    me = lax.axis_index("seg").reshape(1)
    whitened, phases = own_part(me, near, far, segs)
    shifted, extra = shift(phases, segs)
    result = correlate(received, shifted, extra, segs)
    return whitened, result.reshape(-1, stations, LAGS)


def solution(mesh):
    return jax.shard_map(
        on_device,
        mesh=mesh,
        in_specs=(P("sta", "seg"), P("sta", None)),
        out_specs=(P("sta", "seg"), P("seg", "sta", None)),
        check_vma=False,
    )
```

```python
import math

import jax
import jax.numpy as jnp
from jax import lax
from jax.experimental import pallas as pl
from jax.experimental.pallas import tpu as pltpu
from jax.sharding import PartitionSpec as P

LAGS = 512
BS = 2
SLOTS = 2
WATER = 0.5
EPSILON = 1e-06

PH = 16
LANES = 128
FINE = 32
CORES = 2
GROUP = 4
F32 = jnp.float32
BF16 = jnp.bfloat16
MIB = 1 << 20


def dot(a, b):
    return lax.dot_general(a, b, (((1,), (0,)), ((), ())), preferred_element_type=F32)


def dot_t(a, b):
    return lax.dot_general(a, b, (((1,), (1,)), ((), ())), preferred_element_type=F32)


def iota(shape, axis):
    return lax.broadcasted_iota(jnp.int32, shape, axis)


def cos_sin(phase, period):
    phase = phase & (period - 1)
    phase = jnp.where(phase >= period // 2, phase - period, phase)
    theta = phase.astype(F32) * (2.0 * math.pi / period)
    square = theta * theta
    cosine = jnp.full(theta.shape, 1.0 / math.factorial(20), F32)
    sine = jnp.full(theta.shape, 1.0 / math.factorial(21), F32)
    for n in range(9, -1, -1):
        cosine = (1.0 if n % 2 == 0 else -1.0) / math.factorial(2 * n) + square * cosine
        sine = (1.0 if n % 2 == 0 else -1.0) / math.factorial(2 * n + 1) + square * sine
    return cosine, sine * theta


def spread():
    shape = (LANES, PH * LANES)
    source, target = iota(shape, 0), iota(shape, 1)
    hit = (target // LANES == source % PH) & (target % LANES == source // PH)
    return jnp.where(hit, 1.0, 0.0).astype(BF16)


def gather_back():
    shape = (LANES, PH * LANES)
    target, source = iota(shape, 0), iota(shape, 1)
    lane = source % LANES
    place = FINE // PH * (lane % (LANES // 2)) + lane // (LANES // 2)
    hit = (source // LANES == target % PH) & (place == target // PH)
    return jnp.where(hit, 1.0, 0.0).astype(BF16)


def fold(trace_ref, scale, segs, put):
    rows = trace_ref.shape[1] // segs
    low = iota((rows, LANES), 1) < LANES // 2
    for p in range(PH):
        for s in range(segs // 2):
            first = trace_ref[p, 2 * s * rows : (2 * s + 1) * rows, :] * scale
            second = trace_ref[p, (2 * s + 1) * rows : (2 * s + 2) * rows, :] * scale
            put(p, s, jnp.where(low, first, pltpu.roll(second, LANES // 2, 1)).astype(BF16))
            put(p + PH, s, jnp.where(low, pltpu.roll(first, LANES // 2, 1), second).astype(BF16))


def prepare_kernel(owner_count, records_ref, owners_ref, phased_ref, slots_ref):
    stations, length = records_ref.shape
    dests, blocks = owners_ref.shape
    per_tile = LANES // PH
    tiles = jnp.concatenate(
        [records_ref[:, t * LANES : (t + 1) * LANES] for t in range(length // LANES)], axis=0
    )
    parts = dot(tiles, spread())
    phases = []
    for p in range(PH):
        total = None
        for t in range(length // LANES):
            part = parts[t * stations : (t + 1) * stations, p * LANES : (p + 1) * LANES]
            part = pltpu.roll(part, per_tile * t, 1) if t else part
            total = part if total is None else total + part
        phases.append(total.astype(BF16))
    for p in range(PH):
        phased_ref[:, p * LANES : (p + 1) * LANES] = phases[p]
    high = PH // GROUP
    stacked = jnp.concatenate(
        [jnp.concatenate(phases[h * GROUP : (h + 1) * GROUP], axis=1) for h in range(high)], axis=0
    )
    rows, width = owner_count * high * SLOTS * BS, high * stations
    k_of, column = iota((blocks, width), 0), iota((blocks, width), 1)
    expand = jnp.where(column % stations // BS == k_of, 1.0, 0.0)
    named = lax.dot_general(
        owners_ref[...].astype(F32), expand, (((1,), (0,)), ((), ())), preferred_element_type=F32
    )
    row, col = iota((rows, width), 0), iota((rows, width), 1)
    owner = (row // (high * SLOTS * BS)).astype(F32)
    wanted = jnp.zeros((rows, width), F32)
    for d in range(dests):
        wanted = jnp.maximum(wanted, jnp.where(named[d : d + 1, :] == owner, 1.0, 0.0))
    first, second = iota((width, width), 0), iota((width, width), 1)
    earlier = (
        (first // stations == second // stations)
        & (first % stations // BS < second % stations // BS)
        & (first % BS == 0)
    )
    rank = dot(wanted.astype(BF16), jnp.where(earlier, 1.0, 0.0).astype(BF16))
    slot = (row // BS % SLOTS).astype(F32)
    right = (
        (rank == slot)
        & (row % BS == col % BS)
        & (row // (SLOTS * BS) % high == col // stations)
    )
    select = jnp.where(right, wanted, 0.0).astype(BF16)
    slots_ref[...] = dot(select, stacked).astype(BF16)


def prepare(records, owners, owner_count):
    stations, length = records.shape
    rows = owner_count * SLOTS * BS * PH // GROUP
    return pl.pallas_call(
        lambda *refs: prepare_kernel(owner_count, *refs),
        out_shape=(
            jax.ShapeDtypeStruct((stations, length), BF16),
            jax.ShapeDtypeStruct((rows, GROUP * LANES), BF16),
        ),
        in_specs=[pl.BlockSpec(memory_space=pltpu.VMEM)] * 2,
        out_specs=[pl.BlockSpec(memory_space=pltpu.VMEM)] * 2,
        compiler_params=pltpu.CompilerParams(vmem_limit_bytes=16 * MIB),
        cost_estimate=pl.CostEstimate(
            flops=100 * MIB, bytes_accessed=2 * MIB, transcendentals=0
        ),
        name="prepare",
    )(records, owners)


def add(a, b):
    return a[0] + b[0], a[1] + b[1]


def sub(a, b):
    return a[0] - b[0], a[1] - b[1]


def times_i(a, sign):
    return (-a[1], a[0]) if sign > 0 else (a[1], -a[0])


def times(a, b):
    return a[0] * b[0] - a[1] * b[1], a[0] * b[1] + a[1] * b[0]


def unit(a, k, sign):
    k %= 16
    if k == 0:
        return a
    if k == 4:
        return times_i(a, sign)
    if k == 8:
        return -a[0], -a[1]
    if k == 12:
        return times_i(a, -sign)
    angle = 2.0 * math.pi * k / 16
    return times(a, (math.cos(angle), sign * math.sin(angle)))


def four(a, sign):
    s, d = add(a[0], a[2]), sub(a[0], a[2])
    t, e = add(a[1], a[3]), times_i(sub(a[1], a[3]), sign)
    return [add(s, t), add(d, e), sub(s, t), sub(d, e)]


def forward_sixteen(v):
    inner = [four([v[4 * p1 + p0] for p1 in range(4)], 1) for p0 in range(4)]
    out = [None] * 8
    for fa in range(4):
        u = [unit(inner[p0][fa], p0 * fa, 1) for p0 in range(4)]
        s, t = add(u[0], u[2]), add(u[1], u[3])
        out[fa] = add(s, t)
        out[fa + 4] = add(sub(u[0], u[2]), times_i(sub(u[1], u[3]), 1))
        if fa == 0:
            last = s[0] - t[0]
    return out, last


def inverse_sixteen(f):
    out = [None] * 16
    for p0 in range(4):
        inner = []
        for fa in range(4):
            turned = unit(f[fa + 4], 4 * p0, -1)
            inner.append(unit(add(f[fa], turned), p0 * fa, -1))
        for p1, value in enumerate(four(inner, -1)):
            out[4 * p1 + p0] = value
    return out


def seg_total(values, segs):
    rows = values.shape[0] // segs
    total = values[:rows]
    for s in range(1, segs):
        total = total + values[s * rows : (s + 1) * rows]
    return total


def whiten(x_ref, y_ref, f_ref, sum_ref, trace_ref, segs):
    rows = x_ref.shape[1]
    length = PH * LANES
    window = length * segs
    half = PH // 2
    n, k = iota((LANES, LANES), 0), iota((LANES, LANES), 1)
    cosine, sine = cos_sin(n * k, LANES)
    table = jnp.concatenate([cosine, sine], axis=1).astype(BF16)
    folded = FINE // PH * (k % (LANES // 2)) + k // (LANES // 2)
    back = jnp.concatenate(cos_sin(n * folded, LANES), axis=0).astype(BF16)
    turn_cos, turn_sin = cos_sin(iota((PH, LANES), 0) * iota((PH, LANES), 1), length)
    for p in range(PH):
        y_ref[p] = dot(x_ref[p], table)
    lane = iota((8, LANES), 1)

    def forward(i, _):
        at = pl.ds(pl.multiple_of(i * 8, 8), 8)
        v = []
        for p in range(PH):
            y = y_ref[p, at, :LANES], y_ref[p, at, LANES:]
            v.append(times(y, (turn_cos[p : p + 1], turn_sin[p : p + 1])) if p else y)
        out, last = forward_sixteen(v)
        total = None
        for j, (re, im) in enumerate(out):
            if j == 0:
                mag = jnp.where(lane == 0, jnp.abs(re), jnp.sqrt(re * re + im * im))
                im = jnp.where(lane == 0, last, im)
                total = jnp.where(lane == 0, 0.5 * (jnp.abs(re) + jnp.abs(im)), mag)
            else:
                mag = jnp.sqrt(re * re + im * im)
                total = total + mag
            f_ref[j, at, :] = re
            f_ref[half + j, at, :] = im
            f_ref[2 * half + j, at, :] = mag
        sum_ref[at, :] = total
        return 0

    lax.fori_loop(0, rows // 8, forward, 0)
    amp = 2.0 * jnp.sum(seg_total(sum_ref[...], segs), axis=1, keepdims=True)
    level = WATER * amp / window + EPSILON
    sum_ref[...] = jnp.concatenate(
        [jnp.broadcast_to(level, (rows // segs, LANES))] * segs, axis=0
    )

    def inverse(i, _):
        at = pl.ds(pl.multiple_of(i * 8, 8), 8)
        level = sum_ref[at, :]
        f = []
        for j in range(half):
            re, im, mag = f_ref[j, at, :], f_ref[half + j, at, :], f_ref[2 * half + j, at, :]
            if j == 0:
                edge = im / (jnp.abs(im) + level)
                share = 2.0 / (mag + level)
                f.append(
                    (
                        jnp.where(lane == 0, 0.5, 1.0) * (re * share),
                        jnp.where(lane == 0, 0.0, im * share),
                    )
                )
                edge = jnp.where(lane == 0, edge, 0.0)
            else:
                share = 2.0 / (mag + level)
                f.append((re * share, im * share))
        for p, z in enumerate(inverse_sixteen(f)):
            if p:
                z = times(z, (turn_cos[p : p + 1], -turn_sin[p : p + 1]))
            y_ref[p, at, :LANES] = z[0] - edge if p % 2 else z[0] + edge
            y_ref[p, at, LANES:] = z[1]
        return 0

    lax.fori_loop(0, rows // 8, inverse, 0)
    energy = jnp.zeros((rows, LANES), F32)
    for p in range(PH):
        trace = dot(y_ref[p].astype(BF16), back) * (1.0 / length)
        energy = energy + trace * trace
        trace_ref[p] = trace
    energy = jnp.sum(seg_total(energy, segs), axis=1, keepdims=True)
    return lax.rsqrt(energy / window + EPSILON)


def whiten_scratch(rows):
    return [
        pltpu.VMEM((PH, rows, LANES), BF16),
        pltpu.VMEM((PH, rows, 2 * LANES), F32),
        pltpu.VMEM((3 * PH // 2, rows, LANES), F32),
        pltpu.VMEM((rows, LANES), F32),
        pltpu.VMEM((PH, rows, LANES), F32),
    ]


def own_kernel(
    segs, me_ref, near_ref, far_ref, white_ref, phase_ref, x_ref, y_ref, f_ref, sum_ref, trace_ref
):
    rows, length = x_ref.shape[1], PH * LANES
    stations = rows // segs
    per_tile = LANES // PH
    me, chips = me_ref[0], segs // CORES
    for i in range(chips):
        chip = (me // CORES + chips - i) % chips
        for ref, core in ((near_ref, me % CORES), (far_ref, 1 - me % CORES)):
            at = pl.ds(pl.multiple_of((chip * CORES + core) * stations, stations), stations)
            for p in range(PH):
                x_ref[p, at, :] = ref[
                    i * stations : (i + 1) * stations, p * LANES : (p + 1) * LANES
                ]
    scale = whiten(x_ref, y_ref, f_ref, sum_ref, trace_ref, segs)
    def put(p, s, tile):
        phase_ref[s, (FINE - 1 - p) * stations : (FINE - p) * stations, :] = tile.astype(F32)

    fold(trace_ref, scale, segs, put)
    mine = pl.ds(pl.multiple_of(me_ref[0] * stations, stations), stations)
    tiles = [trace_ref[p, mine, :] * scale for p in range(PH)]
    moved = []
    for t in range(length // LANES):
        turn = (LANES - per_tile // 2 * t) % LANES
        moved.append(
            jnp.concatenate(
                [(pltpu.roll(x, turn, 1) if turn else x).astype(BF16) for x in tiles], axis=1
            )
        )
    natural = dot_t(jnp.concatenate(moved, axis=0), gather_back()).astype(BF16)
    for t in range(length // LANES):
        white_ref[:, t * LANES : (t + 1) * LANES] = natural[t * stations : (t + 1) * stations]


def own_part(me, near, far, segs):
    rows, length = 2 * near.shape[0], near.shape[1]
    stations = rows // segs
    return pl.pallas_call(
        lambda *refs: own_kernel(segs, *refs),
        out_shape=(
            jax.ShapeDtypeStruct((stations, length), BF16),
            jax.ShapeDtypeStruct((segs // 2, FINE * stations, LANES), F32),
        ),
        in_specs=[
            pl.BlockSpec(memory_space=pltpu.SMEM),
            pl.BlockSpec(memory_space=pltpu.VMEM),
            pl.BlockSpec(memory_space=pltpu.VMEM),
        ],
        out_specs=[pl.BlockSpec(memory_space=pltpu.VMEM)] * 2,
        scratch_shapes=whiten_scratch(rows),
        compiler_params=pltpu.CompilerParams(vmem_limit_bytes=32 * MIB),
        cost_estimate=pl.CostEstimate(
            flops=2000 * MIB, bytes_accessed=4 * MIB, transcendentals=0
        ),
        name="own",
    )(me, near, far)


def shift_kernel(stations, phase_ref, shifted_hbm, extra_hbm, shifted_ref, extra_ref, sems):
    count = LAGS // FINE
    tiles = phase_ref.shape[0]
    total = tiles * LANES
    lane = iota((FINE, total), 1)

    def copies(a):
        to = shifted_hbm.at[pl.ds(pl.multiple_of(a * LAGS, LAGS), LAGS), :]
        to_extra = extra_hbm.at[pl.ds(pl.multiple_of(a * FINE, FINE), FINE), :]
        return (
            pltpu.make_async_copy(shifted_ref.at[a], to, sems.at[0, a]),
            pltpu.make_async_copy(extra_ref.at[a], to_extra, sems.at[1, a]),
        )

    def body(a, _):
        block = jnp.concatenate(
            [phase_ref[s, pl.ds(a, FINE, stride=stations), :] for s in range(tiles)], axis=1
        )
        for i in range(-1, count):
            m = i + 1 - count // 2
            moved = pltpu.roll(block, m % total, 1) if m else block
            if m > 0:
                moved = jnp.where(lane >= m, moved, 0.0)
            elif m < 0:
                moved = jnp.where(lane < total + m, moved, 0.0)
            moved = moved.astype(BF16)
            if i < 0:
                extra_ref[a] = moved
            else:
                shifted_ref[a, i * FINE : (i + 1) * FINE, :] = moved
        for copy in copies(a):
            copy.start()
        return 0

    lax.fori_loop(0, stations, body, 0)

    def finish(a, _):
        for copy in copies(a):
            copy.wait()
        return 0

    lax.fori_loop(0, stations, finish, 0)


def shift(phases):
    stations = phases.shape[1] // FINE
    total = phases.shape[0] * LANES
    return pl.pallas_call(
        lambda *refs: shift_kernel(stations, *refs),
        out_shape=(
            pltpu.HBM((stations * LAGS, total), BF16),
            pltpu.HBM((stations * FINE, total), BF16),
        ),
        in_specs=[pl.BlockSpec(memory_space=pltpu.VMEM)],
        out_specs=[pl.BlockSpec(memory_space=pltpu.HBM)] * 2,
        scratch_shapes=[
            pltpu.VMEM((stations, LAGS, total), BF16),
            pltpu.VMEM((stations, FINE, total), BF16),
            pltpu.SemaphoreType.DMA((2, stations)),
        ],
        compiler_params=pltpu.CompilerParams(vmem_limit_bytes=16 * MIB),
        cost_estimate=pl.CostEstimate(
            flops=2000 * MIB, bytes_accessed=9 * MIB, transcendentals=0
        ),
        name="shift",
    )(phases)


def correlate_kernel(
    segs, received_ref, shifted_hbm, extra_hbm,
    out_ref,
    x_ref, y_ref, f_ref, sum_ref, trace_ref, phase_ref, edge_ref, total_ref,
    shifted_ref, extra_ref, even_ref, odd_ref, sems,
):
    rows = x_ref.shape[1]
    received = rows // segs
    stations = shifted_ref.shape[0]
    copies = [pltpu.make_async_copy(extra_hbm, extra_ref, sems.at[stations])]
    for a in range(stations):
        block = shifted_hbm.at[pl.ds(a * LAGS, LAGS), :]
        copies.append(pltpu.make_async_copy(block, shifted_ref.at[a], sems.at[a]))
    for copy in copies:
        copy.start()
    high, unit_rows = PH // GROUP, SLOTS * BS
    per_seg = high * received
    to, source = iota((per_seg, per_seg), 0), iota((per_seg, per_seg), 1)
    wanted = (
        to % received // unit_rows * (high * unit_rows) + to // received * unit_rows
    ) + to % unit_rows
    order = jnp.where(source == wanted, 1.0, 0.0).astype(BF16)
    for s in range(segs):
        block = dot(order, received_ref[s * per_seg : (s + 1) * per_seg, :]).astype(BF16)
        for p in range(PH):
            x_ref[p, s * received : (s + 1) * received, :] = block[
                p // GROUP * received : (p // GROUP + 1) * received,
                p % GROUP * LANES : (p % GROUP + 1) * LANES,
            ]
    scale = whiten(x_ref, y_ref, f_ref, sum_ref, trace_ref, segs)

    def put(p, s, tile):
        phase_ref[p * received : (p + 1) * received, s * LANES : (s + 1) * LANES] = tile

    fold(trace_ref, scale, segs, put)
    copies[0].wait()
    edge = dot_t(phase_ref[...], extra_ref[...])
    width = stations * FINE
    lag = iota((received, width), 1) % FINE
    sums = jnp.zeros((received, width), F32)
    for p in range(FINE):
        block = edge[p * received : (p + 1) * received]
        turn = (p + 1 - FINE) % width
        block = pltpu.roll(block, turn, 1) if turn else block
        sums = sums + jnp.where(lag <= p, block, 0.0)
    edge_ref[...] = sums
    lane = iota((received, LAGS), 1)
    norm = 1.0 / math.sqrt(segs * PH * LANES)

    def multiply(a):
        block = shifted_hbm.at[pl.ds(pl.multiple_of(a * LAGS, LAGS), LAGS), :]
        pltpu.make_async_copy(block, shifted_ref.at[a], sems.at[a]).wait()
        return dot_t(phase_ref[...], shifted_ref[a])

    def combine(a, product_ref):
        first = pltpu.roll(edge_ref[...], (stations - a) * FINE, 1)
        sums = jnp.where(lane < FINE, first[:, :LAGS], 0.0)
        for p in range(FINE):
            block = pltpu.roll(product_ref[p * received : (p + 1) * received], p + 1, 1)
            sums = sums + jnp.where(lane > p, block, 0.0)
        sums = sums * norm
        for c in range(LAGS // LANES):
            total_ref[c, pl.ds(a, received, stride=stations), :] = sums[
                :, c * LANES : (c + 1) * LANES
            ]

    even_ref[...] = multiply(0)

    def body(i, _):
        odd_ref[...] = multiply(2 * i + 1)
        combine(2 * i, even_ref)
        even_ref[...] = multiply(2 * i + 2)
        combine(2 * i + 1, odd_ref)
        return 0

    lax.fori_loop(0, stations // 2 - 1, body, 0)
    odd_ref[...] = multiply(stations - 1)
    combine(stations - 2, even_ref)
    combine(stations - 1, odd_ref)
    for c in range(LAGS // LANES):
        out_ref[:, c * LANES : (c + 1) * LANES] = total_ref[c].astype(BF16)


def correlate(received, shifted, extra, segs):
    rows = received.shape[0] // (PH // GROUP)
    count = rows // segs
    stations = shifted.shape[0] // LAGS
    total = shifted.shape[1]
    return pl.pallas_call(
        lambda *refs: correlate_kernel(segs, *refs),
        out_shape=jax.ShapeDtypeStruct((count * stations, LAGS), BF16),
        in_specs=[
            pl.BlockSpec(memory_space=pltpu.VMEM),
            pl.BlockSpec(memory_space=pltpu.HBM),
            pl.BlockSpec(memory_space=pltpu.HBM),
        ],
        out_specs=pl.BlockSpec(memory_space=pltpu.VMEM),
        scratch_shapes=[
            *whiten_scratch(rows),
            pltpu.VMEM((count * FINE, total), BF16),
            pltpu.VMEM((count, stations * FINE), F32),
            pltpu.VMEM((LAGS // LANES, count * stations, LANES), F32),
            pltpu.VMEM((stations, LAGS, total), BF16),
            pltpu.VMEM((stations * FINE, total), BF16),
            pltpu.VMEM((count * FINE, LAGS), F32),
            pltpu.VMEM((count * FINE, LAGS), F32),
            pltpu.SemaphoreType.DMA((stations + 1,)),
        ],
        compiler_params=pltpu.CompilerParams(vmem_limit_bytes=48 * MIB),
        cost_estimate=pl.CostEstimate(
            flops=6000 * MIB, bytes_accessed=20 * MIB, transcendentals=0
        ),
        name="correlate",
    )(
        received,
        pltpu.with_memory_space_constraint(shifted, pltpu.HBM),
        pltpu.with_memory_space_constraint(extra, pltpu.HBM),
    )


def on_device(records, owners):
    stations, length = records.shape
    segs, sources = lax.axis_size("seg"), lax.axis_size("sta")
    phased, slots = prepare(records, owners.T, sources)
    slots = slots.reshape(sources, -1, GROUP * LANES)
    passing = lax.all_to_all(slots, "sta", 0, 0, tiled=True)
    passing = passing.reshape(segs, -1, GROUP * LANES)
    near = [phased]
    for k in range(1, segs // CORES):
        near.append(lax.ppermute(phased, "seg", [(i, (i + k * CORES) % segs) for i in range(segs)]))
    near = jnp.concatenate(near, axis=0)
    far = lax.ppermute(near, "seg", [(i, i ^ 1) for i in range(segs)])
    me = lax.axis_index("seg").reshape(1)
    whitened, phases = own_part(me, near, far, segs)
    shifted, extra = shift(phases)
    passing, shifted, extra = lax.optimization_barrier((passing, shifted, extra))
    received = lax.all_to_all(passing, "seg", 0, 0, tiled=True).reshape(-1, GROUP * LANES)
    result = correlate(received, shifted, extra, segs)
    return whitened, result.reshape(-1, stations, LAGS)


def solution(mesh):
    return jax.shard_map(
        on_device,
        mesh=mesh,
        in_specs=(P("sta", "seg"), P("sta", None)),
        out_specs=(P("sta", "seg"), P("seg", "sta", None)),
        check_vma=False,
    )
```

```python
import math

import jax
import jax.numpy as jnp
from jax import lax
from jax.experimental import pallas as pl
from jax.experimental.pallas import tpu as pltpu
from jax.sharding import PartitionSpec as P

LAGS = 512
BS = 2
SLOTS = 2
WATER = 0.5
EPSILON = 1e-06

PH = 16
LANES = 128
FINE = 32
CORES = 2
GROUP = 4
F32 = jnp.float32
BF16 = jnp.bfloat16
MIB = 1 << 20


def dot(a, b):
    return lax.dot_general(a, b, (((1,), (0,)), ((), ())), preferred_element_type=F32)


def dot_t(a, b):
    return lax.dot_general(a, b, (((1,), (1,)), ((), ())), preferred_element_type=F32)


def in_hbm(x):
    return pltpu.with_memory_space_constraint(x, pltpu.HBM)


def iota(shape, axis):
    return lax.broadcasted_iota(jnp.int32, shape, axis)


def cos_sin(phase, period):
    phase = phase & (period - 1)
    phase = jnp.where(phase >= period // 2, phase - period, phase)
    theta = phase.astype(F32) * (2.0 * math.pi / period)
    square = theta * theta
    cosine = jnp.full(theta.shape, 1.0 / math.factorial(20), F32)
    sine = jnp.full(theta.shape, 1.0 / math.factorial(21), F32)
    for n in range(9, -1, -1):
        cosine = (1.0 if n % 2 == 0 else -1.0) / math.factorial(2 * n) + square * cosine
        sine = (1.0 if n % 2 == 0 else -1.0) / math.factorial(2 * n + 1) + square * sine
    return cosine, sine * theta


def spread():
    shape = (LANES, PH * LANES)
    source, target = iota(shape, 0), iota(shape, 1)
    hit = (target // LANES == source % PH) & (target % LANES == source // PH)
    return jnp.where(hit, 1.0, 0.0).astype(BF16)


def gather_back():
    shape = (LANES, PH * LANES)
    target, source = iota(shape, 0), iota(shape, 1)
    lane = source % LANES
    place = FINE // PH * (lane % (LANES // 2)) + lane // (LANES // 2)
    hit = (source // LANES == target % PH) & (place == target // PH)
    return jnp.where(hit, 1.0, 0.0).astype(BF16)


def fold(trace_ref, scale, segs, put):
    rows = trace_ref.shape[1] // segs
    low = iota((rows, LANES), 1) < LANES // 2
    for p in range(PH):
        for s in range(segs // 2):
            first = trace_ref[p, 2 * s * rows : (2 * s + 1) * rows, :] * scale
            second = trace_ref[p, (2 * s + 1) * rows : (2 * s + 2) * rows, :] * scale
            put(p, s, jnp.where(low, first, pltpu.roll(second, LANES // 2, 1)).astype(BF16))
            put(p + PH, s, jnp.where(low, pltpu.roll(first, LANES // 2, 1), second).astype(BF16))


def prepare_kernel(
    owner_count, records_hbm, owners_hbm, phased_ref, slots_ref, records_ref, owners_ref, sems
):
    loads = [
        pltpu.make_async_copy(records_hbm, records_ref, sems.at[0]),
        pltpu.make_async_copy(owners_hbm, owners_ref, sems.at[1]),
    ]
    for load in loads:
        load.start()
    stations, length = records_ref.shape
    dests, blocks = owners_ref.shape
    per_tile = LANES // PH
    one_hot = spread()
    loads[0].wait()
    tiles = jnp.concatenate(
        [records_ref[:, t * LANES : (t + 1) * LANES] for t in range(length // LANES)], axis=0
    )
    parts = dot(tiles, one_hot)
    phases = []
    for p in range(PH):
        total = None
        for t in range(length // LANES):
            part = parts[t * stations : (t + 1) * stations, p * LANES : (p + 1) * LANES]
            part = pltpu.roll(part, per_tile * t, 1) if t else part
            total = part if total is None else total + part
        phases.append(total.astype(BF16))
    for p in range(PH):
        phased_ref[:, p * LANES : (p + 1) * LANES] = phases[p]
    high = PH // GROUP
    stacked = jnp.concatenate(
        [jnp.concatenate(phases[h * GROUP : (h + 1) * GROUP], axis=1) for h in range(high)], axis=0
    )
    rows, width = owner_count * high * SLOTS * BS, high * stations
    k_of, column = iota((blocks, width), 0), iota((blocks, width), 1)
    expand = jnp.where(column % stations // BS == k_of, 1.0, 0.0)
    loads[1].wait()
    named = lax.dot_general(
        owners_ref[...].astype(F32), expand, (((1,), (0,)), ((), ())), preferred_element_type=F32
    )
    row, col = iota((rows, width), 0), iota((rows, width), 1)
    owner = (row // (high * SLOTS * BS)).astype(F32)
    wanted = jnp.zeros((rows, width), F32)
    for d in range(dests):
        wanted = jnp.maximum(wanted, jnp.where(named[d : d + 1, :] == owner, 1.0, 0.0))
    first, second = iota((width, width), 0), iota((width, width), 1)
    earlier = (
        (first // stations == second // stations)
        & (first % stations // BS < second % stations // BS)
        & (first % BS == 0)
    )
    rank = dot(wanted.astype(BF16), jnp.where(earlier, 1.0, 0.0).astype(BF16))
    slot = (row // BS % SLOTS).astype(F32)
    right = (
        (rank == slot)
        & (row % BS == col % BS)
        & (row // (SLOTS * BS) % high == col // stations)
    )
    select = jnp.where(right, wanted, 0.0).astype(BF16)
    slots_ref[...] = dot(select, stacked).astype(BF16)


def prepare(records, owners, owner_count):
    stations, length = records.shape
    rows = owner_count * SLOTS * BS * PH // GROUP
    return pl.pallas_call(
        lambda *refs: prepare_kernel(owner_count, *refs),
        out_shape=(
            jax.ShapeDtypeStruct((stations, length), BF16),
            jax.ShapeDtypeStruct((rows, GROUP * LANES), BF16),
        ),
        in_specs=[pl.BlockSpec(memory_space=pltpu.HBM)] * 2,
        out_specs=[pl.BlockSpec(memory_space=pltpu.VMEM)] * 2,
        scratch_shapes=[
            pltpu.VMEM(records.shape, records.dtype),
            pltpu.VMEM(owners.shape, owners.dtype),
            pltpu.SemaphoreType.DMA((2,)),
        ],
        compiler_params=pltpu.CompilerParams(vmem_limit_bytes=16 * MIB),
        cost_estimate=pl.CostEstimate(
            flops=100 * MIB, bytes_accessed=2 * MIB, transcendentals=0
        ),
        name="prepare",
    )(in_hbm(records), in_hbm(owners))


def add(a, b):
    return a[0] + b[0], a[1] + b[1]


def sub(a, b):
    return a[0] - b[0], a[1] - b[1]


def times_i(a, sign):
    return (-a[1], a[0]) if sign > 0 else (a[1], -a[0])


def times(a, b):
    return a[0] * b[0] - a[1] * b[1], a[0] * b[1] + a[1] * b[0]


def unit(a, k, sign):
    k %= 16
    if k == 0:
        return a
    if k == 4:
        return times_i(a, sign)
    if k == 8:
        return -a[0], -a[1]
    if k == 12:
        return times_i(a, -sign)
    angle = 2.0 * math.pi * k / 16
    return times(a, (math.cos(angle), sign * math.sin(angle)))


def four(a, sign):
    s, d = add(a[0], a[2]), sub(a[0], a[2])
    t, e = add(a[1], a[3]), times_i(sub(a[1], a[3]), sign)
    return [add(s, t), add(d, e), sub(s, t), sub(d, e)]


def forward_sixteen(v):
    inner = [four([v[4 * p1 + p0] for p1 in range(4)], 1) for p0 in range(4)]
    out = [None] * 8
    for fa in range(4):
        u = [unit(inner[p0][fa], p0 * fa, 1) for p0 in range(4)]
        s, t = add(u[0], u[2]), add(u[1], u[3])
        out[fa] = add(s, t)
        out[fa + 4] = add(sub(u[0], u[2]), times_i(sub(u[1], u[3]), 1))
        if fa == 0:
            last = s[0] - t[0]
    return out, last


def inverse_sixteen(f):
    out = [None] * 16
    for p0 in range(4):
        inner = []
        for fa in range(4):
            turned = unit(f[fa + 4], 4 * p0, -1)
            inner.append(unit(add(f[fa], turned), p0 * fa, -1))
        for p1, value in enumerate(four(inner, -1)):
            out[4 * p1 + p0] = value
    return out


def seg_total(values, segs):
    rows = values.shape[0] // segs
    total = values[:rows]
    for s in range(1, segs):
        total = total + values[s * rows : (s + 1) * rows]
    return total


def whiten(x_ref, y_ref, f_ref, sum_ref, trace_ref, segs):
    rows = x_ref.shape[1]
    length = PH * LANES
    window = length * segs
    half = PH // 2
    n, k = iota((LANES, LANES), 0), iota((LANES, LANES), 1)
    cosine, sine = cos_sin(n * k, LANES)
    table = jnp.concatenate([cosine, sine], axis=1).astype(BF16)
    folded = FINE // PH * (k % (LANES // 2)) + k // (LANES // 2)
    back = jnp.concatenate(cos_sin(n * folded, LANES), axis=0).astype(BF16)
    turn_cos, turn_sin = cos_sin(iota((PH, LANES), 0) * iota((PH, LANES), 1), length)
    for p in range(PH):
        y_ref[p] = dot(x_ref[p], table)
    lane = iota((8, LANES), 1)

    def forward(i, _):
        at = pl.ds(pl.multiple_of(i * 8, 8), 8)
        v = []
        for p in range(PH):
            y = y_ref[p, at, :LANES], y_ref[p, at, LANES:]
            v.append(times(y, (turn_cos[p : p + 1], turn_sin[p : p + 1])) if p else y)
        out, last = forward_sixteen(v)
        total = None
        for j, (re, im) in enumerate(out):
            if j == 0:
                mag = jnp.where(lane == 0, jnp.abs(re), jnp.sqrt(re * re + im * im))
                im = jnp.where(lane == 0, last, im)
                total = jnp.where(lane == 0, 0.5 * (jnp.abs(re) + jnp.abs(im)), mag)
            else:
                mag = jnp.sqrt(re * re + im * im)
                total = total + mag
            f_ref[j, at, :] = re
            f_ref[half + j, at, :] = im
            f_ref[2 * half + j, at, :] = mag
        sum_ref[at, :] = total
        return 0

    lax.fori_loop(0, rows // 8, forward, 0, unroll=4)
    amp = 2.0 * jnp.sum(seg_total(sum_ref[...], segs), axis=1, keepdims=True)
    level = WATER * amp / window + EPSILON
    sum_ref[...] = jnp.concatenate(
        [jnp.broadcast_to(level, (rows // segs, LANES))] * segs, axis=0
    )

    def inverse(i, _):
        at = pl.ds(pl.multiple_of(i * 8, 8), 8)
        level = sum_ref[at, :]
        f = []
        for j in range(half):
            re, im, mag = f_ref[j, at, :], f_ref[half + j, at, :], f_ref[2 * half + j, at, :]
            if j == 0:
                edge = im / (jnp.abs(im) + level)
                share = 2.0 / (mag + level)
                f.append(
                    (
                        jnp.where(lane == 0, 0.5, 1.0) * (re * share),
                        jnp.where(lane == 0, 0.0, im * share),
                    )
                )
                edge = jnp.where(lane == 0, edge, 0.0)
            else:
                share = 2.0 / (mag + level)
                f.append((re * share, im * share))
        for p, z in enumerate(inverse_sixteen(f)):
            if p:
                z = times(z, (turn_cos[p : p + 1], -turn_sin[p : p + 1]))
            y_ref[p, at, :LANES] = z[0] - edge if p % 2 else z[0] + edge
            y_ref[p, at, LANES:] = z[1]
        return 0

    lax.fori_loop(0, rows // 8, inverse, 0, unroll=4)
    energy = jnp.zeros((rows, LANES), F32)
    for p in range(PH):
        trace = dot(y_ref[p].astype(BF16), back) * (1.0 / length)
        energy = energy + trace * trace
        trace_ref[p] = trace
    energy = jnp.sum(seg_total(energy, segs), axis=1, keepdims=True)
    return lax.rsqrt(energy / window + EPSILON)


def whiten_scratch(rows):
    return [
        pltpu.VMEM((PH, rows, LANES), BF16),
        pltpu.VMEM((PH, rows, 2 * LANES), F32),
        pltpu.VMEM((3 * PH // 2, rows, LANES), F32),
        pltpu.VMEM((rows, LANES), F32),
        pltpu.VMEM((PH, rows, LANES), F32),
    ]


def own_kernel(
    segs, me_ref, *refs
):
    pairs, refs = refs[: segs // CORES], refs[segs // CORES :]
    white_ref, phase_ref, x_ref, y_ref, f_ref, sum_ref, trace_ref = refs
    rows, length = x_ref.shape[1], PH * LANES
    stations = rows // segs
    per_tile = LANES // PH
    me, chips = me_ref[0], segs // CORES
    for i, ref in enumerate(pairs):
        chip = (lax.div(me, CORES) + chips - i) & (chips - 1)
        for j in range(CORES):
            core = (me + j) & (CORES - 1)
            at = pl.ds(pl.multiple_of((chip * CORES + core) * stations, stations), stations)
            for p in range(PH):
                x_ref[p, at, :] = ref[
                    j * stations : (j + 1) * stations, p * LANES : (p + 1) * LANES
                ]
    scale = whiten(x_ref, y_ref, f_ref, sum_ref, trace_ref, segs)
    def put(p, s, tile):
        phase_ref[s, (FINE - 1 - p) * stations : (FINE - p) * stations, :] = tile.astype(F32)

    fold(trace_ref, scale, segs, put)
    mine = pl.ds(pl.multiple_of(me_ref[0] * stations, stations), stations)
    tiles = [trace_ref[p, mine, :] * scale for p in range(PH)]
    moved = []
    for t in range(length // LANES):
        turn = (LANES - per_tile // 2 * t) % LANES
        moved.append(
            jnp.concatenate(
                [(pltpu.roll(x, turn, 1) if turn else x).astype(BF16) for x in tiles], axis=1
            )
        )
    natural = dot_t(jnp.concatenate(moved, axis=0), gather_back()).astype(BF16)
    for t in range(length // LANES):
        white_ref[:, t * LANES : (t + 1) * LANES] = natural[t * stations : (t + 1) * stations]


def own_part(me, pairs, segs):
    rows, length = len(pairs) * pairs[0].shape[0], pairs[0].shape[1]
    stations = rows // segs
    return pl.pallas_call(
        lambda *refs: own_kernel(segs, *refs),
        out_shape=(
            jax.ShapeDtypeStruct((stations, length), BF16),
            jax.ShapeDtypeStruct((segs // 2, FINE * stations, LANES), F32),
        ),
        in_specs=[
            pl.BlockSpec(memory_space=pltpu.SMEM),
            *[pl.BlockSpec(memory_space=pltpu.VMEM)] * len(pairs),
        ],
        out_specs=[pl.BlockSpec(memory_space=pltpu.VMEM)] * 2,
        scratch_shapes=whiten_scratch(rows),
        compiler_params=pltpu.CompilerParams(vmem_limit_bytes=32 * MIB),
        cost_estimate=pl.CostEstimate(
            flops=2000 * MIB, bytes_accessed=4 * MIB, transcendentals=0
        ),
        name="own",
    )(me, *pairs)


def shift_kernel(stations, phase_ref, shifted_hbm, extra_hbm, shifted_ref, extra_ref, sems):
    count = LAGS // FINE
    tiles = phase_ref.shape[0]
    total = tiles * LANES
    lane = iota((FINE, total), 1)

    def copies(a):
        to = shifted_hbm.at[pl.ds(pl.multiple_of(a * LAGS, LAGS), LAGS), :]
        to_extra = extra_hbm.at[pl.ds(pl.multiple_of(a * FINE, FINE), FINE), :]
        return (
            pltpu.make_async_copy(shifted_ref.at[a], to, sems.at[0, a]),
            pltpu.make_async_copy(extra_ref.at[a], to_extra, sems.at[1, a]),
        )

    def body(a, _):
        block = jnp.concatenate(
            [phase_ref[s, pl.ds(a, FINE, stride=stations), :] for s in range(tiles)], axis=1
        )
        for i in range(-1, count):
            m = i + 1 - count // 2
            moved = pltpu.roll(block, m % total, 1) if m else block
            if m > 0:
                moved = jnp.where(lane >= m, moved, 0.0)
            elif m < 0:
                moved = jnp.where(lane < total + m, moved, 0.0)
            moved = moved.astype(BF16)
            if i < 0:
                extra_ref[a] = moved
            else:
                shifted_ref[a, i * FINE : (i + 1) * FINE, :] = moved
        for copy in copies(a):
            copy.start()
        return 0

    lax.fori_loop(0, stations, body, 0)

    def finish(a, _):
        for copy in copies(a):
            copy.wait()
        return 0

    lax.fori_loop(0, stations, finish, 0)


def shift(phases):
    stations = phases.shape[1] // FINE
    total = phases.shape[0] * LANES
    return pl.pallas_call(
        lambda *refs: shift_kernel(stations, *refs),
        out_shape=(
            pltpu.HBM((stations * LAGS, total), BF16),
            pltpu.HBM((stations * FINE, total), BF16),
        ),
        in_specs=[pl.BlockSpec(memory_space=pltpu.VMEM)],
        out_specs=[pl.BlockSpec(memory_space=pltpu.HBM)] * 2,
        scratch_shapes=[
            pltpu.VMEM((stations, LAGS, total), BF16),
            pltpu.VMEM((stations, FINE, total), BF16),
            pltpu.SemaphoreType.DMA((2, stations)),
        ],
        compiler_params=pltpu.CompilerParams(vmem_limit_bytes=16 * MIB),
        cost_estimate=pl.CostEstimate(
            flops=2000 * MIB, bytes_accessed=9 * MIB, transcendentals=0
        ),
        name="shift",
    )(phases)


def correlate_kernel(segs, me_ref, *refs):
    chips = segs // CORES
    near, (far_ref, shifted_hbm, extra_hbm, out_ref), refs = (
        refs[:chips],
        refs[chips : chips + 4],
        refs[chips + 4 :],
    )
    x_ref, y_ref, f_ref, sum_ref, trace_ref, phase_ref, edge_ref, total_ref = refs[:8]
    shifted_ref, extra_ref, even_ref, odd_ref, sems = refs[8:]
    rows = x_ref.shape[1]
    received = rows // segs
    stations = shifted_ref.shape[0]
    copies = [pltpu.make_async_copy(extra_hbm, extra_ref, sems.at[stations])]
    for a in range(stations):
        block = shifted_hbm.at[pl.ds(a * LAGS, LAGS), :]
        copies.append(pltpu.make_async_copy(block, shifted_ref.at[a], sems.at[a]))
    for copy in copies:
        copy.start()
    high, unit_rows = PH // GROUP, SLOTS * BS
    per_seg = high * received
    to, at_row = iota((per_seg, per_seg), 0), iota((per_seg, per_seg), 1)
    wanted = (
        to % received // unit_rows * (high * unit_rows) + to // received * unit_rows
    ) + to % unit_rows
    order = jnp.where(at_row == wanted, 1.0, 0.0).astype(BF16)
    me = me_ref[0]
    mine = me & (CORES - 1)
    for s in range(segs):
        i = s // CORES
        chip = (lax.div(me, CORES) + chips - i) & (chips - 1)
        if s % CORES:
            source, seg = far_ref[i], chip * CORES + 1 - mine
        else:
            source = near[i][(chip * CORES if i == 0 else 0) + mine]
            seg = chip * CORES + mine
        block = dot(order, source).astype(BF16)
        at = pl.ds(pl.multiple_of(seg * received, received), received)
        for p in range(PH):
            x_ref[p, at, :] = block[
                p // GROUP * received : (p // GROUP + 1) * received,
                p % GROUP * LANES : (p % GROUP + 1) * LANES,
            ]
    scale = whiten(x_ref, y_ref, f_ref, sum_ref, trace_ref, segs)

    def put(p, s, tile):
        phase_ref[p * received : (p + 1) * received, s * LANES : (s + 1) * LANES] = tile

    fold(trace_ref, scale, segs, put)
    copies[0].wait()
    edge = dot_t(phase_ref[...], extra_ref[...])
    width = stations * FINE
    lag = iota((received, width), 1) % FINE
    sums = jnp.zeros((received, width), F32)
    for p in range(FINE):
        block = edge[p * received : (p + 1) * received]
        turn = (p + 1 - FINE) % width
        block = pltpu.roll(block, turn, 1) if turn else block
        sums = sums + jnp.where(lag <= p, block, 0.0)
    edge_ref[...] = sums
    lane = iota((received, LAGS), 1)
    norm = 1.0 / math.sqrt(segs * PH * LANES)

    def multiply(a):
        block = shifted_hbm.at[pl.ds(pl.multiple_of(a * LAGS, LAGS), LAGS), :]
        pltpu.make_async_copy(block, shifted_ref.at[a], sems.at[a]).wait()
        return dot_t(phase_ref[...], shifted_ref[a])

    def combine(a, product_ref):
        first = pltpu.roll(edge_ref[...], (stations - a) * FINE, 1)
        sums = jnp.where(lane < FINE, first[:, :LAGS], 0.0)
        for p in range(FINE):
            block = pltpu.roll(product_ref[p * received : (p + 1) * received], p + 1, 1)
            sums = sums + jnp.where(lane > p, block, 0.0)
        sums = sums * norm
        for c in range(LAGS // LANES):
            total_ref[c, pl.ds(a, received, stride=stations), :] = sums[
                :, c * LANES : (c + 1) * LANES
            ]

    even_ref[...] = multiply(0)

    def body(i, _):
        odd_ref[...] = multiply(2 * i + 1)
        combine(2 * i, even_ref)
        even_ref[...] = multiply(2 * i + 2)
        combine(2 * i + 1, odd_ref)
        return 0

    lax.fori_loop(0, stations // 2 - 1, body, 0)
    odd_ref[...] = multiply(stations - 1)
    combine(stations - 2, even_ref)
    combine(stations - 1, odd_ref)
    for c in range(LAGS // LANES):
        out_ref[:, c * LANES : (c + 1) * LANES] = total_ref[c].astype(BF16)


def correlate(me, near, far, shifted, extra, segs):
    rows = segs * far.shape[1] // (PH // GROUP)
    count = rows // segs
    stations = shifted.shape[0] // LAGS
    total = shifted.shape[1]
    return pl.pallas_call(
        lambda *refs: correlate_kernel(segs, *refs),
        out_shape=jax.ShapeDtypeStruct((count * stations, LAGS), BF16),
        in_specs=[
            pl.BlockSpec(memory_space=pltpu.SMEM),
            *[pl.BlockSpec(memory_space=pltpu.VMEM)] * (len(near) + 1),
            pl.BlockSpec(memory_space=pltpu.HBM),
            pl.BlockSpec(memory_space=pltpu.HBM),
        ],
        out_specs=pl.BlockSpec(memory_space=pltpu.VMEM),
        scratch_shapes=[
            *whiten_scratch(rows),
            pltpu.VMEM((count * FINE, total), BF16),
            pltpu.VMEM((count, stations * FINE), F32),
            pltpu.VMEM((LAGS // LANES, count * stations, LANES), F32),
            pltpu.VMEM((stations, LAGS, total), BF16),
            pltpu.VMEM((stations * FINE, total), BF16),
            pltpu.VMEM((count * FINE, LAGS), F32),
            pltpu.VMEM((count * FINE, LAGS), F32),
            pltpu.SemaphoreType.DMA((stations + 1,)),
        ],
        compiler_params=pltpu.CompilerParams(vmem_limit_bytes=48 * MIB),
        cost_estimate=pl.CostEstimate(
            flops=6000 * MIB, bytes_accessed=20 * MIB, transcendentals=0
        ),
        name="correlate",
    )(
        me,
        *near,
        far,
        in_hbm(shifted),
        in_hbm(extra),
    )


def on_device(records, owners):
    stations, length = records.shape
    segs, sources = lax.axis_size("seg"), lax.axis_size("sta")
    chips = segs // CORES
    me = lax.axis_index("seg")
    chip = lax.div(me, jnp.int32(CORES))
    along_x = [[(i, (i + k * CORES) % segs) for i in range(segs)] for k in range(chips)]
    across = [(i, i ^ 1) for i in range(segs)]
    phased, slots = prepare(records, owners.T, sources)
    slots = slots.reshape(sources, -1, GROUP * LANES)
    other = lax.ppermute(phased, "seg", across)
    passing = lax.all_to_all(slots, "sta", 0, 0, tiled=True)
    passing = passing.reshape(segs, -1, GROUP * LANES)
    pair = jnp.concatenate([phased, other], axis=0)
    pairs = [pair] + [lax.ppermute(pair, "seg", along_x[k]) for k in range(1, chips)]
    whitened, phases = own_part(me.reshape(1), pairs, segs)
    shifted, extra = shift(phases)
    passing, shifted, extra = lax.optimization_barrier((passing, shifted, extra))
    near = [passing]
    for k in range(1, chips):
        at = ((chip + k) & (chips - 1)) * CORES
        block = lax.dynamic_slice_in_dim(passing, at, CORES, 0)
        near.append(lax.ppermute(block, "seg", along_x[k]))
    other_core = 1 - (me & (CORES - 1))
    give = [lax.dynamic_slice_in_dim(passing, chip * CORES + other_core, 1, 0)]
    give += [lax.dynamic_slice_in_dim(block, other_core, 1, 0) for block in near[1:]]
    far = lax.ppermute(jnp.concatenate(give, axis=0), "seg", across)
    result = correlate(me.reshape(1), near, far, shifted, extra, segs)
    return whitened, result.reshape(-1, stations, LAGS)


def solution(mesh):
    return jax.shard_map(
        on_device,
        mesh=mesh,
        in_specs=(P("sta", "seg"), P("sta", None)),
        out_specs=(P("sta", "seg"), P("seg", "sta", None)),
        check_vma=False,
    )
```

```python
import math

import jax
import jax.numpy as jnp
from jax import lax
from jax.experimental import pallas as pl
from jax.experimental.pallas import tpu as pltpu
from jax.sharding import PartitionSpec as P

LAGS = 512
BS = 2
SLOTS = 2
WATER = 0.5
EPSILON = 1e-06

PH = 16
LANES = 128
FINE = 32
CORES = 2
GROUP = 4
F32 = jnp.float32
BF16 = jnp.bfloat16
MIB = 1 << 20


def dot(a, b):
    return lax.dot_general(a, b, (((1,), (0,)), ((), ())), preferred_element_type=F32)


def dot_t(a, b):
    return lax.dot_general(a, b, (((1,), (1,)), ((), ())), preferred_element_type=F32)


def in_hbm(x):
    return pltpu.with_memory_space_constraint(x, pltpu.HBM)


def iota(shape, axis):
    return lax.broadcasted_iota(jnp.int32, shape, axis)


def cos_sin(phase, period):
    phase = phase & (period - 1)
    phase = jnp.where(phase >= period // 2, phase - period, phase)
    theta = phase.astype(F32) * (2.0 * math.pi / period)
    square = theta * theta
    cosine = jnp.full(theta.shape, 1.0 / math.factorial(20), F32)
    sine = jnp.full(theta.shape, 1.0 / math.factorial(21), F32)
    for n in range(9, -1, -1):
        cosine = (1.0 if n % 2 == 0 else -1.0) / math.factorial(2 * n) + square * cosine
        sine = (1.0 if n % 2 == 0 else -1.0) / math.factorial(2 * n + 1) + square * sine
    return cosine, sine * theta


def spread():
    shape = (LANES, PH * LANES)
    source, target = iota(shape, 0), iota(shape, 1)
    hit = (target // LANES == source % PH) & (target % LANES == source // PH)
    return jnp.where(hit, 1.0, 0.0).astype(BF16)


def gather_back():
    shape = (LANES, PH * LANES)
    target, source = iota(shape, 0), iota(shape, 1)
    lane = source % LANES
    place = FINE // PH * (lane % (LANES // 2)) + lane // (LANES // 2)
    hit = (source // LANES == target % PH) & (place == target // PH)
    return jnp.where(hit, 1.0, 0.0).astype(BF16)


def fold(trace_ref, scale, segs, put):
    rows = trace_ref.shape[1] // segs
    low = iota((rows, LANES), 1) < LANES // 2
    for p in range(PH):
        for s in range(segs // 2):
            first = trace_ref[p, 2 * s * rows : (2 * s + 1) * rows, :] * scale
            second = trace_ref[p, (2 * s + 1) * rows : (2 * s + 2) * rows, :] * scale
            put(p, s, jnp.where(low, first, pltpu.roll(second, LANES // 2, 1)).astype(BF16))
            put(p + PH, s, jnp.where(low, pltpu.roll(first, LANES // 2, 1), second).astype(BF16))


def prepare_kernel(
    owner_count, records_hbm, owners_hbm, phased_hbm, slots_hbm,
    records_ref, owners_ref, phased_ref, slots_ref, sems,
):
    loads = [
        pltpu.make_async_copy(records_hbm, records_ref, sems.at[0]),
        pltpu.make_async_copy(owners_hbm, owners_ref, sems.at[1]),
    ]
    for load in loads:
        load.start()
    stations, length = records_ref.shape
    dests, blocks = owners_ref.shape
    per_tile = LANES // PH
    one_hot = spread()
    loads[0].wait()
    tiles = jnp.concatenate(
        [records_ref[:, t * LANES : (t + 1) * LANES] for t in range(length // LANES)], axis=0
    )
    parts = dot(tiles, one_hot)
    phases = []
    for p in range(PH):
        total = None
        for t in range(length // LANES):
            part = parts[t * stations : (t + 1) * stations, p * LANES : (p + 1) * LANES]
            part = pltpu.roll(part, per_tile * t, 1) if t else part
            total = part if total is None else total + part
        phases.append(total.astype(BF16))
    for p in range(PH):
        phased_ref[:, p * LANES : (p + 1) * LANES] = phases[p]
    stores = [pltpu.make_async_copy(phased_ref, phased_hbm, sems.at[2])]
    stores[0].start()
    high = PH // GROUP
    stacked = jnp.concatenate(
        [jnp.concatenate(phases[h * GROUP : (h + 1) * GROUP], axis=1) for h in range(high)], axis=0
    )
    rows, width = owner_count * high * SLOTS * BS, high * stations
    k_of, column = iota((blocks, width), 0), iota((blocks, width), 1)
    expand = jnp.where(column % stations // BS == k_of, 1.0, 0.0)
    loads[1].wait()
    named = lax.dot_general(
        owners_ref[...].astype(F32), expand, (((1,), (0,)), ((), ())), preferred_element_type=F32
    )
    row, col = iota((rows, width), 0), iota((rows, width), 1)
    owner = (row // (high * SLOTS * BS)).astype(F32)
    wanted = jnp.zeros((rows, width), F32)
    for d in range(dests):
        wanted = jnp.maximum(wanted, jnp.where(named[d : d + 1, :] == owner, 1.0, 0.0))
    first, second = iota((width, width), 0), iota((width, width), 1)
    earlier = (
        (first // stations == second // stations)
        & (first % stations // BS < second % stations // BS)
        & (first % BS == 0)
    )
    rank = dot(wanted.astype(BF16), jnp.where(earlier, 1.0, 0.0).astype(BF16))
    slot = (row // BS % SLOTS).astype(F32)
    right = (
        (rank == slot)
        & (row % BS == col % BS)
        & (row // (SLOTS * BS) % high == col // stations)
    )
    select = jnp.where(right, wanted, 0.0).astype(BF16)
    parts, size = 4, rows // 4
    for i in range(parts):
        at = pl.ds(i * size, size)
        slots_ref[at, :] = dot(select[i * size : (i + 1) * size], stacked).astype(BF16)
        stores.append(pltpu.make_async_copy(slots_ref.at[at, :], slots_hbm.at[at, :], sems.at[3 + i]))
        stores[-1].start()
    for store in stores:
        store.wait()


def prepare(records, owners, owner_count):
    stations, length = records.shape
    rows = owner_count * SLOTS * BS * PH // GROUP
    return pl.pallas_call(
        lambda *refs: prepare_kernel(owner_count, *refs),
        out_shape=(
            pltpu.HBM((stations, length), BF16),
            pltpu.HBM((rows, GROUP * LANES), BF16),
        ),
        in_specs=[pl.BlockSpec(memory_space=pltpu.HBM)] * 2,
        out_specs=[pl.BlockSpec(memory_space=pltpu.HBM)] * 2,
        scratch_shapes=[
            pltpu.VMEM(records.shape, records.dtype),
            pltpu.VMEM(owners.shape, owners.dtype),
            pltpu.VMEM((stations, length), BF16),
            pltpu.VMEM((rows, GROUP * LANES), BF16),
            pltpu.SemaphoreType.DMA((7,)),
        ],
        compiler_params=pltpu.CompilerParams(vmem_limit_bytes=16 * MIB),
        cost_estimate=pl.CostEstimate(
            flops=100 * MIB, bytes_accessed=2 * MIB, transcendentals=0
        ),
        name="prepare",
    )(in_hbm(records), in_hbm(owners))


def copy_kernel(x_hbm, out_hbm, sem):
    copy = pltpu.make_async_copy(x_hbm, out_hbm, sem)
    copy.start()
    copy.wait()


def copied(x):
    return pl.pallas_call(
        copy_kernel,
        out_shape=pltpu.HBM(x.shape, x.dtype),
        in_specs=[pl.BlockSpec(memory_space=pltpu.HBM)],
        out_specs=pl.BlockSpec(memory_space=pltpu.HBM),
        scratch_shapes=[pltpu.SemaphoreType.DMA(())],
        cost_estimate=pl.CostEstimate(flops=1000 * MIB, bytes_accessed=MIB, transcendentals=0),
        name="copied",
    )(in_hbm(x))


def add(a, b):
    return a[0] + b[0], a[1] + b[1]


def sub(a, b):
    return a[0] - b[0], a[1] - b[1]


def times_i(a, sign):
    return (-a[1], a[0]) if sign > 0 else (a[1], -a[0])


def times(a, b):
    return a[0] * b[0] - a[1] * b[1], a[0] * b[1] + a[1] * b[0]


def unit(a, k, sign):
    k %= 16
    if k == 0:
        return a
    if k == 4:
        return times_i(a, sign)
    if k == 8:
        return -a[0], -a[1]
    if k == 12:
        return times_i(a, -sign)
    angle = 2.0 * math.pi * k / 16
    return times(a, (math.cos(angle), sign * math.sin(angle)))


def four(a, sign):
    s, d = add(a[0], a[2]), sub(a[0], a[2])
    t, e = add(a[1], a[3]), times_i(sub(a[1], a[3]), sign)
    return [add(s, t), add(d, e), sub(s, t), sub(d, e)]


def forward_sixteen(v):
    inner = [four([v[4 * p1 + p0] for p1 in range(4)], 1) for p0 in range(4)]
    out = [None] * 8
    for fa in range(4):
        u = [unit(inner[p0][fa], p0 * fa, 1) for p0 in range(4)]
        s, t = add(u[0], u[2]), add(u[1], u[3])
        out[fa] = add(s, t)
        out[fa + 4] = add(sub(u[0], u[2]), times_i(sub(u[1], u[3]), 1))
        if fa == 0:
            last = s[0] - t[0]
    return out, last


def inverse_sixteen(f):
    out = [None] * 16
    for p0 in range(4):
        inner = []
        for fa in range(4):
            turned = unit(f[fa + 4], 4 * p0, -1)
            inner.append(unit(add(f[fa], turned), p0 * fa, -1))
        for p1, value in enumerate(four(inner, -1)):
            out[4 * p1 + p0] = value
    return out


def seg_total(values, segs):
    rows = values.shape[0] // segs
    total = values[:rows]
    for s in range(1, segs):
        total = total + values[s * rows : (s + 1) * rows]
    return total


def whiten(x_ref, y_ref, f_ref, sum_ref, trace_ref, segs):
    rows = x_ref.shape[1]
    length = PH * LANES
    window = length * segs
    half = PH // 2
    n, k = iota((LANES, LANES), 0), iota((LANES, LANES), 1)
    cosine, sine = cos_sin(n * k, LANES)
    table = jnp.concatenate([cosine, sine], axis=1).astype(BF16)
    folded = FINE // PH * (k % (LANES // 2)) + k // (LANES // 2)
    back = jnp.concatenate(cos_sin(n * folded, LANES), axis=0).astype(BF16)
    turn_cos, turn_sin = cos_sin(iota((PH, LANES), 0) * iota((PH, LANES), 1), length)
    for p in range(PH):
        y_ref[p] = dot(x_ref[p], table)
    lane = iota((8, LANES), 1)

    def forward(i, _):
        at = pl.ds(pl.multiple_of(i * 8, 8), 8)
        v = []
        for p in range(PH):
            y = y_ref[p, at, :LANES], y_ref[p, at, LANES:]
            v.append(times(y, (turn_cos[p : p + 1], turn_sin[p : p + 1])) if p else y)
        out, last = forward_sixteen(v)
        total = None
        for j, (re, im) in enumerate(out):
            if j == 0:
                mag = jnp.where(lane == 0, jnp.abs(re), jnp.sqrt(re * re + im * im))
                im = jnp.where(lane == 0, last, im)
                total = jnp.where(lane == 0, 0.5 * (jnp.abs(re) + jnp.abs(im)), mag)
            else:
                mag = jnp.sqrt(re * re + im * im)
                total = total + mag
            f_ref[j, at, :] = re
            f_ref[half + j, at, :] = im
            f_ref[2 * half + j, at, :] = mag
        sum_ref[at, :] = total
        return 0

    lax.fori_loop(0, rows // 8, forward, 0, unroll=4)
    amp = 2.0 * jnp.sum(seg_total(sum_ref[...], segs), axis=1, keepdims=True)
    level = WATER * amp / window + EPSILON
    sum_ref[...] = jnp.concatenate(
        [jnp.broadcast_to(level, (rows // segs, LANES))] * segs, axis=0
    )

    def inverse(i, _):
        at = pl.ds(pl.multiple_of(i * 8, 8), 8)
        level = sum_ref[at, :]
        f = []
        for j in range(half):
            re, im, mag = f_ref[j, at, :], f_ref[half + j, at, :], f_ref[2 * half + j, at, :]
            if j == 0:
                edge = im / (jnp.abs(im) + level)
                share = 2.0 / (mag + level)
                f.append(
                    (
                        jnp.where(lane == 0, 0.5, 1.0) * (re * share),
                        jnp.where(lane == 0, 0.0, im * share),
                    )
                )
                edge = jnp.where(lane == 0, edge, 0.0)
            else:
                share = 2.0 / (mag + level)
                f.append((re * share, im * share))
        for p, z in enumerate(inverse_sixteen(f)):
            if p:
                z = times(z, (turn_cos[p : p + 1], -turn_sin[p : p + 1]))
            y_ref[p, at, :LANES] = z[0] - edge if p % 2 else z[0] + edge
            y_ref[p, at, LANES:] = z[1]
        return 0

    lax.fori_loop(0, rows // 8, inverse, 0, unroll=4)
    energy = jnp.zeros((rows, LANES), F32)
    for p in range(PH):
        trace = dot(y_ref[p].astype(BF16), back) * (1.0 / length)
        energy = energy + trace * trace
        trace_ref[p] = trace
    energy = jnp.sum(seg_total(energy, segs), axis=1, keepdims=True)
    return lax.rsqrt(energy / window + EPSILON)


def whiten_scratch(rows):
    return [
        pltpu.VMEM((PH, rows, LANES), BF16),
        pltpu.VMEM((PH, rows, 2 * LANES), F32),
        pltpu.VMEM((3 * PH // 2, rows, LANES), F32),
        pltpu.VMEM((rows, LANES), F32),
        pltpu.VMEM((PH, rows, LANES), F32),
    ]


def own_kernel(
    segs, me_ref, near_ref, far_ref, white_ref, phase_ref, x_ref, y_ref, f_ref, sum_ref, trace_ref
):
    rows, length = x_ref.shape[1], PH * LANES
    stations = rows // segs
    per_tile = LANES // PH
    me, chips = me_ref[0], segs // CORES
    for i in range(chips):
        chip = (lax.div(me, CORES) + chips - i) & (chips - 1)
        for j, ref in enumerate((near_ref, far_ref)):
            core = (me + j) & (CORES - 1)
            at = pl.ds(pl.multiple_of((chip * CORES + core) * stations, stations), stations)
            for p in range(PH):
                x_ref[p, at, :] = ref[
                    i * stations : (i + 1) * stations, p * LANES : (p + 1) * LANES
                ]
    scale = whiten(x_ref, y_ref, f_ref, sum_ref, trace_ref, segs)
    def put(p, s, tile):
        phase_ref[s, (FINE - 1 - p) * stations : (FINE - p) * stations, :] = tile.astype(F32)

    fold(trace_ref, scale, segs, put)
    mine = pl.ds(pl.multiple_of(me_ref[0] * stations, stations), stations)
    tiles = [trace_ref[p, mine, :] * scale for p in range(PH)]
    moved = []
    for t in range(length // LANES):
        turn = (LANES - per_tile // 2 * t) % LANES
        moved.append(
            jnp.concatenate(
                [(pltpu.roll(x, turn, 1) if turn else x).astype(BF16) for x in tiles], axis=1
            )
        )
    natural = dot_t(jnp.concatenate(moved, axis=0), gather_back()).astype(BF16)
    for t in range(length // LANES):
        white_ref[:, t * LANES : (t + 1) * LANES] = natural[t * stations : (t + 1) * stations]


def own_part(me, pairs, segs):
    rows, length = len(pairs) * pairs[0].shape[0], pairs[0].shape[1]
    stations = rows // segs
    return pl.pallas_call(
        lambda *refs: own_kernel(segs, *refs),
        out_shape=(
            jax.ShapeDtypeStruct((stations, length), BF16),
            jax.ShapeDtypeStruct((segs // 2, FINE * stations, LANES), F32),
        ),
        in_specs=[
            pl.BlockSpec(memory_space=pltpu.SMEM),
            *[pl.BlockSpec(memory_space=pltpu.VMEM)] * len(pairs),
        ],
        out_specs=[pl.BlockSpec(memory_space=pltpu.VMEM)] * 2,
        scratch_shapes=whiten_scratch(rows),
        compiler_params=pltpu.CompilerParams(vmem_limit_bytes=32 * MIB),
        cost_estimate=pl.CostEstimate(
            flops=2000 * MIB, bytes_accessed=4 * MIB, transcendentals=0
        ),
        name="own",
    )(me, *pairs)


def shift_kernel(stations, phase_ref, shifted_hbm, extra_hbm, shifted_ref, extra_ref, sems):
    count = LAGS // FINE
    tiles = phase_ref.shape[0]
    total = tiles * LANES
    lane = iota((FINE, total), 1)

    def copies(a):
        to = shifted_hbm.at[pl.ds(pl.multiple_of(a * LAGS, LAGS), LAGS), :]
        to_extra = extra_hbm.at[pl.ds(pl.multiple_of(a * FINE, FINE), FINE), :]
        return (
            pltpu.make_async_copy(shifted_ref.at[a], to, sems.at[0, a]),
            pltpu.make_async_copy(extra_ref.at[a], to_extra, sems.at[1, a]),
        )

    def body(a, _):
        block = jnp.concatenate(
            [phase_ref[s, pl.ds(a, FINE, stride=stations), :] for s in range(tiles)], axis=1
        )
        for i in range(-1, count):
            m = i + 1 - count // 2
            moved = pltpu.roll(block, m % total, 1) if m else block
            if m > 0:
                moved = jnp.where(lane >= m, moved, 0.0)
            elif m < 0:
                moved = jnp.where(lane < total + m, moved, 0.0)
            moved = moved.astype(BF16)
            if i < 0:
                extra_ref[a] = moved
            else:
                shifted_ref[a, i * FINE : (i + 1) * FINE, :] = moved
        for copy in copies(a):
            copy.start()
        return 0

    lax.fori_loop(0, stations, body, 0)

    def finish(a, _):
        for copy in copies(a):
            copy.wait()
        return 0

    lax.fori_loop(0, stations, finish, 0)


def shift(phases):
    stations = phases.shape[1] // FINE
    total = phases.shape[0] * LANES
    return pl.pallas_call(
        lambda *refs: shift_kernel(stations, *refs),
        out_shape=(
            pltpu.HBM((stations * LAGS, total), BF16),
            pltpu.HBM((stations * FINE, total), BF16),
        ),
        in_specs=[pl.BlockSpec(memory_space=pltpu.VMEM)],
        out_specs=[pl.BlockSpec(memory_space=pltpu.HBM)] * 2,
        scratch_shapes=[
            pltpu.VMEM((stations, LAGS, total), BF16),
            pltpu.VMEM((stations, FINE, total), BF16),
            pltpu.SemaphoreType.DMA((2, stations)),
        ],
        compiler_params=pltpu.CompilerParams(vmem_limit_bytes=16 * MIB),
        cost_estimate=pl.CostEstimate(
            flops=1, bytes_accessed=9 * MIB, transcendentals=0
        ),
        name="shift",
    )(phases)


def correlate_kernel(segs, me_ref, *refs):
    chips = segs // CORES
    near, (far_ref, shifted_hbm, extra_hbm, out_ref), refs = (
        refs[:chips],
        refs[chips : chips + 4],
        refs[chips + 4 :],
    )
    x_ref, y_ref, f_ref, sum_ref, trace_ref, phase_ref, edge_ref, total_ref = refs[:8]
    shifted_ref, extra_ref, even_ref, odd_ref, sems = refs[8:]
    rows = x_ref.shape[1]
    received = rows // segs
    stations = shifted_ref.shape[0]
    copies = [pltpu.make_async_copy(extra_hbm, extra_ref, sems.at[stations])]
    for a in range(stations):
        block = shifted_hbm.at[pl.ds(a * LAGS, LAGS), :]
        copies.append(pltpu.make_async_copy(block, shifted_ref.at[a], sems.at[a]))
    for copy in copies:
        copy.start()
    high, unit_rows = PH // GROUP, SLOTS * BS
    per_seg = high * received
    to, at_row = iota((per_seg, per_seg), 0), iota((per_seg, per_seg), 1)
    wanted = (
        to % received // unit_rows * (high * unit_rows) + to // received * unit_rows
    ) + to % unit_rows
    order = jnp.where(at_row == wanted, 1.0, 0.0).astype(BF16)
    me = me_ref[0]
    mine = me & (CORES - 1)
    for s in range(segs):
        i = s // CORES
        chip = (lax.div(me, CORES) + chips - i) & (chips - 1)
        if s % CORES:
            source, seg = far_ref[i], chip * CORES + 1 - mine
        else:
            source = near[i][(chip * CORES if i == 0 else 0) + mine]
            seg = chip * CORES + mine
        block = dot(order, source).astype(BF16)
        at = pl.ds(pl.multiple_of(seg * received, received), received)
        for p in range(PH):
            x_ref[p, at, :] = block[
                p // GROUP * received : (p // GROUP + 1) * received,
                p % GROUP * LANES : (p % GROUP + 1) * LANES,
            ]
    scale = whiten(x_ref, y_ref, f_ref, sum_ref, trace_ref, segs)

    def put(p, s, tile):
        phase_ref[p * received : (p + 1) * received, s * LANES : (s + 1) * LANES] = tile

    fold(trace_ref, scale, segs, put)
    copies[0].wait()
    edge = dot_t(phase_ref[...], extra_ref[...])
    width = stations * FINE
    lag = iota((received, width), 1) % FINE
    sums = jnp.zeros((received, width), F32)
    for p in range(FINE):
        block = edge[p * received : (p + 1) * received]
        turn = (p + 1 - FINE) % width
        block = pltpu.roll(block, turn, 1) if turn else block
        sums = sums + jnp.where(lag <= p, block, 0.0)
    edge_ref[...] = sums
    lane = iota((received, LAGS), 1)
    norm = 1.0 / math.sqrt(segs * PH * LANES)

    def multiply(a):
        block = shifted_hbm.at[pl.ds(pl.multiple_of(a * LAGS, LAGS), LAGS), :]
        pltpu.make_async_copy(block, shifted_ref.at[a], sems.at[a]).wait()
        return dot_t(phase_ref[...], shifted_ref[a])

    def combine(a, product_ref):
        first = pltpu.roll(edge_ref[...], (stations - a) * FINE, 1)
        sums = jnp.where(lane < FINE, first[:, :LAGS], 0.0)
        for p in range(FINE):
            block = pltpu.roll(product_ref[p * received : (p + 1) * received], p + 1, 1)
            sums = sums + jnp.where(lane > p, block, 0.0)
        sums = sums * norm
        for c in range(LAGS // LANES):
            total_ref[c, pl.ds(a, received, stride=stations), :] = sums[
                :, c * LANES : (c + 1) * LANES
            ]

    even_ref[...] = multiply(0)

    def body(i, _):
        odd_ref[...] = multiply(2 * i + 1)
        combine(2 * i, even_ref)
        even_ref[...] = multiply(2 * i + 2)
        combine(2 * i + 1, odd_ref)
        return 0

    lax.fori_loop(0, stations // 2 - 1, body, 0)
    odd_ref[...] = multiply(stations - 1)
    combine(stations - 2, even_ref)
    combine(stations - 1, odd_ref)
    for c in range(LAGS // LANES):
        out_ref[:, c * LANES : (c + 1) * LANES] = total_ref[c].astype(BF16)


def correlate(me, near, far, shifted, extra, segs):
    rows = segs * far.shape[1] // (PH // GROUP)
    count = rows // segs
    stations = shifted.shape[0] // LAGS
    total = shifted.shape[1]
    return pl.pallas_call(
        lambda *refs: correlate_kernel(segs, *refs),
        out_shape=jax.ShapeDtypeStruct((count * stations, LAGS), BF16),
        in_specs=[
            pl.BlockSpec(memory_space=pltpu.SMEM),
            *[pl.BlockSpec(memory_space=pltpu.VMEM)] * (len(near) + 1),
            pl.BlockSpec(memory_space=pltpu.HBM),
            pl.BlockSpec(memory_space=pltpu.HBM),
        ],
        out_specs=pl.BlockSpec(memory_space=pltpu.VMEM),
        scratch_shapes=[
            *whiten_scratch(rows),
            pltpu.VMEM((count * FINE, total), BF16),
            pltpu.VMEM((count, stations * FINE), F32),
            pltpu.VMEM((LAGS // LANES, count * stations, LANES), F32),
            pltpu.VMEM((stations, LAGS, total), BF16),
            pltpu.VMEM((stations * FINE, total), BF16),
            pltpu.VMEM((count * FINE, LAGS), F32),
            pltpu.VMEM((count * FINE, LAGS), F32),
            pltpu.SemaphoreType.DMA((stations + 1,)),
        ],
        compiler_params=pltpu.CompilerParams(vmem_limit_bytes=48 * MIB),
        cost_estimate=pl.CostEstimate(
            flops=6000 * MIB, bytes_accessed=20 * MIB, transcendentals=0
        ),
        name="correlate",
    )(
        me,
        *near,
        far,
        in_hbm(shifted),
        in_hbm(extra),
    )


def on_device(records, owners):
    stations, length = records.shape
    segs, sources = lax.axis_size("seg"), lax.axis_size("sta")
    chips = segs // CORES
    me = lax.axis_index("seg")
    chip = lax.div(me, jnp.int32(CORES))
    along_x = [[(i, (i + k * CORES) % segs) for i in range(segs)] for k in range(chips)]
    across = [(i, i ^ 1) for i in range(segs)]
    phased, slots = prepare(records, owners.T, sources)
    slots = slots.reshape(sources, -1, GROUP * LANES)
    phased = copied(phased)
    passing = lax.all_to_all(slots, "sta", 0, 0, tiled=True)
    passing = passing.reshape(segs, -1, GROUP * LANES)
    own = [phased] + [lax.ppermute(phased, "seg", along_x[k]) for k in range(1, chips)]
    own = jnp.concatenate(own, axis=0)
    other = lax.ppermute(own, "seg", across)
    whitened, phases = own_part(me.reshape(1), (own, other), segs)
    passing, phases = lax.optimization_barrier((passing, phases))
    shifted, extra = shift(phases)
    near = [passing]
    for k in range(1, chips):
        at = ((chip + k) & (chips - 1)) * CORES
        block = lax.dynamic_slice_in_dim(passing, at, CORES, 0)
        near.append(lax.ppermute(block, "seg", along_x[k]))
    other_core = 1 - (me & (CORES - 1))
    give = [lax.dynamic_slice_in_dim(passing, chip * CORES + other_core, 1, 0)]
    give += [lax.dynamic_slice_in_dim(block, other_core, 1, 0) for block in near[1:]]
    give, shifted, extra = lax.optimization_barrier((jnp.concatenate(give, axis=0), shifted, extra))
    far = lax.ppermute(give, "seg", across)
    result = correlate(me.reshape(1), near, far, shifted, extra, segs)
    return whitened, result.reshape(-1, stations, LAGS)


def solution(mesh):
    return jax.shard_map(
        on_device,
        mesh=mesh,
        in_specs=(P("sta", "seg"), P("sta", None)),
        out_specs=(P("sta", "seg"), P("seg", "sta", None)),
        check_vma=False,
    )
```

```python
import math

import jax
import jax.numpy as jnp
from jax import lax
from jax.experimental import pallas as pl
from jax.experimental.pallas import tpu as pltpu
from jax.sharding import PartitionSpec as P

LAGS = 512
BS = 2
SLOTS = 2
WATER = 0.5
EPSILON = 1e-06

PH = 16
LANES = 128
FINE = 32
CORES = 2
GROUP = 4
F32 = jnp.float32
BF16 = jnp.bfloat16
MIB = 1 << 20


def dot(a, b):
    return lax.dot_general(a, b, (((1,), (0,)), ((), ())), preferred_element_type=F32)


def dot_t(a, b):
    return lax.dot_general(a, b, (((1,), (1,)), ((), ())), preferred_element_type=F32)


def in_hbm(x):
    return pltpu.with_memory_space_constraint(x, pltpu.HBM)


def iota(shape, axis):
    return lax.broadcasted_iota(jnp.int32, shape, axis)


def cos_sin(phase, period):
    phase = phase & (period - 1)
    phase = jnp.where(phase >= period // 2, phase - period, phase)
    theta = phase.astype(F32) * (2.0 * math.pi / period)
    square = theta * theta
    cosine = jnp.full(theta.shape, 1.0 / math.factorial(20), F32)
    sine = jnp.full(theta.shape, 1.0 / math.factorial(21), F32)
    for n in range(9, -1, -1):
        cosine = (1.0 if n % 2 == 0 else -1.0) / math.factorial(2 * n) + square * cosine
        sine = (1.0 if n % 2 == 0 else -1.0) / math.factorial(2 * n + 1) + square * sine
    return cosine, sine * theta


def spread():
    shape = (LANES, PH * LANES)
    source, target = iota(shape, 0), iota(shape, 1)
    hit = (target // LANES == source % PH) & (target % LANES == source // PH)
    return jnp.where(hit, 1.0, 0.0).astype(BF16)


def gather_back():
    shape = (LANES, PH * LANES)
    target, source = iota(shape, 0), iota(shape, 1)
    lane = source % LANES
    place = FINE // PH * (lane % (LANES // 2)) + lane // (LANES // 2)
    hit = (source // LANES == target % PH) & (place == target // PH)
    return jnp.where(hit, 1.0, 0.0).astype(BF16)


def fold(trace_ref, scale, segs, put):
    rows = trace_ref.shape[1] // segs
    low = iota((rows, LANES), 1) < LANES // 2
    for p in range(PH):
        for s in range(segs // 2):
            first = trace_ref[p, 2 * s * rows : (2 * s + 1) * rows, :] * scale
            second = trace_ref[p, (2 * s + 1) * rows : (2 * s + 2) * rows, :] * scale
            put(p, s, jnp.where(low, first, pltpu.roll(second, LANES // 2, 1)).astype(BF16))
            put(p + PH, s, jnp.where(low, pltpu.roll(first, LANES // 2, 1), second).astype(BF16))


def prepare_kernel(
    owner_count, records_hbm, owners_hbm, phased_hbm, slots_hbm,
    records_ref, owners_ref, phased_ref, slots_ref, sems,
):
    loads = [
        pltpu.make_async_copy(records_hbm, records_ref, sems.at[0]),
        pltpu.make_async_copy(owners_hbm, owners_ref, sems.at[1]),
    ]
    for load in loads:
        load.start()
    stations, length = records_ref.shape
    dests, blocks = owners_ref.shape
    per_tile = LANES // PH
    one_hot = spread()
    loads[0].wait()
    tiles = jnp.concatenate(
        [records_ref[:, t * LANES : (t + 1) * LANES] for t in range(length // LANES)], axis=0
    )
    parts = dot(tiles, one_hot)
    phases = []
    for p in range(PH):
        total = None
        for t in range(length // LANES):
            part = parts[t * stations : (t + 1) * stations, p * LANES : (p + 1) * LANES]
            part = pltpu.roll(part, per_tile * t, 1) if t else part
            total = part if total is None else total + part
        phases.append(total.astype(BF16))
    for p in range(PH):
        phased_ref[:, p * LANES : (p + 1) * LANES] = phases[p]
    stores = [pltpu.make_async_copy(phased_ref, phased_hbm, sems.at[2])]
    stores[0].start()
    high = PH // GROUP
    stacked = jnp.concatenate(
        [jnp.concatenate(phases[h * GROUP : (h + 1) * GROUP], axis=1) for h in range(high)], axis=0
    )
    rows, width = owner_count * high * SLOTS * BS, high * stations
    k_of, column = iota((blocks, width), 0), iota((blocks, width), 1)
    expand = jnp.where(column % stations // BS == k_of, 1.0, 0.0)
    loads[1].wait()
    named = lax.dot_general(
        owners_ref[...].astype(F32), expand, (((1,), (0,)), ((), ())), preferred_element_type=F32
    )
    row, col = iota((rows, width), 0), iota((rows, width), 1)
    owner = (row // (high * SLOTS * BS)).astype(F32)
    wanted = jnp.zeros((rows, width), F32)
    for d in range(dests):
        wanted = jnp.maximum(wanted, jnp.where(named[d : d + 1, :] == owner, 1.0, 0.0))
    first, second = iota((width, width), 0), iota((width, width), 1)
    earlier = (
        (first // stations == second // stations)
        & (first % stations // BS < second % stations // BS)
        & (first % BS == 0)
    )
    rank = dot(wanted.astype(BF16), jnp.where(earlier, 1.0, 0.0).astype(BF16))
    slot = (row // BS % SLOTS).astype(F32)
    right = (
        (rank == slot)
        & (row % BS == col % BS)
        & (row // (SLOTS * BS) % high == col // stations)
    )
    select = jnp.where(right, wanted, 0.0).astype(BF16)
    parts, size = 4, rows // 4
    for i in range(parts):
        at = pl.ds(i * size, size)
        slots_ref[at, :] = dot(select[i * size : (i + 1) * size], stacked).astype(BF16)
        stores.append(pltpu.make_async_copy(slots_ref.at[at, :], slots_hbm.at[at, :], sems.at[3 + i]))
        stores[-1].start()
    for store in stores:
        store.wait()


def prepare(records, owners, owner_count):
    stations, length = records.shape
    rows = owner_count * SLOTS * BS * PH // GROUP
    return pl.pallas_call(
        lambda *refs: prepare_kernel(owner_count, *refs),
        out_shape=(
            pltpu.HBM((stations, length), BF16),
            pltpu.HBM((rows, GROUP * LANES), BF16),
        ),
        in_specs=[pl.BlockSpec(memory_space=pltpu.HBM)] * 2,
        out_specs=[pl.BlockSpec(memory_space=pltpu.HBM)] * 2,
        scratch_shapes=[
            pltpu.VMEM(records.shape, records.dtype),
            pltpu.VMEM(owners.shape, owners.dtype),
            pltpu.VMEM((stations, length), BF16),
            pltpu.VMEM((rows, GROUP * LANES), BF16),
            pltpu.SemaphoreType.DMA((7,)),
        ],
        compiler_params=pltpu.CompilerParams(vmem_limit_bytes=16 * MIB),
        cost_estimate=pl.CostEstimate(
            flops=100 * MIB, bytes_accessed=2 * MIB, transcendentals=0
        ),
        name="prepare",
    )(in_hbm(records), in_hbm(owners))


def add(a, b):
    return a[0] + b[0], a[1] + b[1]


def sub(a, b):
    return a[0] - b[0], a[1] - b[1]


def times_i(a, sign):
    return (-a[1], a[0]) if sign > 0 else (a[1], -a[0])


def times(a, b):
    return a[0] * b[0] - a[1] * b[1], a[0] * b[1] + a[1] * b[0]


def unit(a, k, sign):
    k %= 16
    if k == 0:
        return a
    if k == 4:
        return times_i(a, sign)
    if k == 8:
        return -a[0], -a[1]
    if k == 12:
        return times_i(a, -sign)
    angle = 2.0 * math.pi * k / 16
    return times(a, (math.cos(angle), sign * math.sin(angle)))


def four(a, sign):
    s, d = add(a[0], a[2]), sub(a[0], a[2])
    t, e = add(a[1], a[3]), times_i(sub(a[1], a[3]), sign)
    return [add(s, t), add(d, e), sub(s, t), sub(d, e)]


def forward_sixteen(v):
    inner = [four([v[4 * p1 + p0] for p1 in range(4)], 1) for p0 in range(4)]
    out = [None] * 8
    for fa in range(4):
        u = [unit(inner[p0][fa], p0 * fa, 1) for p0 in range(4)]
        s, t = add(u[0], u[2]), add(u[1], u[3])
        out[fa] = add(s, t)
        out[fa + 4] = add(sub(u[0], u[2]), times_i(sub(u[1], u[3]), 1))
        if fa == 0:
            last = s[0] - t[0]
    return out, last


def inverse_sixteen(f):
    out = [None] * 16
    for p0 in range(4):
        inner = []
        for fa in range(4):
            turned = unit(f[fa + 4], 4 * p0, -1)
            inner.append(unit(add(f[fa], turned), p0 * fa, -1))
        for p1, value in enumerate(four(inner, -1)):
            out[4 * p1 + p0] = value
    return out


def seg_total(values, segs):
    rows = values.shape[0] // segs
    total = values[:rows]
    for s in range(1, segs):
        total = total + values[s * rows : (s + 1) * rows]
    return total


def whiten(x_ref, y_ref, f_ref, sum_ref, trace_ref, segs):
    rows = x_ref.shape[1]
    length = PH * LANES
    window = length * segs
    half = PH // 2
    n, k = iota((LANES, LANES), 0), iota((LANES, LANES), 1)
    cosine, sine = cos_sin(n * k, LANES)
    table = jnp.concatenate([cosine, sine], axis=1).astype(BF16)
    folded = FINE // PH * (k % (LANES // 2)) + k // (LANES // 2)
    back = jnp.concatenate(cos_sin(n * folded, LANES), axis=0).astype(BF16)
    turn_cos, turn_sin = cos_sin(iota((PH, LANES), 0) * iota((PH, LANES), 1), length)
    for p in range(PH):
        y_ref[p] = dot(x_ref[p], table)
    lane = iota((8, LANES), 1)

    def forward(i, _):
        at = pl.ds(pl.multiple_of(i * 8, 8), 8)
        v = []
        for p in range(PH):
            y = y_ref[p, at, :LANES], y_ref[p, at, LANES:]
            v.append(times(y, (turn_cos[p : p + 1], turn_sin[p : p + 1])) if p else y)
        out, last = forward_sixteen(v)
        total = None
        for j, (re, im) in enumerate(out):
            if j == 0:
                mag = jnp.where(lane == 0, jnp.abs(re), jnp.sqrt(re * re + im * im))
                im = jnp.where(lane == 0, last, im)
                total = jnp.where(lane == 0, 0.5 * (jnp.abs(re) + jnp.abs(im)), mag)
            else:
                mag = jnp.sqrt(re * re + im * im)
                total = total + mag
            f_ref[j, at, :] = re
            f_ref[half + j, at, :] = im
            f_ref[2 * half + j, at, :] = mag
        sum_ref[at, :] = total
        return 0

    lax.fori_loop(0, rows // 8, forward, 0, unroll=4)
    amp = 2.0 * jnp.sum(seg_total(sum_ref[...], segs), axis=1, keepdims=True)
    level = WATER * amp / window + EPSILON
    sum_ref[...] = jnp.concatenate(
        [jnp.broadcast_to(level, (rows // segs, LANES))] * segs, axis=0
    )

    def inverse(i, _):
        at = pl.ds(pl.multiple_of(i * 8, 8), 8)
        level = sum_ref[at, :]
        f = []
        for j in range(half):
            re, im, mag = f_ref[j, at, :], f_ref[half + j, at, :], f_ref[2 * half + j, at, :]
            if j == 0:
                edge = im / (jnp.abs(im) + level)
                share = 2.0 / (mag + level)
                f.append(
                    (
                        jnp.where(lane == 0, 0.5, 1.0) * (re * share),
                        jnp.where(lane == 0, 0.0, im * share),
                    )
                )
                edge = jnp.where(lane == 0, edge, 0.0)
            else:
                share = 2.0 / (mag + level)
                f.append((re * share, im * share))
        for p, z in enumerate(inverse_sixteen(f)):
            if p:
                z = times(z, (turn_cos[p : p + 1], -turn_sin[p : p + 1]))
            y_ref[p, at, :LANES] = z[0] - edge if p % 2 else z[0] + edge
            y_ref[p, at, LANES:] = z[1]
        return 0

    lax.fori_loop(0, rows // 8, inverse, 0, unroll=4)
    energy = jnp.zeros((rows, LANES), F32)
    for p in range(PH):
        trace = dot(y_ref[p].astype(BF16), back) * (1.0 / length)
        energy = energy + trace * trace
        trace_ref[p] = trace
    energy = jnp.sum(seg_total(energy, segs), axis=1, keepdims=True)
    return lax.rsqrt(energy / window + EPSILON)


def whiten_scratch(rows):
    return [
        pltpu.VMEM((PH, rows, LANES), BF16),
        pltpu.VMEM((PH, rows, 2 * LANES), F32),
        pltpu.VMEM((3 * PH // 2, rows, LANES), F32),
        pltpu.VMEM((rows, LANES), F32),
        pltpu.VMEM((PH, rows, LANES), F32),
    ]


def own_kernel(segs, me_ref, *refs):
    pairs, refs = refs[: segs // CORES], refs[segs // CORES :]
    white_ref, phase_ref, x_ref, y_ref, f_ref, sum_ref, trace_ref = refs
    rows, length = x_ref.shape[1], PH * LANES
    stations = rows // segs
    per_tile = LANES // PH
    me, chips = me_ref[0], segs // CORES
    for i, ref in enumerate(pairs):
        chip = (lax.div(me, CORES) + chips - i) & (chips - 1)
        for j in range(CORES):
            core = (me + j) & (CORES - 1)
            at = pl.ds(pl.multiple_of((chip * CORES + core) * stations, stations), stations)
            for p in range(PH):
                x_ref[p, at, :] = ref[
                    j * stations : (j + 1) * stations, p * LANES : (p + 1) * LANES
                ]
    scale = whiten(x_ref, y_ref, f_ref, sum_ref, trace_ref, segs)
    def put(p, s, tile):
        phase_ref[s, (FINE - 1 - p) * stations : (FINE - p) * stations, :] = tile.astype(F32)

    fold(trace_ref, scale, segs, put)
    mine = pl.ds(pl.multiple_of(me_ref[0] * stations, stations), stations)
    tiles = [trace_ref[p, mine, :] * scale for p in range(PH)]
    moved = []
    for t in range(length // LANES):
        turn = (LANES - per_tile // 2 * t) % LANES
        moved.append(
            jnp.concatenate(
                [(pltpu.roll(x, turn, 1) if turn else x).astype(BF16) for x in tiles], axis=1
            )
        )
    natural = dot_t(jnp.concatenate(moved, axis=0), gather_back()).astype(BF16)
    for t in range(length // LANES):
        white_ref[:, t * LANES : (t + 1) * LANES] = natural[t * stations : (t + 1) * stations]


def own_part(me, pairs, segs):
    rows, length = len(pairs) * pairs[0].shape[0], pairs[0].shape[1]
    stations = rows // segs
    return pl.pallas_call(
        lambda *refs: own_kernel(segs, *refs),
        out_shape=(
            jax.ShapeDtypeStruct((stations, length), BF16),
            jax.ShapeDtypeStruct((segs // 2, FINE * stations, LANES), F32),
        ),
        in_specs=[
            pl.BlockSpec(memory_space=pltpu.SMEM),
            *[pl.BlockSpec(memory_space=pltpu.VMEM)] * len(pairs),
        ],
        out_specs=[pl.BlockSpec(memory_space=pltpu.VMEM)] * 2,
        scratch_shapes=whiten_scratch(rows),
        compiler_params=pltpu.CompilerParams(vmem_limit_bytes=32 * MIB),
        cost_estimate=pl.CostEstimate(
            flops=2000 * MIB, bytes_accessed=4 * MIB, transcendentals=0
        ),
        name="own",
    )(me, *pairs)


def shift_kernel(stations, phase_ref, shifted_hbm, extra_hbm, shifted_ref, extra_ref, sems):
    count = LAGS // FINE
    tiles = phase_ref.shape[0]
    lane = iota((FINE, LANES), 1)

    def copies(a):
        to = shifted_hbm.at[pl.ds(pl.multiple_of(a * LAGS, LAGS), LAGS), :]
        to_extra = extra_hbm.at[pl.ds(pl.multiple_of(a * FINE, FINE), FINE), :]
        return (
            pltpu.make_async_copy(shifted_ref.at[a], to, sems.at[0, a]),
            pltpu.make_async_copy(extra_ref.at[a], to_extra, sems.at[1, a]),
        )

    def body(a, _):
        block = [phase_ref[s, pl.ds(a, FINE, stride=stations), :] for s in range(tiles)]
        zero = jnp.zeros((FINE, LANES), F32)
        for i in range(-1, count):
            m = i + 1 - count // 2
            turned = [pltpu.roll(tile, m % LANES, 1) if m else tile for tile in block]
            for t in range(tiles):
                if m > 0:
                    moved = jnp.where(lane >= m, turned[t], turned[t - 1] if t else zero)
                elif m < 0:
                    later = turned[t + 1] if t + 1 < tiles else zero
                    moved = jnp.where(lane < LANES + m, turned[t], later)
                else:
                    moved = turned[t]
                cols = slice(t * LANES, (t + 1) * LANES)
                if i < 0:
                    extra_ref[a, :, cols] = moved.astype(BF16)
                else:
                    shifted_ref[a, i * FINE : (i + 1) * FINE, cols] = moved.astype(BF16)
        for copy in copies(a):
            copy.start()
        return 0

    lax.fori_loop(0, stations, body, 0, unroll=4)

    def finish(a, _):
        for copy in copies(a):
            copy.wait()
        return 0

    lax.fori_loop(0, stations, finish, 0)


def shift(phases):
    stations = phases.shape[1] // FINE
    total = phases.shape[0] * LANES
    return pl.pallas_call(
        lambda *refs: shift_kernel(stations, *refs),
        out_shape=(
            pltpu.HBM((stations * LAGS, total), BF16),
            pltpu.HBM((stations * FINE, total), BF16),
        ),
        in_specs=[pl.BlockSpec(memory_space=pltpu.VMEM)],
        out_specs=[pl.BlockSpec(memory_space=pltpu.HBM)] * 2,
        scratch_shapes=[
            pltpu.VMEM((stations, LAGS, total), BF16),
            pltpu.VMEM((stations, FINE, total), BF16),
            pltpu.SemaphoreType.DMA((2, stations)),
        ],
        compiler_params=pltpu.CompilerParams(vmem_limit_bytes=16 * MIB),
        cost_estimate=pl.CostEstimate(
            flops=1, bytes_accessed=9 * MIB, transcendentals=0
        ),
        name="shift",
    )(phases)


def correlate_kernel(segs, me_ref, *refs):
    chips = segs // CORES
    near, (far_ref, shifted_hbm, extra_hbm, out_ref), refs = (
        refs[:chips],
        refs[chips : chips + 4],
        refs[chips + 4 :],
    )
    x_ref, y_ref, f_ref, sum_ref, trace_ref, phase_ref, edge_ref, total_ref = refs[:8]
    shifted_ref, extra_ref, even_ref, odd_ref, sems = refs[8:]
    rows = x_ref.shape[1]
    received = rows // segs
    stations = shifted_ref.shape[0]
    copies = [pltpu.make_async_copy(extra_hbm, extra_ref, sems.at[stations])]
    for a in range(stations):
        block = shifted_hbm.at[pl.ds(a * LAGS, LAGS), :]
        copies.append(pltpu.make_async_copy(block, shifted_ref.at[a], sems.at[a]))
    for copy in copies:
        copy.start()
    high, unit_rows = PH // GROUP, SLOTS * BS
    per_seg = high * received
    to, at_row = iota((per_seg, per_seg), 0), iota((per_seg, per_seg), 1)
    wanted = (
        to % received // unit_rows * (high * unit_rows) + to // received * unit_rows
    ) + to % unit_rows
    order = jnp.where(at_row == wanted, 1.0, 0.0).astype(BF16)
    me = me_ref[0]
    mine = me & (CORES - 1)
    for s in range(segs):
        i = s // CORES
        chip = (lax.div(me, CORES) + chips - i) & (chips - 1)
        if s % CORES:
            source, seg = far_ref[i], chip * CORES + 1 - mine
        else:
            source = near[i][(chip * CORES if i == 0 else 0) + mine]
            seg = chip * CORES + mine
        block = dot(order, source).astype(BF16)
        at = pl.ds(pl.multiple_of(seg * received, received), received)
        for p in range(PH):
            x_ref[p, at, :] = block[
                p // GROUP * received : (p // GROUP + 1) * received,
                p % GROUP * LANES : (p % GROUP + 1) * LANES,
            ]
    scale = whiten(x_ref, y_ref, f_ref, sum_ref, trace_ref, segs)

    def put(p, s, tile):
        phase_ref[p * received : (p + 1) * received, s * LANES : (s + 1) * LANES] = tile

    fold(trace_ref, scale, segs, put)
    copies[0].wait()
    edge = dot_t(phase_ref[...], extra_ref[...])
    width = stations * FINE
    lag = iota((received, width), 1) % FINE
    sums = jnp.zeros((received, width), F32)
    for p in range(FINE):
        block = edge[p * received : (p + 1) * received]
        turn = (p + 1 - FINE) % width
        block = pltpu.roll(block, turn, 1) if turn else block
        sums = sums + jnp.where(lag <= p, block, 0.0)
    edge_ref[...] = sums
    lane = iota((received, LAGS), 1)
    norm = 1.0 / math.sqrt(segs * PH * LANES)

    def multiply(a):
        block = shifted_hbm.at[pl.ds(pl.multiple_of(a * LAGS, LAGS), LAGS), :]
        pltpu.make_async_copy(block, shifted_ref.at[a], sems.at[a]).wait()
        return dot_t(phase_ref[...], shifted_ref[a])

    def combine(a, product_ref):
        first = pltpu.roll(edge_ref[...], (stations - a) * FINE, 1)
        sums = jnp.where(lane < FINE, first[:, :LAGS], 0.0)
        for p in range(FINE):
            block = pltpu.roll(product_ref[p * received : (p + 1) * received], p + 1, 1)
            sums = sums + jnp.where(lane > p, block, 0.0)
        sums = sums * norm
        for c in range(LAGS // LANES):
            total_ref[c, pl.ds(a, received, stride=stations), :] = sums[
                :, c * LANES : (c + 1) * LANES
            ]

    even_ref[...] = multiply(0)

    def body(i, _):
        odd_ref[...] = multiply(2 * i + 1)
        combine(2 * i, even_ref)
        even_ref[...] = multiply(2 * i + 2)
        combine(2 * i + 1, odd_ref)
        return 0

    lax.fori_loop(0, stations // 2 - 1, body, 0)
    odd_ref[...] = multiply(stations - 1)
    combine(stations - 2, even_ref)
    combine(stations - 1, odd_ref)
    for c in range(LAGS // LANES):
        out_ref[:, c * LANES : (c + 1) * LANES] = total_ref[c].astype(BF16)


def correlate(me, near, far, shifted, extra, segs):
    rows = segs * far.shape[1] // (PH // GROUP)
    count = rows // segs
    stations = shifted.shape[0] // LAGS
    total = shifted.shape[1]
    return pl.pallas_call(
        lambda *refs: correlate_kernel(segs, *refs),
        out_shape=jax.ShapeDtypeStruct((count * stations, LAGS), BF16),
        in_specs=[
            pl.BlockSpec(memory_space=pltpu.SMEM),
            *[pl.BlockSpec(memory_space=pltpu.VMEM)] * (len(near) + 1),
            pl.BlockSpec(memory_space=pltpu.HBM),
            pl.BlockSpec(memory_space=pltpu.HBM),
        ],
        out_specs=pl.BlockSpec(memory_space=pltpu.VMEM),
        scratch_shapes=[
            *whiten_scratch(rows),
            pltpu.VMEM((count * FINE, total), BF16),
            pltpu.VMEM((count, stations * FINE), F32),
            pltpu.VMEM((LAGS // LANES, count * stations, LANES), F32),
            pltpu.VMEM((stations, LAGS, total), BF16),
            pltpu.VMEM((stations * FINE, total), BF16),
            pltpu.VMEM((count * FINE, LAGS), F32),
            pltpu.VMEM((count * FINE, LAGS), F32),
            pltpu.SemaphoreType.DMA((stations + 1,)),
        ],
        compiler_params=pltpu.CompilerParams(vmem_limit_bytes=48 * MIB),
        cost_estimate=pl.CostEstimate(
            flops=6000 * MIB, bytes_accessed=20 * MIB, transcendentals=0
        ),
        name="correlate",
    )(
        me,
        *near,
        far,
        in_hbm(shifted),
        in_hbm(extra),
    )


def on_device(records, owners):
    stations, length = records.shape
    segs, sources = lax.axis_size("seg"), lax.axis_size("sta")
    chips = segs // CORES
    me = lax.axis_index("seg")
    chip = lax.div(me, jnp.int32(CORES))
    along_x = [[(i, (i + k * CORES) % segs) for i in range(segs)] for k in range(chips)]
    across = [(i, i ^ 1) for i in range(segs)]
    phased, slots = prepare(records, owners.T, sources)
    slots = slots.reshape(sources, -1, GROUP * LANES)
    passing = lax.all_to_all(slots, "sta", 0, 0, tiled=True)
    passing = passing.reshape(segs, -1, GROUP * LANES)
    other = lax.ppermute(phased, "seg", across)
    pair = jnp.concatenate([phased, other], axis=0)
    pairs = [pair] + [lax.ppermute(pair, "seg", along_x[k]) for k in range(1, chips)]
    whitened, phases = own_part(me.reshape(1), pairs, segs)
    passing, phases = lax.optimization_barrier((passing, phases))
    shifted, extra = shift(phases)
    near = [passing]
    for k in range(1, chips):
        at = ((chip + k) & (chips - 1)) * CORES
        block = lax.dynamic_slice_in_dim(passing, at, CORES, 0)
        near.append(lax.ppermute(block, "seg", along_x[k]))
    other_core = 1 - (me & (CORES - 1))
    give = [lax.dynamic_slice_in_dim(passing, chip * CORES + other_core, 1, 0)]
    give += [lax.dynamic_slice_in_dim(block, other_core, 1, 0) for block in near[1:]]
    give, shifted, extra = lax.optimization_barrier((jnp.concatenate(give, axis=0), shifted, extra))
    far = lax.ppermute(give, "seg", across)
    result = correlate(me.reshape(1), near, far, shifted, extra, segs)
    return whitened, result.reshape(-1, stations, LAGS)


def solution(mesh):
    return jax.shard_map(
        on_device,
        mesh=mesh,
        in_specs=(P("sta", "seg"), P("sta", None)),
        out_specs=(P("sta", "seg"), P("seg", "sta", None)),
        check_vma=False,
    )
```

```python
import math

import jax
import jax.numpy as jnp
from jax import lax
from jax.experimental import pallas as pl
from jax.experimental.pallas import tpu as pltpu
from jax.sharding import PartitionSpec as P

LAGS = 512
BS = 2
SLOTS = 2
WATER = 0.5
EPSILON = 1e-06

PH = 16
LANES = 128
FINE = 32
CORES = 2
GROUP = 4
F32 = jnp.float32
BF16 = jnp.bfloat16
MIB = 1 << 20


def dot(a, b):
    return lax.dot_general(a, b, (((1,), (0,)), ((), ())), preferred_element_type=F32)


def dot_t(a, b):
    return lax.dot_general(a, b, (((1,), (1,)), ((), ())), preferred_element_type=F32)


def in_hbm(x):
    return pltpu.with_memory_space_constraint(x, pltpu.HBM)


def iota(shape, axis):
    return lax.broadcasted_iota(jnp.int32, shape, axis)


def cos_sin(phase, period):
    phase = phase & (period - 1)
    phase = jnp.where(phase >= period // 2, phase - period, phase)
    theta = phase.astype(F32) * (2.0 * math.pi / period)
    square = theta * theta
    cosine = jnp.full(theta.shape, 1.0 / math.factorial(20), F32)
    sine = jnp.full(theta.shape, 1.0 / math.factorial(21), F32)
    for n in range(9, -1, -1):
        cosine = (1.0 if n % 2 == 0 else -1.0) / math.factorial(2 * n) + square * cosine
        sine = (1.0 if n % 2 == 0 else -1.0) / math.factorial(2 * n + 1) + square * sine
    return cosine, sine * theta


def spread():
    shape = (LANES, PH * LANES)
    source, target = iota(shape, 0), iota(shape, 1)
    hit = (target // LANES == source % PH) & (target % LANES == source // PH)
    return jnp.where(hit, 1.0, 0.0).astype(BF16)


def gather_back():
    shape = (LANES, PH * LANES)
    target, source = iota(shape, 0), iota(shape, 1)
    lane = source % LANES
    place = FINE // PH * (lane % (LANES // 2)) + lane // (LANES // 2)
    hit = (source // LANES == target % PH) & (place == target // PH)
    return jnp.where(hit, 1.0, 0.0).astype(BF16)


def fold(trace_ref, scale, segs, put):
    rows = trace_ref.shape[1] // segs
    low = iota((rows, LANES), 1) < LANES // 2
    for p in range(PH):
        for s in range(segs // 2):
            first = trace_ref[p, 2 * s * rows : (2 * s + 1) * rows, :] * scale
            second = trace_ref[p, (2 * s + 1) * rows : (2 * s + 2) * rows, :] * scale
            put(p, s, jnp.where(low, first, pltpu.roll(second, LANES // 2, 1)).astype(BF16))
            put(p + PH, s, jnp.where(low, pltpu.roll(first, LANES // 2, 1), second).astype(BF16))


def prepare_kernel(
    owner_count, records_hbm, owners_hbm, phased_hbm, slots_hbm,
    records_ref, owners_ref, phased_ref, slots_ref, sems,
):
    loads = [
        pltpu.make_async_copy(records_hbm, records_ref, sems.at[0]),
        pltpu.make_async_copy(owners_hbm, owners_ref, sems.at[1]),
    ]
    for load in loads:
        load.start()
    stations, length = records_ref.shape
    dests, blocks = owners_ref.shape
    per_tile = LANES // PH
    one_hot = spread()
    for load in loads:
        load.wait()
    tiles = jnp.concatenate(
        [records_ref[:, t * LANES : (t + 1) * LANES] for t in range(length // LANES)], axis=0
    )
    parts = dot(tiles, one_hot)
    phases = []
    for p in range(PH):
        total = None
        for t in range(length // LANES):
            part = parts[t * stations : (t + 1) * stations, p * LANES : (p + 1) * LANES]
            part = pltpu.roll(part, per_tile * t, 1) if t else part
            total = part if total is None else total + part
        phases.append(total.astype(BF16))
    for p in range(PH):
        phased_ref[:, p * LANES : (p + 1) * LANES] = phases[p]
    stores = [pltpu.make_async_copy(phased_ref, phased_hbm, sems.at[2])]
    stores[0].start()
    high = PH // GROUP
    stacked = jnp.concatenate(
        [jnp.concatenate(phases[h * GROUP : (h + 1) * GROUP], axis=1) for h in range(high)], axis=0
    )
    rows, width = owner_count * high * SLOTS * BS, high * stations
    k_of, column = iota((blocks, width), 0), iota((blocks, width), 1)
    expand = jnp.where(column % stations // BS == k_of, 1.0, 0.0)
    named = lax.dot_general(
        owners_ref[...].astype(F32), expand, (((1,), (0,)), ((), ())), preferred_element_type=F32
    )
    row, col = iota((rows, width), 0), iota((rows, width), 1)
    owner = (row // (high * SLOTS * BS)).astype(F32)
    wanted = jnp.zeros((rows, width), F32)
    for d in range(dests):
        wanted = jnp.maximum(wanted, jnp.where(named[d : d + 1, :] == owner, 1.0, 0.0))
    first, second = iota((width, width), 0), iota((width, width), 1)
    earlier = (
        (first // stations == second // stations)
        & (first % stations // BS < second % stations // BS)
        & (first % BS == 0)
    )
    rank = dot(wanted.astype(BF16), jnp.where(earlier, 1.0, 0.0).astype(BF16))
    slot = (row // BS % SLOTS).astype(F32)
    right = (
        (rank == slot)
        & (row % BS == col % BS)
        & (row // (SLOTS * BS) % high == col // stations)
    )
    select = jnp.where(right, wanted, 0.0).astype(BF16)
    parts, size = 4, rows // 4
    for i in range(parts):
        at = pl.ds(i * size, size)
        slots_ref[at, :] = dot(select[i * size : (i + 1) * size], stacked).astype(BF16)
        stores.append(pltpu.make_async_copy(slots_ref.at[at, :], slots_hbm.at[at, :], sems.at[3 + i]))
        stores[-1].start()
    for store in stores:
        store.wait()


def prepare(records, owners, owner_count):
    stations, length = records.shape
    rows = owner_count * SLOTS * BS * PH // GROUP
    return pl.pallas_call(
        lambda *refs: prepare_kernel(owner_count, *refs),
        out_shape=(
            pltpu.HBM((stations, length), BF16),
            pltpu.HBM((rows, GROUP * LANES), BF16),
        ),
        in_specs=[pl.BlockSpec(memory_space=pltpu.HBM)] * 2,
        out_specs=[pl.BlockSpec(memory_space=pltpu.HBM)] * 2,
        scratch_shapes=[
            pltpu.VMEM(records.shape, records.dtype),
            pltpu.VMEM(owners.shape, owners.dtype),
            pltpu.VMEM((stations, length), BF16),
            pltpu.VMEM((rows, GROUP * LANES), BF16),
            pltpu.SemaphoreType.DMA((7,)),
        ],
        compiler_params=pltpu.CompilerParams(vmem_limit_bytes=16 * MIB),
        cost_estimate=pl.CostEstimate(
            flops=100 * MIB, bytes_accessed=2 * MIB, transcendentals=0
        ),
        name="prepare",
    )(in_hbm(records), in_hbm(owners))


def add(a, b):
    return a[0] + b[0], a[1] + b[1]


def sub(a, b):
    return a[0] - b[0], a[1] - b[1]


def times_i(a, sign):
    return (-a[1], a[0]) if sign > 0 else (a[1], -a[0])


def times(a, b):
    return a[0] * b[0] - a[1] * b[1], a[0] * b[1] + a[1] * b[0]


def unit(a, k, sign):
    k %= 16
    if k == 0:
        return a
    if k == 4:
        return times_i(a, sign)
    if k == 8:
        return -a[0], -a[1]
    if k == 12:
        return times_i(a, -sign)
    angle = 2.0 * math.pi * k / 16
    return times(a, (math.cos(angle), sign * math.sin(angle)))


def four(a, sign):
    s, d = add(a[0], a[2]), sub(a[0], a[2])
    t, e = add(a[1], a[3]), times_i(sub(a[1], a[3]), sign)
    return [add(s, t), add(d, e), sub(s, t), sub(d, e)]


def forward_sixteen(v):
    inner = [four([v[4 * p1 + p0] for p1 in range(4)], 1) for p0 in range(4)]
    out = [None] * 8
    for fa in range(4):
        u = [unit(inner[p0][fa], p0 * fa, 1) for p0 in range(4)]
        s, t = add(u[0], u[2]), add(u[1], u[3])
        out[fa] = add(s, t)
        out[fa + 4] = add(sub(u[0], u[2]), times_i(sub(u[1], u[3]), 1))
        if fa == 0:
            last = s[0] - t[0]
    return out, last


def inverse_sixteen(f):
    out = [None] * 16
    for p0 in range(4):
        inner = []
        for fa in range(4):
            turned = unit(f[fa + 4], 4 * p0, -1)
            inner.append(unit(add(f[fa], turned), p0 * fa, -1))
        for p1, value in enumerate(four(inner, -1)):
            out[4 * p1 + p0] = value
    return out


def seg_total(values, segs):
    rows = values.shape[0] // segs
    total = values[:rows]
    for s in range(1, segs):
        total = total + values[s * rows : (s + 1) * rows]
    return total


def whiten(x_ref, y_ref, f_ref, sum_ref, trace_ref, segs):
    rows = x_ref.shape[1]
    length = PH * LANES
    window = length * segs
    half = PH // 2
    n, k = iota((LANES, LANES), 0), iota((LANES, LANES), 1)
    cosine, sine = cos_sin(n * k, LANES)
    table = jnp.concatenate([cosine, sine], axis=1).astype(BF16)
    folded = FINE // PH * (k % (LANES // 2)) + k // (LANES // 2)
    back = jnp.concatenate(cos_sin(n * folded, LANES), axis=0).astype(BF16)
    turn_cos, turn_sin = cos_sin(iota((PH, LANES), 0) * iota((PH, LANES), 1), length)
    for p in range(PH):
        y_ref[p] = dot(x_ref[p], table)
    lane = iota((8, LANES), 1)

    def forward(i, _):
        at = pl.ds(pl.multiple_of(i * 8, 8), 8)
        v = []
        for p in range(PH):
            y = y_ref[p, at, :LANES], y_ref[p, at, LANES:]
            v.append(times(y, (turn_cos[p : p + 1], turn_sin[p : p + 1])) if p else y)
        out, last = forward_sixteen(v)
        total = None
        for j, (re, im) in enumerate(out):
            if j == 0:
                mag = jnp.where(lane == 0, jnp.abs(re), jnp.sqrt(re * re + im * im))
                im = jnp.where(lane == 0, last, im)
                total = jnp.where(lane == 0, 0.5 * (jnp.abs(re) + jnp.abs(im)), mag)
            else:
                mag = jnp.sqrt(re * re + im * im)
                total = total + mag
            f_ref[j, at, :] = re
            f_ref[half + j, at, :] = im
            f_ref[2 * half + j, at, :] = mag
        sum_ref[at, :] = total
        return 0

    lax.fori_loop(0, rows // 8, forward, 0, unroll=4)
    amp = 2.0 * jnp.sum(seg_total(sum_ref[...], segs), axis=1, keepdims=True)
    level = WATER * amp / window + EPSILON
    sum_ref[...] = jnp.concatenate(
        [jnp.broadcast_to(level, (rows // segs, LANES))] * segs, axis=0
    )

    def inverse(i, _):
        at = pl.ds(pl.multiple_of(i * 8, 8), 8)
        level = sum_ref[at, :]
        f = []
        for j in range(half):
            re, im, mag = f_ref[j, at, :], f_ref[half + j, at, :], f_ref[2 * half + j, at, :]
            if j == 0:
                edge = im / (jnp.abs(im) + level)
                share = 2.0 / (mag + level)
                f.append(
                    (
                        jnp.where(lane == 0, 0.5, 1.0) * (re * share),
                        jnp.where(lane == 0, 0.0, im * share),
                    )
                )
                edge = jnp.where(lane == 0, edge, 0.0)
            else:
                share = 2.0 / (mag + level)
                f.append((re * share, im * share))
        for p, z in enumerate(inverse_sixteen(f)):
            if p:
                z = times(z, (turn_cos[p : p + 1], -turn_sin[p : p + 1]))
            y_ref[p, at, :LANES] = z[0] - edge if p % 2 else z[0] + edge
            y_ref[p, at, LANES:] = z[1]
        return 0

    lax.fori_loop(0, rows // 8, inverse, 0, unroll=4)
    energy = jnp.zeros((rows, LANES), F32)
    for p in range(PH):
        trace = dot(y_ref[p].astype(BF16), back) * (1.0 / length)
        energy = energy + trace * trace
        trace_ref[p] = trace
    energy = jnp.sum(seg_total(energy, segs), axis=1, keepdims=True)
    return lax.rsqrt(energy / window + EPSILON)


def whiten_scratch(rows):
    return [
        pltpu.VMEM((PH, rows, LANES), BF16),
        pltpu.VMEM((PH, rows, 2 * LANES), F32),
        pltpu.VMEM((3 * PH // 2, rows, LANES), F32),
        pltpu.VMEM((rows, LANES), F32),
        pltpu.VMEM((PH, rows, LANES), F32),
    ]


def own_kernel(segs, me_ref, *refs):
    pairs, refs = refs[: segs // CORES], refs[segs // CORES :]
    white_ref, phase_ref, x_ref, y_ref, f_ref, sum_ref, trace_ref = refs
    rows, length = x_ref.shape[1], PH * LANES
    stations = rows // segs
    per_tile = LANES // PH
    me, chips = me_ref[0], segs // CORES
    for i, ref in enumerate(pairs):
        chip = (lax.div(me, CORES) + chips - i) & (chips - 1)
        for j in range(CORES):
            core = (me + j) & (CORES - 1)
            at = pl.ds(pl.multiple_of((chip * CORES + core) * stations, stations), stations)
            for p in range(PH):
                x_ref[p, at, :] = ref[
                    j * stations : (j + 1) * stations, p * LANES : (p + 1) * LANES
                ]
    scale = whiten(x_ref, y_ref, f_ref, sum_ref, trace_ref, segs)
    def put(p, s, tile):
        phase_ref[s, (FINE - 1 - p) * stations : (FINE - p) * stations, :] = tile.astype(F32)

    fold(trace_ref, scale, segs, put)
    mine = pl.ds(pl.multiple_of(me * stations, stations), stations)
    for p in range(PH):
        white_ref[:, p * LANES : (p + 1) * LANES] = (trace_ref[p, mine, :] * scale).astype(BF16)


def order_kernel(phased_ref, white_ref):
    stations, length = phased_ref.shape
    per_tile = LANES // PH
    tiles = [phased_ref[:, p * LANES : (p + 1) * LANES].astype(F32) for p in range(PH)]
    moved = []
    for t in range(length // LANES):
        turn = (LANES - per_tile // 2 * t) % LANES
        moved.append(
            jnp.concatenate(
                [(pltpu.roll(x, turn, 1) if turn else x).astype(BF16) for x in tiles], axis=1
            )
        )
    natural = dot_t(jnp.concatenate(moved, axis=0), gather_back()).astype(BF16)
    for t in range(length // LANES):
        white_ref[:, t * LANES : (t + 1) * LANES] = natural[t * stations : (t + 1) * stations]


def in_sample_order(phased):
    return pl.pallas_call(
        order_kernel,
        out_shape=jax.ShapeDtypeStruct(phased.shape, BF16),
        in_specs=[pl.BlockSpec(memory_space=pltpu.VMEM)],
        out_specs=pl.BlockSpec(memory_space=pltpu.VMEM),
        compiler_params=pltpu.CompilerParams(vmem_limit_bytes=8 * MIB),
        cost_estimate=pl.CostEstimate(flops=1000 * MIB, bytes_accessed=MIB, transcendentals=0),
        name="order",
    )(phased)


def pack_kernel(me_ref, *refs):
    near, out_ref = refs[:-1], refs[-1]
    other = 1 - (me_ref[0] & (CORES - 1))
    chip = lax.div(me_ref[0], CORES)
    for i, ref in enumerate(near):
        out_ref[i] = ref[(chip * CORES if i == 0 else 0) + other]


def pack(me, near):
    return pl.pallas_call(
        pack_kernel,
        out_shape=jax.ShapeDtypeStruct((len(near), *near[0].shape[1:]), BF16),
        in_specs=[
            pl.BlockSpec(memory_space=pltpu.SMEM),
            *[pl.BlockSpec(memory_space=pltpu.VMEM)] * len(near),
        ],
        out_specs=pl.BlockSpec(memory_space=pltpu.VMEM),
        compiler_params=pltpu.CompilerParams(vmem_limit_bytes=8 * MIB),
        cost_estimate=pl.CostEstimate(flops=0, bytes_accessed=MIB, transcendentals=0),
        name="pack",
    )(me, *near)


def own_part(me, pairs, segs):
    rows, length = len(pairs) * pairs[0].shape[0], pairs[0].shape[1]
    stations = rows // segs
    return pl.pallas_call(
        lambda *refs: own_kernel(segs, *refs),
        out_shape=(
            jax.ShapeDtypeStruct((stations, length), BF16),
            jax.ShapeDtypeStruct((segs // 2, FINE * stations, LANES), F32),
        ),
        in_specs=[
            pl.BlockSpec(memory_space=pltpu.SMEM),
            *[pl.BlockSpec(memory_space=pltpu.VMEM)] * len(pairs),
        ],
        out_specs=[pl.BlockSpec(memory_space=pltpu.VMEM)] * 2,
        scratch_shapes=whiten_scratch(rows),
        compiler_params=pltpu.CompilerParams(vmem_limit_bytes=32 * MIB),
        cost_estimate=pl.CostEstimate(
            flops=2000 * MIB, bytes_accessed=4 * MIB, transcendentals=0
        ),
        name="own",
    )(me, *pairs)


def shift_kernel(stations, phase_ref, shifted_hbm, extra_hbm, shifted_ref, extra_ref, sems):
    count = LAGS // FINE
    tiles = phase_ref.shape[0]
    lane = iota((FINE, LANES), 1)

    def copies(a):
        to = shifted_hbm.at[pl.ds(pl.multiple_of(a * LAGS, LAGS), LAGS), :]
        to_extra = extra_hbm.at[pl.ds(pl.multiple_of(a * FINE, FINE), FINE), :]
        return (
            pltpu.make_async_copy(shifted_ref.at[a], to, sems.at[0, a]),
            pltpu.make_async_copy(extra_ref.at[a], to_extra, sems.at[1, a]),
        )

    def body(a, _):
        block = [phase_ref[s, pl.ds(a, FINE, stride=stations), :] for s in range(tiles)]
        zero = jnp.zeros((FINE, LANES), F32)
        for i in range(-1, count):
            m = i + 1 - count // 2
            turned = [pltpu.roll(tile, m % LANES, 1) if m else tile for tile in block]
            for t in range(tiles):
                if m > 0:
                    moved = jnp.where(lane >= m, turned[t], turned[t - 1] if t else zero)
                elif m < 0:
                    later = turned[t + 1] if t + 1 < tiles else zero
                    moved = jnp.where(lane < LANES + m, turned[t], later)
                else:
                    moved = turned[t]
                cols = slice(t * LANES, (t + 1) * LANES)
                if i < 0:
                    extra_ref[a, :, cols] = moved.astype(BF16)
                else:
                    shifted_ref[a, i * FINE : (i + 1) * FINE, cols] = moved.astype(BF16)
        for copy in copies(a):
            copy.start()
        return 0

    lax.fori_loop(0, stations, body, 0, unroll=4)

    def finish(a, _):
        for copy in copies(a):
            copy.wait()
        return 0

    lax.fori_loop(0, stations, finish, 0)


def shift(phases):
    stations = phases.shape[1] // FINE
    total = phases.shape[0] * LANES
    return pl.pallas_call(
        lambda *refs: shift_kernel(stations, *refs),
        out_shape=(
            pltpu.HBM((stations * LAGS, total), BF16),
            pltpu.HBM((stations * FINE, total), BF16),
        ),
        in_specs=[pl.BlockSpec(memory_space=pltpu.VMEM)],
        out_specs=[pl.BlockSpec(memory_space=pltpu.HBM)] * 2,
        scratch_shapes=[
            pltpu.VMEM((stations, LAGS, total), BF16),
            pltpu.VMEM((stations, FINE, total), BF16),
            pltpu.SemaphoreType.DMA((2, stations)),
        ],
        compiler_params=pltpu.CompilerParams(vmem_limit_bytes=16 * MIB),
        cost_estimate=pl.CostEstimate(
            flops=1, bytes_accessed=9 * MIB, transcendentals=0
        ),
        name="shift",
    )(phases)


def correlate_kernel(segs, me_ref, *refs):
    chips = segs // CORES
    near, (far_ref, shifted_hbm, extra_hbm, out_ref), refs = (
        refs[:chips],
        refs[chips : chips + 4],
        refs[chips + 4 :],
    )
    x_ref, y_ref, f_ref, sum_ref, trace_ref, phase_ref, edge_ref, total_ref = refs[:8]
    shifted_ref, extra_ref, even_ref, odd_ref, sems = refs[8:]
    rows = x_ref.shape[1]
    received = rows // segs
    stations = shifted_ref.shape[0]
    copies = [pltpu.make_async_copy(extra_hbm, extra_ref, sems.at[stations])]
    for a in range(stations):
        block = shifted_hbm.at[pl.ds(a * LAGS, LAGS), :]
        copies.append(pltpu.make_async_copy(block, shifted_ref.at[a], sems.at[a]))
    for copy in copies:
        copy.start()
    high, unit_rows = PH // GROUP, SLOTS * BS
    per_seg = high * received
    to, at_row = iota((per_seg, per_seg), 0), iota((per_seg, per_seg), 1)
    wanted = (
        to % received // unit_rows * (high * unit_rows) + to // received * unit_rows
    ) + to % unit_rows
    order = jnp.where(at_row == wanted, 1.0, 0.0).astype(BF16)
    me = me_ref[0]
    mine = me & (CORES - 1)
    for s in range(segs):
        i = s // CORES
        chip = (lax.div(me, CORES) + chips - i) & (chips - 1)
        if s % CORES:
            source, seg = far_ref[i], chip * CORES + 1 - mine
        else:
            source = near[i][(chip * CORES if i == 0 else 0) + mine]
            seg = chip * CORES + mine
        block = dot(order, source).astype(BF16)
        at = pl.ds(pl.multiple_of(seg * received, received), received)
        for p in range(PH):
            x_ref[p, at, :] = block[
                p // GROUP * received : (p // GROUP + 1) * received,
                p % GROUP * LANES : (p % GROUP + 1) * LANES,
            ]
    scale = whiten(x_ref, y_ref, f_ref, sum_ref, trace_ref, segs)

    def put(p, s, tile):
        phase_ref[p * received : (p + 1) * received, s * LANES : (s + 1) * LANES] = tile

    fold(trace_ref, scale, segs, put)
    copies[0].wait()
    edge = dot_t(phase_ref[...], extra_ref[...])
    width = stations * FINE
    lag = iota((received, width), 1) % FINE
    sums = jnp.zeros((received, width), F32)
    for p in range(FINE):
        block = edge[p * received : (p + 1) * received]
        turn = (p + 1 - FINE) % width
        block = pltpu.roll(block, turn, 1) if turn else block
        sums = sums + jnp.where(lag <= p, block, 0.0)
    edge_ref[...] = sums
    lane = iota((received, LAGS), 1)
    norm = 1.0 / math.sqrt(segs * PH * LANES)

    def multiply(a):
        block = shifted_hbm.at[pl.ds(pl.multiple_of(a * LAGS, LAGS), LAGS), :]
        pltpu.make_async_copy(block, shifted_ref.at[a], sems.at[a]).wait()
        return dot_t(phase_ref[...], shifted_ref[a])

    def combine(a, product_ref):
        first = pltpu.roll(edge_ref[...], (stations - a) * FINE, 1)
        sums = jnp.where(lane < FINE, first[:, :LAGS], 0.0)
        for p in range(FINE):
            block = pltpu.roll(product_ref[p * received : (p + 1) * received], p + 1, 1)
            sums = sums + jnp.where(lane > p, block, 0.0)
        sums = sums * norm
        for c in range(LAGS // LANES):
            total_ref[c, pl.ds(a, received, stride=stations), :] = sums[
                :, c * LANES : (c + 1) * LANES
            ]

    even_ref[...] = multiply(0)

    def body(i, _):
        odd_ref[...] = multiply(2 * i + 1)
        combine(2 * i, even_ref)
        even_ref[...] = multiply(2 * i + 2)
        combine(2 * i + 1, odd_ref)
        return 0

    lax.fori_loop(0, stations // 2 - 1, body, 0)
    odd_ref[...] = multiply(stations - 1)
    combine(stations - 2, even_ref)
    combine(stations - 1, odd_ref)
    for c in range(LAGS // LANES):
        out_ref[:, c * LANES : (c + 1) * LANES] = total_ref[c].astype(BF16)


def correlate(me, near, far, shifted, extra, segs):
    rows = segs * far.shape[1] // (PH // GROUP)
    count = rows // segs
    stations = shifted.shape[0] // LAGS
    total = shifted.shape[1]
    return pl.pallas_call(
        lambda *refs: correlate_kernel(segs, *refs),
        out_shape=jax.ShapeDtypeStruct((count * stations, LAGS), BF16),
        in_specs=[
            pl.BlockSpec(memory_space=pltpu.SMEM),
            *[pl.BlockSpec(memory_space=pltpu.VMEM)] * (len(near) + 1),
            pl.BlockSpec(memory_space=pltpu.HBM),
            pl.BlockSpec(memory_space=pltpu.HBM),
        ],
        out_specs=pl.BlockSpec(memory_space=pltpu.VMEM),
        scratch_shapes=[
            *whiten_scratch(rows),
            pltpu.VMEM((count * FINE, total), BF16),
            pltpu.VMEM((count, stations * FINE), F32),
            pltpu.VMEM((LAGS // LANES, count * stations, LANES), F32),
            pltpu.VMEM((stations, LAGS, total), BF16),
            pltpu.VMEM((stations * FINE, total), BF16),
            pltpu.VMEM((count * FINE, LAGS), F32),
            pltpu.VMEM((count * FINE, LAGS), F32),
            pltpu.SemaphoreType.DMA((stations + 1,)),
        ],
        compiler_params=pltpu.CompilerParams(vmem_limit_bytes=48 * MIB),
        cost_estimate=pl.CostEstimate(
            flops=6000 * MIB, bytes_accessed=20 * MIB, transcendentals=0
        ),
        name="correlate",
    )(
        me,
        *near,
        far,
        in_hbm(shifted),
        in_hbm(extra),
    )


def on_device(records, owners):
    stations, length = records.shape
    segs, sources = lax.axis_size("seg"), lax.axis_size("sta")
    chips = segs // CORES
    me = lax.axis_index("seg")
    chip = lax.div(me, jnp.int32(CORES))
    along_x = [[(i, (i + k * CORES) % segs) for i in range(segs)] for k in range(chips)]
    across = [(i, i ^ 1) for i in range(segs)]
    phased, slots = prepare(records, owners.T, sources)
    slots = slots.reshape(sources, -1, GROUP * LANES)
    passing = lax.all_to_all(slots, "sta", 0, 0, tiled=True)
    passing = passing.reshape(segs, -1, GROUP * LANES)
    other = lax.ppermute(phased, "seg", across)
    pair = jnp.concatenate([phased, other], axis=0)
    pairs = [pair] + [lax.ppermute(pair, "seg", along_x[k]) for k in range(1, chips)]
    mine, phases = own_part(me.reshape(1), pairs, segs)
    passing, phases = lax.optimization_barrier((passing, phases))
    shifted, extra = shift(phases)
    near = [passing]
    for k in range(1, chips):
        at = ((chip + k) & (chips - 1)) * CORES
        block = lax.dynamic_slice_in_dim(passing, at, CORES, 0)
        near.append(lax.ppermute(block, "seg", along_x[k]))
    near, shifted, extra, mine = lax.optimization_barrier((near, shifted, extra, mine))
    far = lax.ppermute(pack(me.reshape(1), near), "seg", across)
    whitened = in_sample_order(mine)
    result = correlate(me.reshape(1), near, far, shifted, extra, segs)
    return whitened, result.reshape(-1, stations, LAGS)


def solution(mesh):
    return jax.shard_map(
        on_device,
        mesh=mesh,
        in_specs=(P("sta", "seg"), P("sta", None)),
        out_specs=(P("sta", "seg"), P("seg", "sta", None)),
        check_vma=False,
    )
```

```python
import math

import jax
import jax.numpy as jnp
from jax import lax
from jax.experimental import pallas as pl
from jax.experimental.pallas import tpu as pltpu
from jax.sharding import PartitionSpec as P

LAGS = 512
BS = 2
SLOTS = 2
WATER = 0.5
EPSILON = 1e-06

PH = 16
LANES = 128
STEPS = (0, 2, 1, 3)
FINE = 32
CORES = 2
GROUP = 4
F32 = jnp.float32
BF16 = jnp.bfloat16
MIB = 1 << 20


def dot(a, b):
    return lax.dot_general(a, b, (((1,), (0,)), ((), ())), preferred_element_type=F32)


def dot_t(a, b):
    return lax.dot_general(a, b, (((1,), (1,)), ((), ())), preferred_element_type=F32)


def in_hbm(x):
    return pltpu.with_memory_space_constraint(x, pltpu.HBM)


def iota(shape, axis):
    return lax.broadcasted_iota(jnp.int32, shape, axis)


def cos_sin(phase, period):
    phase = phase & (period - 1)
    phase = jnp.where(phase >= period // 2, phase - period, phase)
    theta = phase.astype(F32) * (2.0 * math.pi / period)
    square = theta * theta
    cosine = jnp.full(theta.shape, 1.0 / math.factorial(20), F32)
    sine = jnp.full(theta.shape, 1.0 / math.factorial(21), F32)
    for n in range(9, -1, -1):
        cosine = (1.0 if n % 2 == 0 else -1.0) / math.factorial(2 * n) + square * cosine
        sine = (1.0 if n % 2 == 0 else -1.0) / math.factorial(2 * n + 1) + square * sine
    return cosine, sine * theta


def spread():
    shape = (LANES, PH * LANES)
    source, target = iota(shape, 0), iota(shape, 1)
    hit = (target // LANES == source % PH) & (target % LANES == source // PH)
    return jnp.where(hit, 1.0, 0.0).astype(BF16)


def gather_back():
    shape = (LANES, PH * LANES)
    target, source = iota(shape, 0), iota(shape, 1)
    lane = source % LANES
    place = FINE // PH * (lane % (LANES // 2)) + lane // (LANES // 2)
    hit = (source // LANES == target % PH) & (place == target // PH)
    return jnp.where(hit, 1.0, 0.0).astype(BF16)


def fold(trace_ref, scale, segs, put):
    rows = trace_ref.shape[1] // segs
    low = iota((rows, LANES), 1) < LANES // 2
    for p in range(PH):
        for s in range(segs // 2):
            first = trace_ref[p, 2 * s * rows : (2 * s + 1) * rows, :] * scale
            second = trace_ref[p, (2 * s + 1) * rows : (2 * s + 2) * rows, :] * scale
            put(p, s, jnp.where(low, first, pltpu.roll(second, LANES // 2, 1)).astype(BF16))
            put(p + PH, s, jnp.where(low, pltpu.roll(first, LANES // 2, 1), second).astype(BF16))


def prepare_kernel(
    owner_count, records_hbm, owners_hbm, phased_hbm, slots_hbm,
    records_ref, owners_ref, phased_ref, slots_ref, sems,
):
    loads = [
        pltpu.make_async_copy(records_hbm, records_ref, sems.at[0]),
        pltpu.make_async_copy(owners_hbm, owners_ref, sems.at[1]),
    ]
    for load in loads:
        load.start()
    stations, length = records_ref.shape
    dests, blocks = owners_ref.shape
    per_tile = LANES // PH
    one_hot = spread()
    for load in loads:
        load.wait()
    tiles = jnp.concatenate(
        [records_ref[:, t * LANES : (t + 1) * LANES] for t in range(length // LANES)], axis=0
    )
    parts = dot(tiles, one_hot)
    phases = []
    for p in range(PH):
        total = None
        for t in range(length // LANES):
            part = parts[t * stations : (t + 1) * stations, p * LANES : (p + 1) * LANES]
            part = pltpu.roll(part, per_tile * t, 1) if t else part
            total = part if total is None else total + part
        phases.append(total.astype(BF16))
    for p in range(PH):
        phased_ref[:, p * LANES : (p + 1) * LANES] = phases[p]
    stores = [pltpu.make_async_copy(phased_ref, phased_hbm, sems.at[2])]
    stores[0].start()
    high = PH // GROUP
    stacked = jnp.concatenate(
        [jnp.concatenate(phases[h * GROUP : (h + 1) * GROUP], axis=1) for h in range(high)], axis=0
    )
    rows, width = owner_count * high * SLOTS * BS, high * stations
    k_of, column = iota((blocks, width), 0), iota((blocks, width), 1)
    expand = jnp.where(column % stations // BS == k_of, 1.0, 0.0)
    named = lax.dot_general(
        owners_ref[...].astype(F32), expand, (((1,), (0,)), ((), ())), preferred_element_type=F32
    )
    row, col = iota((rows, width), 0), iota((rows, width), 1)
    owner = (row // (high * SLOTS * BS)).astype(F32)
    wanted = jnp.zeros((rows, width), F32)
    for d in range(dests):
        wanted = jnp.maximum(wanted, jnp.where(named[d : d + 1, :] == owner, 1.0, 0.0))
    first, second = iota((width, width), 0), iota((width, width), 1)
    earlier = (
        (first // stations == second // stations)
        & (first % stations // BS < second % stations // BS)
        & (first % BS == 0)
    )
    rank = dot(wanted.astype(BF16), jnp.where(earlier, 1.0, 0.0).astype(BF16))
    slot = (row // BS % SLOTS).astype(F32)
    right = (
        (rank == slot)
        & (row % BS == col % BS)
        & (row // (SLOTS * BS) % high == col // stations)
    )
    select = jnp.where(right, wanted, 0.0).astype(BF16)
    parts, size = 4, rows // 4
    for i in range(parts):
        at = pl.ds(i * size, size)
        slots_ref[at, :] = dot(select[i * size : (i + 1) * size], stacked).astype(BF16)
        stores.append(pltpu.make_async_copy(slots_ref.at[at, :], slots_hbm.at[at, :], sems.at[3 + i]))
        stores[-1].start()
    for store in stores:
        store.wait()


def prepare(records, owners, owner_count):
    stations, length = records.shape
    rows = owner_count * SLOTS * BS * PH // GROUP
    return pl.pallas_call(
        lambda *refs: prepare_kernel(owner_count, *refs),
        out_shape=(
            pltpu.HBM((stations, length), BF16),
            pltpu.HBM((rows, GROUP * LANES), BF16),
        ),
        in_specs=[pl.BlockSpec(memory_space=pltpu.HBM)] * 2,
        out_specs=[pl.BlockSpec(memory_space=pltpu.HBM)] * 2,
        scratch_shapes=[
            pltpu.VMEM(records.shape, records.dtype),
            pltpu.VMEM(owners.shape, owners.dtype),
            pltpu.VMEM((stations, length), BF16),
            pltpu.VMEM((rows, GROUP * LANES), BF16),
            pltpu.SemaphoreType.DMA((7,)),
        ],
        compiler_params=pltpu.CompilerParams(vmem_limit_bytes=16 * MIB),
        cost_estimate=pl.CostEstimate(
            flops=100 * MIB, bytes_accessed=2 * MIB, transcendentals=0
        ),
        name="prepare",
    )(in_hbm(records), in_hbm(owners))


def add(a, b):
    return a[0] + b[0], a[1] + b[1]


def sub(a, b):
    return a[0] - b[0], a[1] - b[1]


def times_i(a, sign):
    return (-a[1], a[0]) if sign > 0 else (a[1], -a[0])


def times(a, b):
    return a[0] * b[0] - a[1] * b[1], a[0] * b[1] + a[1] * b[0]


def unit(a, k, sign):
    k %= 16
    if k == 0:
        return a
    if k == 4:
        return times_i(a, sign)
    if k == 8:
        return -a[0], -a[1]
    if k == 12:
        return times_i(a, -sign)
    angle = 2.0 * math.pi * k / 16
    return times(a, (math.cos(angle), sign * math.sin(angle)))


def four(a, sign):
    s, d = add(a[0], a[2]), sub(a[0], a[2])
    t, e = add(a[1], a[3]), times_i(sub(a[1], a[3]), sign)
    return [add(s, t), add(d, e), sub(s, t), sub(d, e)]


def forward_sixteen(v):
    inner = [four([v[4 * p1 + p0] for p1 in range(4)], 1) for p0 in range(4)]
    out = [None] * 8
    for fa in range(4):
        u = [unit(inner[p0][fa], p0 * fa, 1) for p0 in range(4)]
        s, t = add(u[0], u[2]), add(u[1], u[3])
        out[fa] = add(s, t)
        out[fa + 4] = add(sub(u[0], u[2]), times_i(sub(u[1], u[3]), 1))
        if fa == 0:
            last = s[0] - t[0]
    return out, last


def inverse_sixteen(f):
    out = [None] * 16
    for p0 in range(4):
        inner = []
        for fa in range(4):
            turned = unit(f[fa + 4], 4 * p0, -1)
            inner.append(unit(add(f[fa], turned), p0 * fa, -1))
        for p1, value in enumerate(four(inner, -1)):
            out[4 * p1 + p0] = value
    return out


def seg_total(values, segs):
    rows = values.shape[0] // segs
    total = values[:rows]
    for s in range(1, segs):
        total = total + values[s * rows : (s + 1) * rows]
    return total


def whiten(x_ref, y_ref, f_ref, sum_ref, trace_ref, segs):
    rows = x_ref.shape[1]
    length = PH * LANES
    window = length * segs
    half = PH // 2
    n, k = iota((LANES, LANES), 0), iota((LANES, LANES), 1)
    cosine, sine = cos_sin(n * k, LANES)
    table = jnp.concatenate([cosine, sine], axis=1).astype(BF16)
    folded = FINE // PH * (k % (LANES // 2)) + k // (LANES // 2)
    back = jnp.concatenate(cos_sin(n * folded, LANES), axis=0).astype(BF16)
    turn_cos, turn_sin = cos_sin(iota((PH, LANES), 0) * iota((PH, LANES), 1), length)
    for p in range(PH):
        y_ref[p] = dot(x_ref[p], table)
    lane = iota((8, LANES), 1)

    def forward(i, _):
        at = pl.ds(pl.multiple_of(i * 8, 8), 8)
        v = []
        for p in range(PH):
            y = y_ref[p, at, :LANES], y_ref[p, at, LANES:]
            v.append(times(y, (turn_cos[p : p + 1], turn_sin[p : p + 1])) if p else y)
        out, last = forward_sixteen(v)
        total = None
        for j, (re, im) in enumerate(out):
            if j == 0:
                mag = jnp.where(lane == 0, jnp.abs(re), jnp.sqrt(re * re + im * im))
                im = jnp.where(lane == 0, last, im)
                total = jnp.where(lane == 0, 0.5 * (jnp.abs(re) + jnp.abs(im)), mag)
            else:
                mag = jnp.sqrt(re * re + im * im)
                total = total + mag
            f_ref[j, at, :] = re
            f_ref[half + j, at, :] = im
            f_ref[2 * half + j, at, :] = mag
        sum_ref[at, :] = total
        return 0

    lax.fori_loop(0, rows // 8, forward, 0, unroll=4)
    amp = 2.0 * jnp.sum(seg_total(sum_ref[...], segs), axis=1, keepdims=True)
    level = WATER * amp / window + EPSILON
    sum_ref[...] = jnp.concatenate(
        [jnp.broadcast_to(level, (rows // segs, LANES))] * segs, axis=0
    )

    def inverse(i, _):
        at = pl.ds(pl.multiple_of(i * 8, 8), 8)
        level = sum_ref[at, :]
        f = []
        for j in range(half):
            re, im, mag = f_ref[j, at, :], f_ref[half + j, at, :], f_ref[2 * half + j, at, :]
            if j == 0:
                edge = im / (jnp.abs(im) + level)
                share = 2.0 / (mag + level)
                f.append(
                    (
                        jnp.where(lane == 0, 0.5, 1.0) * (re * share),
                        jnp.where(lane == 0, 0.0, im * share),
                    )
                )
                edge = jnp.where(lane == 0, edge, 0.0)
            else:
                share = 2.0 / (mag + level)
                f.append((re * share, im * share))
        for p, z in enumerate(inverse_sixteen(f)):
            if p:
                z = times(z, (turn_cos[p : p + 1], -turn_sin[p : p + 1]))
            y_ref[p, at, :LANES] = z[0] - edge if p % 2 else z[0] + edge
            y_ref[p, at, LANES:] = z[1]
        return 0

    lax.fori_loop(0, rows // 8, inverse, 0, unroll=4)
    energy = jnp.zeros((rows, LANES), F32)
    for p in range(PH):
        trace = dot(y_ref[p].astype(BF16), back) * (1.0 / length)
        energy = energy + trace * trace
        trace_ref[p] = trace
    energy = jnp.sum(seg_total(energy, segs), axis=1, keepdims=True)
    return lax.rsqrt(energy / window + EPSILON)


def whiten_scratch(rows):
    return [
        pltpu.VMEM((PH, rows, LANES), BF16),
        pltpu.VMEM((PH, rows, 2 * LANES), F32),
        pltpu.VMEM((3 * PH // 2, rows, LANES), F32),
        pltpu.VMEM((rows, LANES), F32),
        pltpu.VMEM((PH, rows, LANES), F32),
    ]


def own_kernel(segs, me_ref, *refs):
    pairs, refs = refs[: segs // CORES], refs[segs // CORES :]
    white_ref, phase_ref, x_ref, y_ref, f_ref, sum_ref, trace_ref = refs
    rows, length = x_ref.shape[1], PH * LANES
    stations = rows // segs
    per_tile = LANES // PH
    me, chips = me_ref[0], segs // CORES
    for i, ref in enumerate(pairs):
        chip = (lax.div(me, CORES) + chips - STEPS[i]) & (chips - 1)
        for j in range(CORES):
            core = (me + j) & (CORES - 1)
            at = pl.ds(pl.multiple_of((chip * CORES + core) * stations, stations), stations)
            for p in range(PH):
                x_ref[p, at, :] = ref[
                    j * stations : (j + 1) * stations, p * LANES : (p + 1) * LANES
                ]
    scale = whiten(x_ref, y_ref, f_ref, sum_ref, trace_ref, segs)
    def put(p, s, tile):
        phase_ref[s, (FINE - 1 - p) * stations : (FINE - p) * stations, :] = tile.astype(F32)

    fold(trace_ref, scale, segs, put)
    mine = pl.ds(pl.multiple_of(me * stations, stations), stations)
    for p in range(PH):
        white_ref[:, p * LANES : (p + 1) * LANES] = (trace_ref[p, mine, :] * scale).astype(BF16)


def order_kernel(phased_ref, white_ref):
    stations, length = phased_ref.shape
    per_tile = LANES // PH
    tiles = [phased_ref[:, p * LANES : (p + 1) * LANES].astype(F32) for p in range(PH)]
    moved = []
    for t in range(length // LANES):
        turn = (LANES - per_tile // 2 * t) % LANES
        moved.append(
            jnp.concatenate(
                [(pltpu.roll(x, turn, 1) if turn else x).astype(BF16) for x in tiles], axis=1
            )
        )
    natural = dot_t(jnp.concatenate(moved, axis=0), gather_back()).astype(BF16)
    for t in range(length // LANES):
        white_ref[:, t * LANES : (t + 1) * LANES] = natural[t * stations : (t + 1) * stations]


def in_sample_order(phased):
    return pl.pallas_call(
        order_kernel,
        out_shape=jax.ShapeDtypeStruct(phased.shape, BF16),
        in_specs=[pl.BlockSpec(memory_space=pltpu.VMEM)],
        out_specs=pl.BlockSpec(memory_space=pltpu.VMEM),
        compiler_params=pltpu.CompilerParams(vmem_limit_bytes=8 * MIB),
        cost_estimate=pl.CostEstimate(flops=1000 * MIB, bytes_accessed=MIB, transcendentals=0),
        name="order",
    )(phased)


def pack_kernel(me_ref, *refs):
    near, out_ref = refs[:-1], refs[-1]
    other = 1 - (me_ref[0] & (CORES - 1))
    chip = lax.div(me_ref[0], CORES)
    for i, ref in enumerate(near):
        out_ref[i] = ref[(chip * CORES if i == 0 else 0) + other]


def pack(me, near):
    return pl.pallas_call(
        pack_kernel,
        out_shape=jax.ShapeDtypeStruct((len(near), *near[0].shape[1:]), BF16),
        in_specs=[
            pl.BlockSpec(memory_space=pltpu.SMEM),
            *[pl.BlockSpec(memory_space=pltpu.VMEM)] * len(near),
        ],
        out_specs=pl.BlockSpec(memory_space=pltpu.VMEM),
        compiler_params=pltpu.CompilerParams(vmem_limit_bytes=8 * MIB),
        cost_estimate=pl.CostEstimate(flops=0, bytes_accessed=MIB, transcendentals=0),
        name="pack",
    )(me, *near)


def own_part(me, pairs, segs):
    rows, length = len(pairs) * pairs[0].shape[0], pairs[0].shape[1]
    stations = rows // segs
    return pl.pallas_call(
        lambda *refs: own_kernel(segs, *refs),
        out_shape=(
            jax.ShapeDtypeStruct((stations, length), BF16),
            jax.ShapeDtypeStruct((segs // 2, FINE * stations, LANES), F32),
        ),
        in_specs=[
            pl.BlockSpec(memory_space=pltpu.SMEM),
            *[pl.BlockSpec(memory_space=pltpu.VMEM)] * len(pairs),
        ],
        out_specs=[pl.BlockSpec(memory_space=pltpu.VMEM)] * 2,
        scratch_shapes=whiten_scratch(rows),
        compiler_params=pltpu.CompilerParams(vmem_limit_bytes=32 * MIB),
        cost_estimate=pl.CostEstimate(
            flops=2000 * MIB, bytes_accessed=4 * MIB, transcendentals=0
        ),
        name="own",
    )(me, *pairs)


def shift_kernel(stations, phase_ref, shifted_hbm, extra_hbm, shifted_ref, extra_ref, sems):
    count = LAGS // FINE
    tiles = phase_ref.shape[0]
    lane = iota((FINE, LANES), 1)

    def copies(a):
        to = shifted_hbm.at[pl.ds(pl.multiple_of(a * LAGS, LAGS), LAGS), :]
        to_extra = extra_hbm.at[pl.ds(pl.multiple_of(a * FINE, FINE), FINE), :]
        return (
            pltpu.make_async_copy(shifted_ref.at[a], to, sems.at[0, a]),
            pltpu.make_async_copy(extra_ref.at[a], to_extra, sems.at[1, a]),
        )

    def body(a, _):
        block = [phase_ref[s, pl.ds(a, FINE, stride=stations), :] for s in range(tiles)]
        zero = jnp.zeros((FINE, LANES), F32)
        for i in range(-1, count):
            m = i + 1 - count // 2
            turned = [pltpu.roll(tile, m % LANES, 1) if m else tile for tile in block]
            for t in range(tiles):
                if m > 0:
                    moved = jnp.where(lane >= m, turned[t], turned[t - 1] if t else zero)
                elif m < 0:
                    later = turned[t + 1] if t + 1 < tiles else zero
                    moved = jnp.where(lane < LANES + m, turned[t], later)
                else:
                    moved = turned[t]
                cols = slice(t * LANES, (t + 1) * LANES)
                if i < 0:
                    extra_ref[a, :, cols] = moved.astype(BF16)
                else:
                    shifted_ref[a, i * FINE : (i + 1) * FINE, cols] = moved.astype(BF16)
        for copy in copies(a):
            copy.start()
        return 0

    lax.fori_loop(0, stations, body, 0, unroll=4)

    def finish(a, _):
        for copy in copies(a):
            copy.wait()
        return 0

    lax.fori_loop(0, stations, finish, 0)


def shift(phases):
    stations = phases.shape[1] // FINE
    total = phases.shape[0] * LANES
    return pl.pallas_call(
        lambda *refs: shift_kernel(stations, *refs),
        out_shape=(
            pltpu.HBM((stations * LAGS, total), BF16),
            pltpu.HBM((stations * FINE, total), BF16),
        ),
        in_specs=[pl.BlockSpec(memory_space=pltpu.VMEM)],
        out_specs=[pl.BlockSpec(memory_space=pltpu.HBM)] * 2,
        scratch_shapes=[
            pltpu.VMEM((stations, LAGS, total), BF16),
            pltpu.VMEM((stations, FINE, total), BF16),
            pltpu.SemaphoreType.DMA((2, stations)),
        ],
        compiler_params=pltpu.CompilerParams(vmem_limit_bytes=16 * MIB),
        cost_estimate=pl.CostEstimate(
            flops=1, bytes_accessed=9 * MIB, transcendentals=0
        ),
        name="shift",
    )(phases)


def correlate_kernel(segs, me_ref, *refs):
    chips = segs // CORES
    near, (far_ref, shifted_hbm, extra_hbm, out_ref), refs = (
        refs[:chips],
        refs[chips : chips + 4],
        refs[chips + 4 :],
    )
    x_ref, y_ref, f_ref, sum_ref, trace_ref, phase_ref, edge_ref, total_ref = refs[:8]
    shifted_ref, extra_ref, even_ref, odd_ref, sems = refs[8:]
    rows = x_ref.shape[1]
    received = rows // segs
    stations = shifted_ref.shape[0]
    copies = [pltpu.make_async_copy(extra_hbm, extra_ref, sems.at[stations])]
    for a in range(stations):
        block = shifted_hbm.at[pl.ds(a * LAGS, LAGS), :]
        copies.append(pltpu.make_async_copy(block, shifted_ref.at[a], sems.at[a]))
    for copy in copies:
        copy.start()
    high, unit_rows = PH // GROUP, SLOTS * BS
    per_seg = high * received
    to, at_row = iota((per_seg, per_seg), 0), iota((per_seg, per_seg), 1)
    wanted = (
        to % received // unit_rows * (high * unit_rows) + to // received * unit_rows
    ) + to % unit_rows
    order = jnp.where(at_row == wanted, 1.0, 0.0).astype(BF16)
    me = me_ref[0]
    mine = me & (CORES - 1)
    for s in range(segs):
        i = s // CORES
        chip = (lax.div(me, CORES) + chips - STEPS[i]) & (chips - 1)
        if s % CORES:
            source, seg = far_ref[i], chip * CORES + 1 - mine
        else:
            source = near[i][(chip * CORES if i == 0 else 0) + mine]
            seg = chip * CORES + mine
        block = dot(order, source).astype(BF16)
        at = pl.ds(pl.multiple_of(seg * received, received), received)
        for p in range(PH):
            x_ref[p, at, :] = block[
                p // GROUP * received : (p // GROUP + 1) * received,
                p % GROUP * LANES : (p % GROUP + 1) * LANES,
            ]
    scale = whiten(x_ref, y_ref, f_ref, sum_ref, trace_ref, segs)

    def put(p, s, tile):
        phase_ref[p * received : (p + 1) * received, s * LANES : (s + 1) * LANES] = tile

    fold(trace_ref, scale, segs, put)
    copies[0].wait()
    edge = dot_t(phase_ref[...], extra_ref[...])
    width = stations * FINE
    lag = iota((received, width), 1) % FINE
    sums = jnp.zeros((received, width), F32)
    for p in range(FINE):
        block = edge[p * received : (p + 1) * received]
        turn = (p + 1 - FINE) % width
        block = pltpu.roll(block, turn, 1) if turn else block
        sums = sums + jnp.where(lag <= p, block, 0.0)
    edge_ref[...] = sums
    lane = iota((received, LAGS), 1)
    norm = 1.0 / math.sqrt(segs * PH * LANES)

    def multiply(a):
        block = shifted_hbm.at[pl.ds(pl.multiple_of(a * LAGS, LAGS), LAGS), :]
        pltpu.make_async_copy(block, shifted_ref.at[a], sems.at[a]).wait()
        return dot_t(phase_ref[...], shifted_ref[a])

    def combine(a, product_ref):
        first = pltpu.roll(edge_ref[...], (stations - a) * FINE, 1)
        sums = jnp.where(lane < FINE, first[:, :LAGS], 0.0)
        for p in range(FINE):
            block = pltpu.roll(product_ref[p * received : (p + 1) * received], p + 1, 1)
            sums = sums + jnp.where(lane > p, block, 0.0)
        sums = sums * norm
        for c in range(LAGS // LANES):
            total_ref[c, pl.ds(a, received, stride=stations), :] = sums[
                :, c * LANES : (c + 1) * LANES
            ]

    even_ref[...] = multiply(0)

    def body(i, _):
        odd_ref[...] = multiply(2 * i + 1)
        combine(2 * i, even_ref)
        even_ref[...] = multiply(2 * i + 2)
        combine(2 * i + 1, odd_ref)
        return 0

    lax.fori_loop(0, stations // 2 - 1, body, 0)
    odd_ref[...] = multiply(stations - 1)
    combine(stations - 2, even_ref)
    combine(stations - 1, odd_ref)
    for c in range(LAGS // LANES):
        out_ref[:, c * LANES : (c + 1) * LANES] = total_ref[c].astype(BF16)


def correlate(me, near, far, shifted, extra, segs):
    rows = segs * far.shape[1] // (PH // GROUP)
    count = rows // segs
    stations = shifted.shape[0] // LAGS
    total = shifted.shape[1]
    return pl.pallas_call(
        lambda *refs: correlate_kernel(segs, *refs),
        out_shape=jax.ShapeDtypeStruct((count * stations, LAGS), BF16),
        in_specs=[
            pl.BlockSpec(memory_space=pltpu.SMEM),
            *[pl.BlockSpec(memory_space=pltpu.VMEM)] * (len(near) + 1),
            pl.BlockSpec(memory_space=pltpu.HBM),
            pl.BlockSpec(memory_space=pltpu.HBM),
        ],
        out_specs=pl.BlockSpec(memory_space=pltpu.VMEM),
        scratch_shapes=[
            *whiten_scratch(rows),
            pltpu.VMEM((count * FINE, total), BF16),
            pltpu.VMEM((count, stations * FINE), F32),
            pltpu.VMEM((LAGS // LANES, count * stations, LANES), F32),
            pltpu.VMEM((stations, LAGS, total), BF16),
            pltpu.VMEM((stations * FINE, total), BF16),
            pltpu.VMEM((count * FINE, LAGS), F32),
            pltpu.VMEM((count * FINE, LAGS), F32),
            pltpu.SemaphoreType.DMA((stations + 1,)),
        ],
        compiler_params=pltpu.CompilerParams(vmem_limit_bytes=48 * MIB),
        cost_estimate=pl.CostEstimate(
            flops=6000 * MIB, bytes_accessed=20 * MIB, transcendentals=0
        ),
        name="correlate",
    )(
        me,
        *near,
        far,
        in_hbm(shifted),
        in_hbm(extra),
    )


def on_device(records, owners):
    stations, length = records.shape
    segs, sources = lax.axis_size("seg"), lax.axis_size("sta")
    chips = segs // CORES
    me = lax.axis_index("seg")
    chip = lax.div(me, jnp.int32(CORES))
    along_x = [[(i, (i + k * CORES) % segs) for i in range(segs)] for k in range(chips)]
    across = [(i, i ^ 1) for i in range(segs)]
    phased, slots = prepare(records, owners.T, sources)
    slots = slots.reshape(sources, -1, GROUP * LANES)
    passing = lax.all_to_all(slots, "sta", 0, 0, tiled=True)
    passing = passing.reshape(segs, -1, GROUP * LANES)
    other = lax.ppermute(phased, "seg", across)
    pair = jnp.concatenate([phased, other], axis=0)
    pairs = [pair] + [lax.ppermute(pair, "seg", along_x[k]) for k in STEPS[1:]]
    mine, phases = own_part(me.reshape(1), pairs, segs)
    passing, phases = lax.optimization_barrier((passing, phases))
    shifted, extra = shift(phases)
    near = [passing]
    for k in STEPS[1:]:
        at = ((chip + k) & (chips - 1)) * CORES
        block = lax.dynamic_slice_in_dim(passing, at, CORES, 0)
        near.append(lax.ppermute(block, "seg", along_x[k]))
    near, shifted, extra, mine = lax.optimization_barrier((near, shifted, extra, mine))
    far = lax.ppermute(pack(me.reshape(1), near), "seg", across)
    whitened = in_sample_order(mine)
    result = correlate(me.reshape(1), near, far, shifted, extra, segs)
    return whitened, result.reshape(-1, stations, LAGS)


def solution(mesh):
    return jax.shard_map(
        on_device,
        mesh=mesh,
        in_specs=(P("sta", "seg"), P("sta", None)),
        out_specs=(P("sta", "seg"), P("seg", "sta", None)),
        check_vma=False,
    )
```

```python
import math

import jax
import jax.numpy as jnp
from jax import lax
from jax.experimental import pallas as pl
from jax.experimental.pallas import tpu as pltpu
from jax.sharding import PartitionSpec as P

LAGS = 512
BS = 2
SLOTS = 2
WATER = 0.5
EPSILON = 1e-06

PH = 16
LANES = 128
STEPS = (0, 2, 3, 1)
FINE = 32
CORES = 2
GROUP = 4
F32 = jnp.float32
BF16 = jnp.bfloat16
MIB = 1 << 20


def dot(a, b):
    return lax.dot_general(a, b, (((1,), (0,)), ((), ())), preferred_element_type=F32)


def dot_t(a, b):
    return lax.dot_general(a, b, (((1,), (1,)), ((), ())), preferred_element_type=F32)


def in_hbm(x):
    return pltpu.with_memory_space_constraint(x, pltpu.HBM)


def iota(shape, axis):
    return lax.broadcasted_iota(jnp.int32, shape, axis)


def cos_sin(phase, period):
    phase = phase & (period - 1)
    phase = jnp.where(phase >= period // 2, phase - period, phase)
    theta = phase.astype(F32) * (2.0 * math.pi / period)
    square = theta * theta
    cosine = jnp.full(theta.shape, 1.0 / math.factorial(20), F32)
    sine = jnp.full(theta.shape, 1.0 / math.factorial(21), F32)
    for n in range(9, -1, -1):
        cosine = (1.0 if n % 2 == 0 else -1.0) / math.factorial(2 * n) + square * cosine
        sine = (1.0 if n % 2 == 0 else -1.0) / math.factorial(2 * n + 1) + square * sine
    return cosine, sine * theta


def spread():
    shape = (LANES, PH * LANES)
    source, target = iota(shape, 0), iota(shape, 1)
    hit = (target // LANES == source % PH) & (target % LANES == source // PH)
    return jnp.where(hit, 1.0, 0.0).astype(BF16)


def gather_back():
    shape = (LANES, PH * LANES)
    target, source = iota(shape, 0), iota(shape, 1)
    lane = source % LANES
    place = FINE // PH * (lane % (LANES // 2)) + lane // (LANES // 2)
    hit = (source // LANES == target % PH) & (place == target // PH)
    return jnp.where(hit, 1.0, 0.0).astype(BF16)


def fold(trace_ref, scale, segs, put):
    rows = trace_ref.shape[1] // segs
    low = iota((rows, LANES), 1) < LANES // 2
    for p in range(PH):
        for s in range(segs // 2):
            first = trace_ref[p, 2 * s * rows : (2 * s + 1) * rows, :] * scale
            second = trace_ref[p, (2 * s + 1) * rows : (2 * s + 2) * rows, :] * scale
            put(p, s, jnp.where(low, first, pltpu.roll(second, LANES // 2, 1)).astype(BF16))
            put(p + PH, s, jnp.where(low, pltpu.roll(first, LANES // 2, 1), second).astype(BF16))


def prepare_kernel(
    owner_count, records_hbm, owners_hbm, phased_hbm, slots_hbm,
    records_ref, owners_ref, phased_ref, slots_ref, sems,
):
    loads = [
        pltpu.make_async_copy(records_hbm, records_ref, sems.at[0]),
        pltpu.make_async_copy(owners_hbm, owners_ref, sems.at[1]),
    ]
    for load in loads:
        load.start()
    stations, length = records_ref.shape
    dests, blocks = owners_ref.shape
    per_tile = LANES // PH
    one_hot = spread()
    for load in loads:
        load.wait()
    tiles = jnp.concatenate(
        [records_ref[:, t * LANES : (t + 1) * LANES] for t in range(length // LANES)], axis=0
    )
    parts = dot(tiles, one_hot)
    phases = []
    for p in range(PH):
        total = None
        for t in range(length // LANES):
            part = parts[t * stations : (t + 1) * stations, p * LANES : (p + 1) * LANES]
            part = pltpu.roll(part, per_tile * t, 1) if t else part
            total = part if total is None else total + part
        phases.append(total.astype(BF16))
    for p in range(PH):
        phased_ref[:, p * LANES : (p + 1) * LANES] = phases[p]
    stores = [pltpu.make_async_copy(phased_ref, phased_hbm, sems.at[2])]
    stores[0].start()
    high = PH // GROUP
    stacked = jnp.concatenate(
        [jnp.concatenate(phases[h * GROUP : (h + 1) * GROUP], axis=1) for h in range(high)], axis=0
    )
    rows, width = owner_count * high * SLOTS * BS, high * stations
    k_of, column = iota((blocks, width), 0), iota((blocks, width), 1)
    expand = jnp.where(column % stations // BS == k_of, 1.0, 0.0)
    named = lax.dot_general(
        owners_ref[...].astype(F32), expand, (((1,), (0,)), ((), ())), preferred_element_type=F32
    )
    row, col = iota((rows, width), 0), iota((rows, width), 1)
    owner = (row // (high * SLOTS * BS)).astype(F32)
    wanted = jnp.zeros((rows, width), F32)
    for d in range(dests):
        wanted = jnp.maximum(wanted, jnp.where(named[d : d + 1, :] == owner, 1.0, 0.0))
    first, second = iota((width, width), 0), iota((width, width), 1)
    earlier = (
        (first // stations == second // stations)
        & (first % stations // BS < second % stations // BS)
        & (first % BS == 0)
    )
    rank = dot(wanted.astype(BF16), jnp.where(earlier, 1.0, 0.0).astype(BF16))
    slot = (row // BS % SLOTS).astype(F32)
    right = (
        (rank == slot)
        & (row % BS == col % BS)
        & (row // (SLOTS * BS) % high == col // stations)
    )
    select = jnp.where(right, wanted, 0.0).astype(BF16)
    parts, size = 4, rows // 4
    for i in range(parts):
        at = pl.ds(i * size, size)
        slots_ref[at, :] = dot(select[i * size : (i + 1) * size], stacked).astype(BF16)
        stores.append(pltpu.make_async_copy(slots_ref.at[at, :], slots_hbm.at[at, :], sems.at[3 + i]))
        stores[-1].start()
    for store in stores:
        store.wait()


def prepare(records, owners, owner_count):
    stations, length = records.shape
    rows = owner_count * SLOTS * BS * PH // GROUP
    return pl.pallas_call(
        lambda *refs: prepare_kernel(owner_count, *refs),
        out_shape=(
            pltpu.HBM((stations, length), BF16),
            pltpu.HBM((rows, GROUP * LANES), BF16),
        ),
        in_specs=[pl.BlockSpec(memory_space=pltpu.HBM)] * 2,
        out_specs=[pl.BlockSpec(memory_space=pltpu.HBM)] * 2,
        scratch_shapes=[
            pltpu.VMEM(records.shape, records.dtype),
            pltpu.VMEM(owners.shape, owners.dtype),
            pltpu.VMEM((stations, length), BF16),
            pltpu.VMEM((rows, GROUP * LANES), BF16),
            pltpu.SemaphoreType.DMA((7,)),
        ],
        compiler_params=pltpu.CompilerParams(vmem_limit_bytes=16 * MIB),
        cost_estimate=pl.CostEstimate(
            flops=100 * MIB, bytes_accessed=2 * MIB, transcendentals=0
        ),
        name="prepare",
    )(in_hbm(records), in_hbm(owners))


def add(a, b):
    return a[0] + b[0], a[1] + b[1]


def sub(a, b):
    return a[0] - b[0], a[1] - b[1]


def times_i(a, sign):
    return (-a[1], a[0]) if sign > 0 else (a[1], -a[0])


def times(a, b):
    return a[0] * b[0] - a[1] * b[1], a[0] * b[1] + a[1] * b[0]


def unit(a, k, sign):
    k %= 16
    if k == 0:
        return a
    if k == 4:
        return times_i(a, sign)
    if k == 8:
        return -a[0], -a[1]
    if k == 12:
        return times_i(a, -sign)
    angle = 2.0 * math.pi * k / 16
    return times(a, (math.cos(angle), sign * math.sin(angle)))


def four(a, sign):
    s, d = add(a[0], a[2]), sub(a[0], a[2])
    t, e = add(a[1], a[3]), times_i(sub(a[1], a[3]), sign)
    return [add(s, t), add(d, e), sub(s, t), sub(d, e)]


def forward_sixteen(v):
    inner = [four([v[4 * p1 + p0] for p1 in range(4)], 1) for p0 in range(4)]
    out = [None] * 8
    for fa in range(4):
        u = [unit(inner[p0][fa], p0 * fa, 1) for p0 in range(4)]
        s, t = add(u[0], u[2]), add(u[1], u[3])
        out[fa] = add(s, t)
        out[fa + 4] = add(sub(u[0], u[2]), times_i(sub(u[1], u[3]), 1))
        if fa == 0:
            last = s[0] - t[0]
    return out, last


def inverse_sixteen(f):
    out = [None] * 16
    for p0 in range(4):
        inner = []
        for fa in range(4):
            turned = unit(f[fa + 4], 4 * p0, -1)
            inner.append(unit(add(f[fa], turned), p0 * fa, -1))
        for p1, value in enumerate(four(inner, -1)):
            out[4 * p1 + p0] = value
    return out


def seg_total(values, segs):
    rows = values.shape[0] // segs
    total = values[:rows]
    for s in range(1, segs):
        total = total + values[s * rows : (s + 1) * rows]
    return total


def whiten(x_ref, y_ref, f_ref, sum_ref, trace_ref, segs):
    rows = x_ref.shape[1]
    length = PH * LANES
    window = length * segs
    half = PH // 2
    n, k = iota((LANES, LANES), 0), iota((LANES, LANES), 1)
    cosine, sine = cos_sin(n * k, LANES)
    table = jnp.concatenate([cosine, sine], axis=1).astype(BF16)
    folded = FINE // PH * (k % (LANES // 2)) + k // (LANES // 2)
    back = jnp.concatenate(cos_sin(n * folded, LANES), axis=0).astype(BF16)
    turn_cos, turn_sin = cos_sin(iota((PH, LANES), 0) * iota((PH, LANES), 1), length)
    for p in range(PH):
        y_ref[p] = dot(x_ref[p], table)
    lane = iota((8, LANES), 1)

    def forward(i, _):
        at = pl.ds(pl.multiple_of(i * 8, 8), 8)
        v = []
        for p in range(PH):
            y = y_ref[p, at, :LANES], y_ref[p, at, LANES:]
            v.append(times(y, (turn_cos[p : p + 1], turn_sin[p : p + 1])) if p else y)
        out, last = forward_sixteen(v)
        total = None
        for j, (re, im) in enumerate(out):
            if j == 0:
                mag = jnp.where(lane == 0, jnp.abs(re), jnp.sqrt(re * re + im * im))
                im = jnp.where(lane == 0, last, im)
                total = jnp.where(lane == 0, 0.5 * (jnp.abs(re) + jnp.abs(im)), mag)
            else:
                mag = jnp.sqrt(re * re + im * im)
                total = total + mag
            f_ref[j, at, :] = re
            f_ref[half + j, at, :] = im
            f_ref[2 * half + j, at, :] = mag
        sum_ref[at, :] = total
        return 0

    lax.fori_loop(0, rows // 8, forward, 0, unroll=4)
    amp = 2.0 * jnp.sum(seg_total(sum_ref[...], segs), axis=1, keepdims=True)
    level = WATER * amp / window + EPSILON
    sum_ref[...] = jnp.concatenate(
        [jnp.broadcast_to(level, (rows // segs, LANES))] * segs, axis=0
    )

    def inverse(i, _):
        at = pl.ds(pl.multiple_of(i * 8, 8), 8)
        level = sum_ref[at, :]
        f = []
        for j in range(half):
            re, im, mag = f_ref[j, at, :], f_ref[half + j, at, :], f_ref[2 * half + j, at, :]
            if j == 0:
                edge = im / (jnp.abs(im) + level)
                share = 2.0 / (mag + level)
                f.append(
                    (
                        jnp.where(lane == 0, 0.5, 1.0) * (re * share),
                        jnp.where(lane == 0, 0.0, im * share),
                    )
                )
                edge = jnp.where(lane == 0, edge, 0.0)
            else:
                share = 2.0 / (mag + level)
                f.append((re * share, im * share))
        for p, z in enumerate(inverse_sixteen(f)):
            if p:
                z = times(z, (turn_cos[p : p + 1], -turn_sin[p : p + 1]))
            y_ref[p, at, :LANES] = z[0] - edge if p % 2 else z[0] + edge
            y_ref[p, at, LANES:] = z[1]
        return 0

    lax.fori_loop(0, rows // 8, inverse, 0, unroll=4)
    energy = jnp.zeros((rows, LANES), F32)
    for p in range(PH):
        trace = dot(y_ref[p].astype(BF16), back) * (1.0 / length)
        energy = energy + trace * trace
        trace_ref[p] = trace
    energy = jnp.sum(seg_total(energy, segs), axis=1, keepdims=True)
    return lax.rsqrt(energy / window + EPSILON)


def whiten_scratch(rows):
    return [
        pltpu.VMEM((PH, rows, LANES), BF16),
        pltpu.VMEM((PH, rows, 2 * LANES), F32),
        pltpu.VMEM((3 * PH // 2, rows, LANES), F32),
        pltpu.VMEM((rows, LANES), F32),
        pltpu.VMEM((PH, rows, LANES), F32),
    ]


def own_kernel(segs, me_ref, *refs):
    pairs, refs = refs[: segs // CORES], refs[segs // CORES :]
    white_ref, phase_ref, x_ref, y_ref, f_ref, sum_ref, trace_ref = refs
    rows, length = x_ref.shape[1], PH * LANES
    stations = rows // segs
    per_tile = LANES // PH
    me, chips = me_ref[0], segs // CORES
    for i, ref in enumerate(pairs):
        chip = (lax.div(me, CORES) + chips - STEPS[i]) & (chips - 1)
        for j in range(CORES):
            core = (me + j) & (CORES - 1)
            at = pl.ds(pl.multiple_of((chip * CORES + core) * stations, stations), stations)
            for p in range(PH):
                x_ref[p, at, :] = ref[
                    j * stations : (j + 1) * stations, p * LANES : (p + 1) * LANES
                ]
    scale = whiten(x_ref, y_ref, f_ref, sum_ref, trace_ref, segs)
    def put(p, s, tile):
        phase_ref[s, (FINE - 1 - p) * stations : (FINE - p) * stations, :] = tile.astype(F32)

    fold(trace_ref, scale, segs, put)
    mine = pl.ds(pl.multiple_of(me * stations, stations), stations)
    for p in range(PH):
        white_ref[:, p * LANES : (p + 1) * LANES] = (trace_ref[p, mine, :] * scale).astype(BF16)


def order_kernel(phased_ref, white_ref):
    stations, length = phased_ref.shape
    per_tile = LANES // PH
    tiles = [phased_ref[:, p * LANES : (p + 1) * LANES].astype(F32) for p in range(PH)]
    moved = []
    for t in range(length // LANES):
        turn = (LANES - per_tile // 2 * t) % LANES
        moved.append(
            jnp.concatenate(
                [(pltpu.roll(x, turn, 1) if turn else x).astype(BF16) for x in tiles], axis=1
            )
        )
    natural = dot_t(jnp.concatenate(moved, axis=0), gather_back()).astype(BF16)
    for t in range(length // LANES):
        white_ref[:, t * LANES : (t + 1) * LANES] = natural[t * stations : (t + 1) * stations]


def in_sample_order(phased):
    return pl.pallas_call(
        order_kernel,
        out_shape=jax.ShapeDtypeStruct(phased.shape, BF16),
        in_specs=[pl.BlockSpec(memory_space=pltpu.VMEM)],
        out_specs=pl.BlockSpec(memory_space=pltpu.VMEM),
        compiler_params=pltpu.CompilerParams(vmem_limit_bytes=8 * MIB),
        cost_estimate=pl.CostEstimate(flops=1000 * MIB, bytes_accessed=MIB, transcendentals=0),
        name="order",
    )(phased)


def pack_kernel(me_ref, *refs):
    near, out_ref = refs[:-1], refs[-1]
    other = 1 - (me_ref[0] & (CORES - 1))
    chip = lax.div(me_ref[0], CORES)
    for i, ref in enumerate(near):
        out_ref[i] = ref[(chip * CORES if i == 0 else 0) + other]


def pack(me, near):
    return pl.pallas_call(
        pack_kernel,
        out_shape=jax.ShapeDtypeStruct((len(near), *near[0].shape[1:]), BF16),
        in_specs=[
            pl.BlockSpec(memory_space=pltpu.SMEM),
            *[pl.BlockSpec(memory_space=pltpu.VMEM)] * len(near),
        ],
        out_specs=pl.BlockSpec(memory_space=pltpu.VMEM),
        compiler_params=pltpu.CompilerParams(vmem_limit_bytes=8 * MIB),
        cost_estimate=pl.CostEstimate(flops=0, bytes_accessed=MIB, transcendentals=0),
        name="pack",
    )(me, *near)


def own_part(me, pairs, segs):
    rows, length = len(pairs) * pairs[0].shape[0], pairs[0].shape[1]
    stations = rows // segs
    return pl.pallas_call(
        lambda *refs: own_kernel(segs, *refs),
        out_shape=(
            jax.ShapeDtypeStruct((stations, length), BF16),
            jax.ShapeDtypeStruct((segs // 2, FINE * stations, LANES), F32),
        ),
        in_specs=[
            pl.BlockSpec(memory_space=pltpu.SMEM),
            *[pl.BlockSpec(memory_space=pltpu.VMEM)] * len(pairs),
        ],
        out_specs=[pl.BlockSpec(memory_space=pltpu.VMEM)] * 2,
        scratch_shapes=whiten_scratch(rows),
        compiler_params=pltpu.CompilerParams(vmem_limit_bytes=32 * MIB),
        cost_estimate=pl.CostEstimate(
            flops=2000 * MIB, bytes_accessed=4 * MIB, transcendentals=0
        ),
        name="own",
    )(me, *pairs)


def shift_kernel(stations, phase_ref, shifted_hbm, extra_hbm, shifted_ref, extra_ref, sems):
    count = LAGS // FINE
    tiles = phase_ref.shape[0]
    lane = iota((FINE, LANES), 1)

    def copies(a):
        to = shifted_hbm.at[pl.ds(pl.multiple_of(a * LAGS, LAGS), LAGS), :]
        to_extra = extra_hbm.at[pl.ds(pl.multiple_of(a * FINE, FINE), FINE), :]
        return (
            pltpu.make_async_copy(shifted_ref.at[a], to, sems.at[0, a]),
            pltpu.make_async_copy(extra_ref.at[a], to_extra, sems.at[1, a]),
        )

    def body(a, _):
        block = [phase_ref[s, pl.ds(a, FINE, stride=stations), :] for s in range(tiles)]
        zero = jnp.zeros((FINE, LANES), F32)
        for i in range(-1, count):
            m = i + 1 - count // 2
            turned = [pltpu.roll(tile, m % LANES, 1) if m else tile for tile in block]
            for t in range(tiles):
                if m > 0:
                    moved = jnp.where(lane >= m, turned[t], turned[t - 1] if t else zero)
                elif m < 0:
                    later = turned[t + 1] if t + 1 < tiles else zero
                    moved = jnp.where(lane < LANES + m, turned[t], later)
                else:
                    moved = turned[t]
                cols = slice(t * LANES, (t + 1) * LANES)
                if i < 0:
                    extra_ref[a, :, cols] = moved.astype(BF16)
                else:
                    shifted_ref[a, i * FINE : (i + 1) * FINE, cols] = moved.astype(BF16)
        for copy in copies(a):
            copy.start()
        return 0

    lax.fori_loop(0, stations, body, 0, unroll=4)

    def finish(a, _):
        for copy in copies(a):
            copy.wait()
        return 0

    lax.fori_loop(0, stations, finish, 0)


def shift(phases):
    stations = phases.shape[1] // FINE
    total = phases.shape[0] * LANES
    return pl.pallas_call(
        lambda *refs: shift_kernel(stations, *refs),
        out_shape=(
            pltpu.HBM((stations * LAGS, total), BF16),
            pltpu.HBM((stations * FINE, total), BF16),
        ),
        in_specs=[pl.BlockSpec(memory_space=pltpu.VMEM)],
        out_specs=[pl.BlockSpec(memory_space=pltpu.HBM)] * 2,
        scratch_shapes=[
            pltpu.VMEM((stations, LAGS, total), BF16),
            pltpu.VMEM((stations, FINE, total), BF16),
            pltpu.SemaphoreType.DMA((2, stations)),
        ],
        compiler_params=pltpu.CompilerParams(vmem_limit_bytes=16 * MIB),
        cost_estimate=pl.CostEstimate(
            flops=1, bytes_accessed=9 * MIB, transcendentals=0
        ),
        name="shift",
    )(phases)


def correlate_kernel(segs, me_ref, *refs):
    chips = segs // CORES
    near, (far_ref, shifted_hbm, extra_hbm, out_ref), refs = (
        refs[:chips],
        refs[chips : chips + 4],
        refs[chips + 4 :],
    )
    x_ref, y_ref, f_ref, sum_ref, trace_ref, phase_ref, edge_ref, total_ref = refs[:8]
    shifted_ref, extra_ref, even_ref, odd_ref, sems = refs[8:]
    rows = x_ref.shape[1]
    received = rows // segs
    stations = shifted_ref.shape[0]
    copies = [pltpu.make_async_copy(extra_hbm, extra_ref, sems.at[stations])]
    for a in range(stations):
        block = shifted_hbm.at[pl.ds(a * LAGS, LAGS), :]
        copies.append(pltpu.make_async_copy(block, shifted_ref.at[a], sems.at[a]))
    for copy in copies:
        copy.start()
    high, unit_rows = PH // GROUP, SLOTS * BS
    per_seg = high * received
    to, at_row = iota((per_seg, per_seg), 0), iota((per_seg, per_seg), 1)
    wanted = (
        to % received // unit_rows * (high * unit_rows) + to // received * unit_rows
    ) + to % unit_rows
    order = jnp.where(at_row == wanted, 1.0, 0.0).astype(BF16)
    me = me_ref[0]
    mine = me & (CORES - 1)
    for s in range(segs):
        i = s // CORES
        chip = (lax.div(me, CORES) + chips - STEPS[i]) & (chips - 1)
        if s % CORES:
            source, seg = far_ref[i], chip * CORES + 1 - mine
        else:
            source = near[i][(chip * CORES if i == 0 else 0) + mine]
            seg = chip * CORES + mine
        block = dot(order, source).astype(BF16)
        at = pl.ds(pl.multiple_of(seg * received, received), received)
        for p in range(PH):
            x_ref[p, at, :] = block[
                p // GROUP * received : (p // GROUP + 1) * received,
                p % GROUP * LANES : (p % GROUP + 1) * LANES,
            ]
    scale = whiten(x_ref, y_ref, f_ref, sum_ref, trace_ref, segs)

    def put(p, s, tile):
        phase_ref[p * received : (p + 1) * received, s * LANES : (s + 1) * LANES] = tile

    fold(trace_ref, scale, segs, put)
    copies[0].wait()
    edge = dot_t(phase_ref[...], extra_ref[...])
    width = stations * FINE
    lag = iota((received, width), 1) % FINE
    sums = jnp.zeros((received, width), F32)
    for p in range(FINE):
        block = edge[p * received : (p + 1) * received]
        turn = (p + 1 - FINE) % width
        block = pltpu.roll(block, turn, 1) if turn else block
        sums = sums + jnp.where(lag <= p, block, 0.0)
    edge_ref[...] = sums
    lane = iota((received, LAGS), 1)
    norm = 1.0 / math.sqrt(segs * PH * LANES)

    def multiply(a):
        block = shifted_hbm.at[pl.ds(pl.multiple_of(a * LAGS, LAGS), LAGS), :]
        pltpu.make_async_copy(block, shifted_ref.at[a], sems.at[a]).wait()
        return dot_t(phase_ref[...], shifted_ref[a])

    def combine(a, product_ref):
        first = pltpu.roll(edge_ref[...], (stations - a) * FINE, 1)
        sums = jnp.where(lane < FINE, first[:, :LAGS], 0.0)
        for p in range(FINE):
            block = pltpu.roll(product_ref[p * received : (p + 1) * received], p + 1, 1)
            sums = sums + jnp.where(lane > p, block, 0.0)
        sums = sums * norm
        for c in range(LAGS // LANES):
            total_ref[c, pl.ds(a, received, stride=stations), :] = sums[
                :, c * LANES : (c + 1) * LANES
            ]

    even_ref[...] = multiply(0)

    def body(i, _):
        odd_ref[...] = multiply(2 * i + 1)
        combine(2 * i, even_ref)
        even_ref[...] = multiply(2 * i + 2)
        combine(2 * i + 1, odd_ref)
        return 0

    lax.fori_loop(0, stations // 2 - 1, body, 0)
    odd_ref[...] = multiply(stations - 1)
    combine(stations - 2, even_ref)
    combine(stations - 1, odd_ref)
    for c in range(LAGS // LANES):
        out_ref[:, c * LANES : (c + 1) * LANES] = total_ref[c].astype(BF16)


def correlate(me, near, far, shifted, extra, segs):
    rows = segs * far.shape[1] // (PH // GROUP)
    count = rows // segs
    stations = shifted.shape[0] // LAGS
    total = shifted.shape[1]
    return pl.pallas_call(
        lambda *refs: correlate_kernel(segs, *refs),
        out_shape=jax.ShapeDtypeStruct((count * stations, LAGS), BF16),
        in_specs=[
            pl.BlockSpec(memory_space=pltpu.SMEM),
            *[pl.BlockSpec(memory_space=pltpu.VMEM)] * (len(near) + 1),
            pl.BlockSpec(memory_space=pltpu.HBM),
            pl.BlockSpec(memory_space=pltpu.HBM),
        ],
        out_specs=pl.BlockSpec(memory_space=pltpu.VMEM),
        scratch_shapes=[
            *whiten_scratch(rows),
            pltpu.VMEM((count * FINE, total), BF16),
            pltpu.VMEM((count, stations * FINE), F32),
            pltpu.VMEM((LAGS // LANES, count * stations, LANES), F32),
            pltpu.VMEM((stations, LAGS, total), BF16),
            pltpu.VMEM((stations * FINE, total), BF16),
            pltpu.VMEM((count * FINE, LAGS), F32),
            pltpu.VMEM((count * FINE, LAGS), F32),
            pltpu.SemaphoreType.DMA((stations + 1,)),
        ],
        compiler_params=pltpu.CompilerParams(vmem_limit_bytes=48 * MIB),
        cost_estimate=pl.CostEstimate(
            flops=6000 * MIB, bytes_accessed=20 * MIB, transcendentals=0
        ),
        name="correlate",
    )(
        me,
        *near,
        far,
        in_hbm(shifted),
        in_hbm(extra),
    )


def on_device(records, owners):
    stations, length = records.shape
    segs, sources = lax.axis_size("seg"), lax.axis_size("sta")
    chips = segs // CORES
    me = lax.axis_index("seg")
    chip = lax.div(me, jnp.int32(CORES))
    along_x = [[(i, (i + k * CORES) % segs) for i in range(segs)] for k in range(chips)]
    across = [(i, i ^ 1) for i in range(segs)]
    phased, slots = prepare(records, owners.T, sources)
    slots = slots.reshape(sources, -1, GROUP * LANES)
    passing = lax.all_to_all(slots, "sta", 0, 0, tiled=True)
    passing = passing.reshape(segs, -1, GROUP * LANES)
    other = lax.ppermute(phased, "seg", across)
    pair = jnp.concatenate([phased, other], axis=0)
    pairs = [pair] + [lax.ppermute(pair, "seg", along_x[k]) for k in STEPS[1:]]
    mine, phases = own_part(me.reshape(1), pairs, segs)
    passing, phases = lax.optimization_barrier((passing, phases))
    shifted, extra = shift(phases)
    near = [passing]
    for k in STEPS[1:]:
        at = ((chip + k) & (chips - 1)) * CORES
        block = lax.dynamic_slice_in_dim(passing, at, CORES, 0)
        near.append(lax.ppermute(block, "seg", along_x[k]))
    near, shifted, extra, mine = lax.optimization_barrier((near, shifted, extra, mine))
    far = lax.ppermute(pack(me.reshape(1), near), "seg", across)
    whitened = in_sample_order(mine)
    result = correlate(me.reshape(1), near, far, shifted, extra, segs)
    return whitened, result.reshape(-1, stations, LAGS)


def solution(mesh):
    return jax.shard_map(
        on_device,
        mesh=mesh,
        in_specs=(P("sta", "seg"), P("sta", None)),
        out_specs=(P("sta", "seg"), P("seg", "sta", None)),
        check_vma=False,
    )
```

```python
import math

import jax
import jax.numpy as jnp
from jax import lax
from jax.experimental import pallas as pl
from jax.experimental.pallas import tpu as pltpu
from jax.sharding import PartitionSpec as P

LAGS = 512
BS = 2
SLOTS = 2
WATER = 0.5
EPSILON = 1e-06

PH = 16
LANES = 128
STEPS = (0, 2, 3, 1)
FINE = 32
CORES = 2
GROUP = 4
F32 = jnp.float32
BF16 = jnp.bfloat16
MIB = 1 << 20


def dot(a, b):
    return lax.dot_general(a, b, (((1,), (0,)), ((), ())), preferred_element_type=F32)


def dot_t(a, b):
    return lax.dot_general(a, b, (((1,), (1,)), ((), ())), preferred_element_type=F32)


def in_hbm(x):
    return pltpu.with_memory_space_constraint(x, pltpu.HBM)


def iota(shape, axis):
    return lax.broadcasted_iota(jnp.int32, shape, axis)


def cos_sin(phase, period):
    phase = phase & (period - 1)
    phase = jnp.where(phase >= period // 2, phase - period, phase)
    theta = phase.astype(F32) * (2.0 * math.pi / period)
    square = theta * theta
    cosine = jnp.full(theta.shape, 1.0 / math.factorial(20), F32)
    sine = jnp.full(theta.shape, 1.0 / math.factorial(21), F32)
    for n in range(9, -1, -1):
        cosine = (1.0 if n % 2 == 0 else -1.0) / math.factorial(2 * n) + square * cosine
        sine = (1.0 if n % 2 == 0 else -1.0) / math.factorial(2 * n + 1) + square * sine
    return cosine, sine * theta


def spread():
    shape = (LANES, PH * LANES)
    source, target = iota(shape, 0), iota(shape, 1)
    hit = (target // LANES == source % PH) & (target % LANES == source // PH)
    return jnp.where(hit, 1.0, 0.0).astype(BF16)


def gather_back():
    shape = (LANES, PH * LANES)
    target, source = iota(shape, 0), iota(shape, 1)
    lane = source % LANES
    place = FINE // PH * (lane % (LANES // 2)) + lane // (LANES // 2)
    hit = (source // LANES == target % PH) & (place == target // PH)
    return jnp.where(hit, 1.0, 0.0).astype(BF16)


def fold(trace_ref, scale, segs, put):
    rows = trace_ref.shape[1] // segs
    low = iota((rows, LANES), 1) < LANES // 2
    for p in range(PH):
        for s in range(segs // 2):
            first = trace_ref[p, 2 * s * rows : (2 * s + 1) * rows, :] * scale
            second = trace_ref[p, (2 * s + 1) * rows : (2 * s + 2) * rows, :] * scale
            put(p, s, jnp.where(low, first, pltpu.roll(second, LANES // 2, 1)).astype(BF16))
            put(p + PH, s, jnp.where(low, pltpu.roll(first, LANES // 2, 1), second).astype(BF16))


def prepare_kernel(
    owner_count, records_hbm, owners_hbm, phased_hbm, slots_hbm,
    records_ref, owners_ref, phased_ref, slots_ref, sems,
):
    loads = [
        pltpu.make_async_copy(records_hbm, records_ref, sems.at[0]),
        pltpu.make_async_copy(owners_hbm, owners_ref, sems.at[1]),
    ]
    for load in loads:
        load.start()
    stations, length = records_ref.shape
    dests, blocks = owners_ref.shape
    per_tile = LANES // PH
    one_hot = spread()
    for load in loads:
        load.wait()
    tiles = jnp.concatenate(
        [records_ref[:, t * LANES : (t + 1) * LANES] for t in range(length // LANES)], axis=0
    )
    parts = dot(tiles, one_hot)
    phases = []
    for p in range(PH):
        total = None
        for t in range(length // LANES):
            part = parts[t * stations : (t + 1) * stations, p * LANES : (p + 1) * LANES]
            part = pltpu.roll(part, per_tile * t, 1) if t else part
            total = part if total is None else total + part
        phases.append(total.astype(BF16))
    for p in range(PH):
        phased_ref[:, p * LANES : (p + 1) * LANES] = phases[p]
    stores = [pltpu.make_async_copy(phased_ref, phased_hbm, sems.at[2])]
    stores[0].start()
    high = PH // GROUP
    stacked = jnp.concatenate(
        [jnp.concatenate(phases[h * GROUP : (h + 1) * GROUP], axis=1) for h in range(high)], axis=0
    )
    rows, width = owner_count * high * SLOTS * BS, high * stations
    k_of, column = iota((blocks, width), 0), iota((blocks, width), 1)
    expand = jnp.where(column % stations // BS == k_of, 1.0, 0.0)
    named = lax.dot_general(
        owners_ref[...].astype(F32), expand, (((1,), (0,)), ((), ())), preferred_element_type=F32
    )
    row, col = iota((rows, width), 0), iota((rows, width), 1)
    owner = (row // (high * SLOTS * BS)).astype(F32)
    wanted = jnp.zeros((rows, width), F32)
    for d in range(dests):
        wanted = jnp.maximum(wanted, jnp.where(named[d : d + 1, :] == owner, 1.0, 0.0))
    first, second = iota((width, width), 0), iota((width, width), 1)
    earlier = (
        (first // stations == second // stations)
        & (first % stations // BS < second % stations // BS)
        & (first % BS == 0)
    )
    rank = dot(wanted.astype(BF16), jnp.where(earlier, 1.0, 0.0).astype(BF16))
    slot = (row // BS % SLOTS).astype(F32)
    right = (
        (rank == slot)
        & (row % BS == col % BS)
        & (row // (SLOTS * BS) % high == col // stations)
    )
    select = jnp.where(right, wanted, 0.0).astype(BF16)
    parts, size = 4, rows // 4
    for i in range(parts):
        at = pl.ds(i * size, size)
        slots_ref[at, :] = dot(select[i * size : (i + 1) * size], stacked).astype(BF16)
        stores.append(pltpu.make_async_copy(slots_ref.at[at, :], slots_hbm.at[at, :], sems.at[3 + i]))
        stores[-1].start()
    for store in stores:
        store.wait()


def prepare(records, owners, owner_count):
    stations, length = records.shape
    rows = owner_count * SLOTS * BS * PH // GROUP
    return pl.pallas_call(
        lambda *refs: prepare_kernel(owner_count, *refs),
        out_shape=(
            pltpu.HBM((stations, length), BF16),
            pltpu.HBM((rows, GROUP * LANES), BF16),
        ),
        in_specs=[pl.BlockSpec(memory_space=pltpu.HBM)] * 2,
        out_specs=[pl.BlockSpec(memory_space=pltpu.HBM)] * 2,
        scratch_shapes=[
            pltpu.VMEM(records.shape, records.dtype),
            pltpu.VMEM(owners.shape, owners.dtype),
            pltpu.VMEM((stations, length), BF16),
            pltpu.VMEM((rows, GROUP * LANES), BF16),
            pltpu.SemaphoreType.DMA((7,)),
        ],
        compiler_params=pltpu.CompilerParams(vmem_limit_bytes=16 * MIB),
        cost_estimate=pl.CostEstimate(
            flops=100 * MIB, bytes_accessed=2 * MIB, transcendentals=0
        ),
        name="prepare",
    )(in_hbm(records), in_hbm(owners))


def add(a, b):
    return a[0] + b[0], a[1] + b[1]


def sub(a, b):
    return a[0] - b[0], a[1] - b[1]


def times_i(a, sign):
    return (-a[1], a[0]) if sign > 0 else (a[1], -a[0])


def times(a, b):
    return a[0] * b[0] - a[1] * b[1], a[0] * b[1] + a[1] * b[0]


def unit(a, k, sign):
    k %= 16
    if k == 0:
        return a
    if k == 4:
        return times_i(a, sign)
    if k == 8:
        return -a[0], -a[1]
    if k == 12:
        return times_i(a, -sign)
    angle = 2.0 * math.pi * k / 16
    return times(a, (math.cos(angle), sign * math.sin(angle)))


def four(a, sign):
    s, d = add(a[0], a[2]), sub(a[0], a[2])
    t, e = add(a[1], a[3]), times_i(sub(a[1], a[3]), sign)
    return [add(s, t), add(d, e), sub(s, t), sub(d, e)]


def forward_sixteen(v):
    inner = [four([v[4 * p1 + p0] for p1 in range(4)], 1) for p0 in range(4)]
    out = [None] * 8
    for fa in range(4):
        u = [unit(inner[p0][fa], p0 * fa, 1) for p0 in range(4)]
        s, t = add(u[0], u[2]), add(u[1], u[3])
        out[fa] = add(s, t)
        out[fa + 4] = add(sub(u[0], u[2]), times_i(sub(u[1], u[3]), 1))
        if fa == 0:
            last = s[0] - t[0]
    return out, last


def inverse_sixteen(f):
    out = [None] * 16
    for p0 in range(4):
        inner = []
        for fa in range(4):
            turned = unit(f[fa + 4], 4 * p0, -1)
            inner.append(unit(add(f[fa], turned), p0 * fa, -1))
        for p1, value in enumerate(four(inner, -1)):
            out[4 * p1 + p0] = value
    return out


def seg_total(values, segs):
    rows = values.shape[0] // segs
    total = values[:rows]
    for s in range(1, segs):
        total = total + values[s * rows : (s + 1) * rows]
    return total


def whiten(x_ref, y_ref, f_ref, sum_ref, trace_ref, segs):
    rows = x_ref.shape[1]
    length = PH * LANES
    window = length * segs
    half = PH // 2
    n, k = iota((LANES, LANES), 0), iota((LANES, LANES), 1)
    cosine, sine = cos_sin(n * k, LANES)
    table = jnp.concatenate([cosine, sine], axis=1).astype(BF16)
    folded = FINE // PH * (k % (LANES // 2)) + k // (LANES // 2)
    back = jnp.concatenate(cos_sin(n * folded, LANES), axis=0).astype(BF16)
    turn_cos, turn_sin = cos_sin(iota((PH, LANES), 0) * iota((PH, LANES), 1), length)
    for p in range(PH):
        y_ref[p] = dot(x_ref[p], table)
    lane = iota((8, LANES), 1)

    def forward(i, _):
        at = pl.ds(pl.multiple_of(i * 8, 8), 8)
        v = []
        for p in range(PH):
            y = y_ref[p, at, :LANES], y_ref[p, at, LANES:]
            v.append(times(y, (turn_cos[p : p + 1], turn_sin[p : p + 1])) if p else y)
        out, last = forward_sixteen(v)
        total = None
        for j, (re, im) in enumerate(out):
            if j == 0:
                mag = jnp.where(lane == 0, jnp.abs(re), jnp.sqrt(re * re + im * im))
                im = jnp.where(lane == 0, last, im)
                total = jnp.where(lane == 0, 0.5 * (jnp.abs(re) + jnp.abs(im)), mag)
            else:
                mag = jnp.sqrt(re * re + im * im)
                total = total + mag
            f_ref[j, at, :] = re
            f_ref[half + j, at, :] = im
            f_ref[2 * half + j, at, :] = mag
        sum_ref[at, :] = total
        return 0

    lax.fori_loop(0, rows // 8, forward, 0, unroll=4)
    amp = 2.0 * jnp.sum(seg_total(sum_ref[...], segs), axis=1, keepdims=True)
    level = WATER * amp / window + EPSILON
    sum_ref[...] = jnp.concatenate(
        [jnp.broadcast_to(level, (rows // segs, LANES))] * segs, axis=0
    )

    def inverse(i, _):
        at = pl.ds(pl.multiple_of(i * 8, 8), 8)
        level = sum_ref[at, :]
        f = []
        for j in range(half):
            re, im, mag = f_ref[j, at, :], f_ref[half + j, at, :], f_ref[2 * half + j, at, :]
            if j == 0:
                edge = im / (jnp.abs(im) + level)
                share = 2.0 / (mag + level)
                f.append(
                    (
                        jnp.where(lane == 0, 0.5, 1.0) * (re * share),
                        jnp.where(lane == 0, 0.0, im * share),
                    )
                )
                edge = jnp.where(lane == 0, edge, 0.0)
            else:
                share = 2.0 / (mag + level)
                f.append((re * share, im * share))
        for p, z in enumerate(inverse_sixteen(f)):
            if p:
                z = times(z, (turn_cos[p : p + 1], -turn_sin[p : p + 1]))
            y_ref[p, at, :LANES] = z[0] - edge if p % 2 else z[0] + edge
            y_ref[p, at, LANES:] = z[1]
        return 0

    lax.fori_loop(0, rows // 8, inverse, 0, unroll=4)
    energy = jnp.zeros((rows, LANES), F32)
    for p in range(PH):
        trace = dot(y_ref[p].astype(BF16), back) * (1.0 / length)
        energy = energy + trace * trace
        trace_ref[p] = trace
    energy = jnp.sum(seg_total(energy, segs), axis=1, keepdims=True)
    return lax.rsqrt(energy / window + EPSILON)


def whiten_scratch(rows):
    return [
        pltpu.VMEM((PH, rows, LANES), BF16),
        pltpu.VMEM((PH, rows, 2 * LANES), F32),
        pltpu.VMEM((3 * PH // 2, rows, LANES), F32),
        pltpu.VMEM((rows, LANES), F32),
        pltpu.VMEM((PH, rows, LANES), F32),
    ]


def own_kernel(segs, me_ref, *refs):
    pairs, refs = refs[: segs // CORES], refs[segs // CORES :]
    white_ref, phase_ref, x_ref, y_ref, f_ref, sum_ref, trace_ref = refs
    rows, length = x_ref.shape[1], PH * LANES
    stations = rows // segs
    per_tile = LANES // PH
    me, chips = me_ref[0], segs // CORES
    for i, ref in enumerate(pairs):
        chip = (lax.div(me, CORES) + chips - STEPS[i]) & (chips - 1)
        for j in range(CORES):
            core = (me + j) & (CORES - 1)
            at = pl.ds(pl.multiple_of((chip * CORES + core) * stations, stations), stations)
            for p in range(PH):
                x_ref[p, at, :] = ref[
                    j * stations : (j + 1) * stations, p * LANES : (p + 1) * LANES
                ]
    scale = whiten(x_ref, y_ref, f_ref, sum_ref, trace_ref, segs)
    def put(p, s, tile):
        phase_ref[s, (FINE - 1 - p) * stations : (FINE - p) * stations, :] = tile.astype(F32)

    fold(trace_ref, scale, segs, put)
    mine = pl.ds(pl.multiple_of(me * stations, stations), stations)
    for p in range(PH):
        white_ref[:, p * LANES : (p + 1) * LANES] = (trace_ref[p, mine, :] * scale).astype(BF16)


def order_kernel(phased_ref, white_ref):
    stations, length = phased_ref.shape
    per_tile = LANES // PH
    tiles = [phased_ref[:, p * LANES : (p + 1) * LANES].astype(F32) for p in range(PH)]
    moved = []
    for t in range(length // LANES):
        turn = (LANES - per_tile // 2 * t) % LANES
        moved.append(
            jnp.concatenate(
                [(pltpu.roll(x, turn, 1) if turn else x).astype(BF16) for x in tiles], axis=1
            )
        )
    natural = dot_t(jnp.concatenate(moved, axis=0), gather_back()).astype(BF16)
    for t in range(length // LANES):
        white_ref[:, t * LANES : (t + 1) * LANES] = natural[t * stations : (t + 1) * stations]


def in_sample_order(phased):
    return pl.pallas_call(
        order_kernel,
        out_shape=jax.ShapeDtypeStruct(phased.shape, BF16),
        in_specs=[pl.BlockSpec(memory_space=pltpu.VMEM)],
        out_specs=pl.BlockSpec(memory_space=pltpu.VMEM),
        compiler_params=pltpu.CompilerParams(vmem_limit_bytes=8 * MIB),
        cost_estimate=pl.CostEstimate(flops=1000 * MIB, bytes_accessed=MIB, transcendentals=0),
        name="order",
    )(phased)


def pack_kernel(me_ref, *refs):
    near, out_ref = refs[:-1], refs[-1]
    other = 1 - (me_ref[0] & (CORES - 1))
    chip = lax.div(me_ref[0], CORES)
    for i, ref in enumerate(near):
        out_ref[i] = ref[(chip * CORES if i == 0 else 0) + other]


def pack(me, near):
    return pl.pallas_call(
        pack_kernel,
        out_shape=jax.ShapeDtypeStruct((len(near), *near[0].shape[1:]), BF16),
        in_specs=[
            pl.BlockSpec(memory_space=pltpu.SMEM),
            *[pl.BlockSpec(memory_space=pltpu.VMEM)] * len(near),
        ],
        out_specs=pl.BlockSpec(memory_space=pltpu.VMEM),
        compiler_params=pltpu.CompilerParams(vmem_limit_bytes=8 * MIB),
        cost_estimate=pl.CostEstimate(flops=0, bytes_accessed=MIB, transcendentals=0),
        name="pack",
    )(me, *near)


def own_part(me, pairs, segs):
    rows, length = len(pairs) * pairs[0].shape[0], pairs[0].shape[1]
    stations = rows // segs
    return pl.pallas_call(
        lambda *refs: own_kernel(segs, *refs),
        out_shape=(
            jax.ShapeDtypeStruct((stations, length), BF16),
            jax.ShapeDtypeStruct((segs // 2, FINE * stations, LANES), F32),
        ),
        in_specs=[
            pl.BlockSpec(memory_space=pltpu.SMEM),
            *[pl.BlockSpec(memory_space=pltpu.VMEM)] * len(pairs),
        ],
        out_specs=[pl.BlockSpec(memory_space=pltpu.VMEM)] * 2,
        scratch_shapes=whiten_scratch(rows),
        compiler_params=pltpu.CompilerParams(vmem_limit_bytes=32 * MIB),
        cost_estimate=pl.CostEstimate(
            flops=2000 * MIB, bytes_accessed=4 * MIB, transcendentals=0
        ),
        name="own",
    )(me, *pairs)


def shift_kernel(stations, phase_ref, shifted_hbm, extra_hbm, shifted_ref, extra_ref, sems):
    count = LAGS // FINE
    tiles = phase_ref.shape[0]
    lane = iota((FINE, LANES), 1)

    def copies(a):
        to = shifted_hbm.at[pl.ds(pl.multiple_of(a * LAGS, LAGS), LAGS), :]
        to_extra = extra_hbm.at[pl.ds(pl.multiple_of(a * FINE, FINE), FINE), :]
        return (
            pltpu.make_async_copy(shifted_ref.at[a], to, sems.at[0, a]),
            pltpu.make_async_copy(extra_ref.at[a], to_extra, sems.at[1, a]),
        )

    def body(a, _):
        block = [phase_ref[s, pl.ds(a, FINE, stride=stations), :] for s in range(tiles)]
        zero = jnp.zeros((FINE, LANES), F32)
        for i in range(-1, count):
            m = i + 1 - count // 2
            turned = [pltpu.roll(tile, m % LANES, 1) if m else tile for tile in block]
            for t in range(tiles):
                if m > 0:
                    moved = jnp.where(lane >= m, turned[t], turned[t - 1] if t else zero)
                elif m < 0:
                    later = turned[t + 1] if t + 1 < tiles else zero
                    moved = jnp.where(lane < LANES + m, turned[t], later)
                else:
                    moved = turned[t]
                cols = slice(t * LANES, (t + 1) * LANES)
                if i < 0:
                    extra_ref[a, :, cols] = moved.astype(BF16)
                else:
                    shifted_ref[a, i * FINE : (i + 1) * FINE, cols] = moved.astype(BF16)
        for copy in copies(a):
            copy.start()
        return 0

    lax.fori_loop(0, stations, body, 0, unroll=4)

    def finish(a, _):
        for copy in copies(a):
            copy.wait()
        return 0

    lax.fori_loop(0, stations, finish, 0)


def shift(phases):
    stations = phases.shape[1] // FINE
    total = phases.shape[0] * LANES
    return pl.pallas_call(
        lambda *refs: shift_kernel(stations, *refs),
        out_shape=(
            pltpu.HBM((stations * LAGS, total), BF16),
            pltpu.HBM((stations * FINE, total), BF16),
        ),
        in_specs=[pl.BlockSpec(memory_space=pltpu.VMEM)],
        out_specs=[pl.BlockSpec(memory_space=pltpu.HBM)] * 2,
        scratch_shapes=[
            pltpu.VMEM((stations, LAGS, total), BF16),
            pltpu.VMEM((stations, FINE, total), BF16),
            pltpu.SemaphoreType.DMA((2, stations)),
        ],
        compiler_params=pltpu.CompilerParams(vmem_limit_bytes=16 * MIB),
        cost_estimate=pl.CostEstimate(
            flops=1, bytes_accessed=9 * MIB, transcendentals=0
        ),
        name="shift",
    )(phases)


def correlate_kernel(segs, me_ref, *refs):
    chips = segs // CORES
    near, (far_ref, shifted_hbm, extra_hbm, out_ref), refs = (
        refs[:chips],
        refs[chips : chips + 4],
        refs[chips + 4 :],
    )
    x_ref, y_ref, f_ref, sum_ref, trace_ref, phase_ref, edge_ref, total_ref = refs[:8]
    shifted_ref, extra_ref, even_ref, odd_ref, sems = refs[8:]
    rows = x_ref.shape[1]
    received = rows // segs
    stations = shifted_ref.shape[0]
    copies = [pltpu.make_async_copy(extra_hbm, extra_ref, sems.at[stations])]
    for a in range(stations):
        block = shifted_hbm.at[pl.ds(a * LAGS, LAGS), :]
        copies.append(pltpu.make_async_copy(block, shifted_ref.at[a], sems.at[a]))
    for copy in copies:
        copy.start()
    high, unit_rows = PH // GROUP, SLOTS * BS
    per_seg = high * received
    to, at_row = iota((per_seg, per_seg), 0), iota((per_seg, per_seg), 1)
    wanted = (
        to % received // unit_rows * (high * unit_rows) + to // received * unit_rows
    ) + to % unit_rows
    order = jnp.where(at_row == wanted, 1.0, 0.0).astype(BF16)
    me = me_ref[0]
    mine = me & (CORES - 1)
    for s in range(segs):
        i = s // CORES
        chip = (lax.div(me, CORES) + chips - STEPS[i]) & (chips - 1)
        if s % CORES:
            source, seg = far_ref[i], chip * CORES + 1 - mine
        else:
            source = near[i][(chip * CORES if i == 0 else 0) + mine]
            seg = chip * CORES + mine
        block = dot(order, source).astype(BF16)
        at = pl.ds(pl.multiple_of(seg * received, received), received)
        for p in range(PH):
            x_ref[p, at, :] = block[
                p // GROUP * received : (p // GROUP + 1) * received,
                p % GROUP * LANES : (p % GROUP + 1) * LANES,
            ]
    scale = whiten(x_ref, y_ref, f_ref, sum_ref, trace_ref, segs)

    def put(p, s, tile):
        phase_ref[p * received : (p + 1) * received, s * LANES : (s + 1) * LANES] = tile

    fold(trace_ref, scale, segs, put)
    for copy in copies:
        copy.wait()
    edge = dot_t(phase_ref[...], extra_ref[...])
    width = stations * FINE
    lag = iota((received, width), 1) % FINE
    sums = jnp.zeros((received, width), F32)
    for p in range(FINE):
        block = edge[p * received : (p + 1) * received]
        turn = (p + 1 - FINE) % width
        block = pltpu.roll(block, turn, 1) if turn else block
        sums = sums + jnp.where(lag <= p, block, 0.0)
    edge_ref[...] = sums
    lane = iota((received, LAGS), 1)
    norm = 1.0 / math.sqrt(segs * PH * LANES)

    def multiply(a):
        return dot_t(phase_ref[...], shifted_ref[a])

    def combine(a, product_ref):
        first = pltpu.roll(edge_ref[...], (stations - a) * FINE, 1)
        sums = jnp.where(lane < FINE, first[:, :LAGS], 0.0)
        for p in range(FINE):
            block = pltpu.roll(product_ref[p * received : (p + 1) * received], p + 1, 1)
            sums = sums + jnp.where(lane > p, block, 0.0)
        sums = sums * norm
        for c in range(LAGS // LANES):
            total_ref[c, pl.ds(a, received, stride=stations), :] = sums[
                :, c * LANES : (c + 1) * LANES
            ]

    even_ref[...] = multiply(0)

    def body(i, _):
        odd_ref[...] = multiply(2 * i + 1)
        combine(2 * i, even_ref)
        even_ref[...] = multiply(2 * i + 2)
        combine(2 * i + 1, odd_ref)
        return 0

    lax.fori_loop(0, stations // 2 - 1, body, 0)
    odd_ref[...] = multiply(stations - 1)
    combine(stations - 2, even_ref)
    combine(stations - 1, odd_ref)
    for c in range(LAGS // LANES):
        out_ref[:, c * LANES : (c + 1) * LANES] = total_ref[c].astype(BF16)


def correlate(me, near, far, shifted, extra, segs):
    rows = segs * far.shape[1] // (PH // GROUP)
    count = rows // segs
    stations = shifted.shape[0] // LAGS
    total = shifted.shape[1]
    return pl.pallas_call(
        lambda *refs: correlate_kernel(segs, *refs),
        out_shape=jax.ShapeDtypeStruct((count * stations, LAGS), BF16),
        in_specs=[
            pl.BlockSpec(memory_space=pltpu.SMEM),
            *[pl.BlockSpec(memory_space=pltpu.VMEM)] * (len(near) + 1),
            pl.BlockSpec(memory_space=pltpu.HBM),
            pl.BlockSpec(memory_space=pltpu.HBM),
        ],
        out_specs=pl.BlockSpec(memory_space=pltpu.VMEM),
        scratch_shapes=[
            *whiten_scratch(rows),
            pltpu.VMEM((count * FINE, total), BF16),
            pltpu.VMEM((count, stations * FINE), F32),
            pltpu.VMEM((LAGS // LANES, count * stations, LANES), F32),
            pltpu.VMEM((stations, LAGS, total), BF16),
            pltpu.VMEM((stations * FINE, total), BF16),
            pltpu.VMEM((count * FINE, LAGS), F32),
            pltpu.VMEM((count * FINE, LAGS), F32),
            pltpu.SemaphoreType.DMA((stations + 1,)),
        ],
        compiler_params=pltpu.CompilerParams(vmem_limit_bytes=48 * MIB),
        cost_estimate=pl.CostEstimate(
            flops=6000 * MIB, bytes_accessed=20 * MIB, transcendentals=0
        ),
        name="correlate",
    )(
        me,
        *near,
        far,
        in_hbm(shifted),
        in_hbm(extra),
    )


def on_device(records, owners):
    stations, length = records.shape
    segs, sources = lax.axis_size("seg"), lax.axis_size("sta")
    chips = segs // CORES
    me = lax.axis_index("seg")
    chip = lax.div(me, jnp.int32(CORES))
    along_x = [[(i, (i + k * CORES) % segs) for i in range(segs)] for k in range(chips)]
    across = [(i, i ^ 1) for i in range(segs)]
    phased, slots = prepare(records, owners.T, sources)
    slots = slots.reshape(sources, -1, GROUP * LANES)
    passing = lax.all_to_all(slots, "sta", 0, 0, tiled=True)
    passing = passing.reshape(segs, -1, GROUP * LANES)
    other = lax.ppermute(phased, "seg", across)
    pair = jnp.concatenate([phased, other], axis=0)
    pairs = [pair] + [lax.ppermute(pair, "seg", along_x[k]) for k in STEPS[1:]]
    mine, phases = own_part(me.reshape(1), pairs, segs)
    passing, phases = lax.optimization_barrier((passing, phases))
    shifted, extra = shift(phases)
    near = [passing]
    for k in STEPS[1:]:
        at = ((chip + k) & (chips - 1)) * CORES
        block = lax.dynamic_slice_in_dim(passing, at, CORES, 0)
        near.append(lax.ppermute(block, "seg", along_x[k]))
    near, shifted, extra, mine = lax.optimization_barrier((near, shifted, extra, mine))
    far = lax.ppermute(pack(me.reshape(1), near), "seg", across)
    whitened = in_sample_order(mine)
    result = correlate(me.reshape(1), near, far, shifted, extra, segs)
    return whitened, result.reshape(-1, stations, LAGS)


def solution(mesh):
    return jax.shard_map(
        on_device,
        mesh=mesh,
        in_specs=(P("sta", "seg"), P("sta", None)),
        out_specs=(P("sta", "seg"), P("seg", "sta", None)),
        check_vma=False,
    )
```

```python
import math

import jax
import jax.numpy as jnp
from jax import lax
from jax.experimental import pallas as pl
from jax.experimental.pallas import tpu as pltpu
from jax.sharding import PartitionSpec as P

LAGS = 512
BS = 2
SLOTS = 2
WATER = 0.5
EPSILON = 1e-06

PH = 16
LANES = 128
STEPS = (0, 2, 3, 1)
FINE = 32
CORES = 2
GROUP = 4
F32 = jnp.float32
BF16 = jnp.bfloat16
MIB = 1 << 20


def dot(a, b):
    return lax.dot_general(a, b, (((1,), (0,)), ((), ())), preferred_element_type=F32)


def dot_t(a, b):
    return lax.dot_general(a, b, (((1,), (1,)), ((), ())), preferred_element_type=F32)


def in_hbm(x):
    return pltpu.with_memory_space_constraint(x, pltpu.HBM)


def iota(shape, axis):
    return lax.broadcasted_iota(jnp.int32, shape, axis)


def cos_sin(phase, period):
    phase = phase & (period - 1)
    phase = jnp.where(phase >= period // 2, phase - period, phase)
    theta = phase.astype(F32) * (2.0 * math.pi / period)
    square = theta * theta
    cosine = jnp.full(theta.shape, 1.0 / math.factorial(20), F32)
    sine = jnp.full(theta.shape, 1.0 / math.factorial(21), F32)
    for n in range(9, -1, -1):
        cosine = (1.0 if n % 2 == 0 else -1.0) / math.factorial(2 * n) + square * cosine
        sine = (1.0 if n % 2 == 0 else -1.0) / math.factorial(2 * n + 1) + square * sine
    return cosine, sine * theta


def spread():
    shape = (LANES, PH * LANES)
    source, target = iota(shape, 0), iota(shape, 1)
    hit = (target // LANES == source % PH) & (target % LANES == source // PH)
    return jnp.where(hit, 1.0, 0.0).astype(BF16)


def gather_back():
    shape = (LANES, PH * LANES)
    target, source = iota(shape, 0), iota(shape, 1)
    lane = source % LANES
    place = FINE // PH * (lane % (LANES // 2)) + lane // (LANES // 2)
    hit = (source // LANES == target % PH) & (place == target // PH)
    return jnp.where(hit, 1.0, 0.0).astype(BF16)


def fold(trace_ref, scale, segs, put):
    rows = trace_ref.shape[1] // segs
    low = iota((rows, LANES), 1) < LANES // 2
    for p in range(PH):
        for s in range(segs // 2):
            first = trace_ref[p, 2 * s * rows : (2 * s + 1) * rows, :] * scale
            second = trace_ref[p, (2 * s + 1) * rows : (2 * s + 2) * rows, :] * scale
            put(p, s, jnp.where(low, first, pltpu.roll(second, LANES // 2, 1)).astype(BF16))
            put(p + PH, s, jnp.where(low, pltpu.roll(first, LANES // 2, 1), second).astype(BF16))


def prepare_kernel(
    owner_count, records_hbm, owners_hbm, phased_hbm, slots_hbm,
    records_ref, owners_ref, phased_ref, slots_ref, sems,
):
    loads = [
        pltpu.make_async_copy(records_hbm, records_ref, sems.at[0]),
        pltpu.make_async_copy(owners_hbm, owners_ref, sems.at[1]),
    ]
    for load in loads:
        load.start()
    stations, length = records_ref.shape
    dests, blocks = owners_ref.shape
    per_tile = LANES // PH
    one_hot = spread()
    for load in loads:
        load.wait()
    tiles = jnp.concatenate(
        [records_ref[:, t * LANES : (t + 1) * LANES] for t in range(length // LANES)], axis=0
    )
    parts = dot(tiles, one_hot)
    phases = []
    for p in range(PH):
        total = None
        for t in range(length // LANES):
            part = parts[t * stations : (t + 1) * stations, p * LANES : (p + 1) * LANES]
            part = pltpu.roll(part, per_tile * t, 1) if t else part
            total = part if total is None else total + part
        phases.append(total.astype(BF16))
    for p in range(PH):
        phased_ref[:, p * LANES : (p + 1) * LANES] = phases[p]
    stores = [pltpu.make_async_copy(phased_ref, phased_hbm, sems.at[2])]
    stores[0].start()
    high = PH // GROUP
    stacked = jnp.concatenate(
        [jnp.concatenate(phases[h * GROUP : (h + 1) * GROUP], axis=1) for h in range(high)], axis=0
    )
    rows, width = owner_count * high * SLOTS * BS, high * stations
    k_of, column = iota((blocks, width), 0), iota((blocks, width), 1)
    expand = jnp.where(column % stations // BS == k_of, 1.0, 0.0)
    named = lax.dot_general(
        owners_ref[...].astype(F32), expand, (((1,), (0,)), ((), ())), preferred_element_type=F32
    )
    row, col = iota((rows, width), 0), iota((rows, width), 1)
    owner = (row // (high * SLOTS * BS)).astype(F32)
    wanted = jnp.zeros((rows, width), F32)
    for d in range(dests):
        wanted = jnp.maximum(wanted, jnp.where(named[d : d + 1, :] == owner, 1.0, 0.0))
    first, second = iota((width, width), 0), iota((width, width), 1)
    earlier = (
        (first // stations == second // stations)
        & (first % stations // BS < second % stations // BS)
        & (first % BS == 0)
    )
    rank = dot(wanted.astype(BF16), jnp.where(earlier, 1.0, 0.0).astype(BF16))
    slot = (row // BS % SLOTS).astype(F32)
    right = (
        (rank == slot)
        & (row % BS == col % BS)
        & (row // (SLOTS * BS) % high == col // stations)
    )
    select = jnp.where(right, wanted, 0.0).astype(BF16)
    parts, size = 4, rows // 4
    for i in range(parts):
        at = pl.ds(i * size, size)
        slots_ref[at, :] = dot(select[i * size : (i + 1) * size], stacked).astype(BF16)
        stores.append(pltpu.make_async_copy(slots_ref.at[at, :], slots_hbm.at[at, :], sems.at[3 + i]))
        stores[-1].start()
    for store in stores:
        store.wait()


def prepare(records, owners, owner_count):
    stations, length = records.shape
    rows = owner_count * SLOTS * BS * PH // GROUP
    return pl.pallas_call(
        lambda *refs: prepare_kernel(owner_count, *refs),
        out_shape=(
            pltpu.HBM((stations, length), BF16),
            pltpu.HBM((rows, GROUP * LANES), BF16),
        ),
        in_specs=[pl.BlockSpec(memory_space=pltpu.HBM)] * 2,
        out_specs=[pl.BlockSpec(memory_space=pltpu.HBM)] * 2,
        scratch_shapes=[
            pltpu.VMEM(records.shape, records.dtype),
            pltpu.VMEM(owners.shape, owners.dtype),
            pltpu.VMEM((stations, length), BF16),
            pltpu.VMEM((rows, GROUP * LANES), BF16),
            pltpu.SemaphoreType.DMA((7,)),
        ],
        compiler_params=pltpu.CompilerParams(vmem_limit_bytes=16 * MIB),
        cost_estimate=pl.CostEstimate(
            flops=100 * MIB, bytes_accessed=2 * MIB, transcendentals=0
        ),
        name="prepare",
    )(in_hbm(records), in_hbm(owners))


def add(a, b):
    return a[0] + b[0], a[1] + b[1]


def sub(a, b):
    return a[0] - b[0], a[1] - b[1]


def times_i(a, sign):
    return (-a[1], a[0]) if sign > 0 else (a[1], -a[0])


def times(a, b):
    return a[0] * b[0] - a[1] * b[1], a[0] * b[1] + a[1] * b[0]


def unit(a, k, sign):
    k %= 16
    if k == 0:
        return a
    if k == 4:
        return times_i(a, sign)
    if k == 8:
        return -a[0], -a[1]
    if k == 12:
        return times_i(a, -sign)
    angle = 2.0 * math.pi * k / 16
    return times(a, (math.cos(angle), sign * math.sin(angle)))


def four(a, sign):
    s, d = add(a[0], a[2]), sub(a[0], a[2])
    t, e = add(a[1], a[3]), times_i(sub(a[1], a[3]), sign)
    return [add(s, t), add(d, e), sub(s, t), sub(d, e)]


def forward_sixteen(v):
    inner = [four([v[4 * p1 + p0] for p1 in range(4)], 1) for p0 in range(4)]
    out = [None] * 8
    for fa in range(4):
        u = [unit(inner[p0][fa], p0 * fa, 1) for p0 in range(4)]
        s, t = add(u[0], u[2]), add(u[1], u[3])
        out[fa] = add(s, t)
        out[fa + 4] = add(sub(u[0], u[2]), times_i(sub(u[1], u[3]), 1))
        if fa == 0:
            last = s[0] - t[0]
    return out, last


def inverse_sixteen(f):
    out = [None] * 16
    for p0 in range(4):
        inner = []
        for fa in range(4):
            turned = unit(f[fa + 4], 4 * p0, -1)
            inner.append(unit(add(f[fa], turned), p0 * fa, -1))
        for p1, value in enumerate(four(inner, -1)):
            out[4 * p1 + p0] = value
    return out


def seg_total(values, segs):
    rows = values.shape[0] // segs
    total = values[:rows]
    for s in range(1, segs):
        total = total + values[s * rows : (s + 1) * rows]
    return total


def whiten(x_ref, y_ref, f_ref, sum_ref, trace_ref, segs):
    rows = x_ref.shape[1]
    length = PH * LANES
    window = length * segs
    half = PH // 2
    n, k = iota((LANES, LANES), 0), iota((LANES, LANES), 1)
    cosine, sine = cos_sin(n * k, LANES)
    table = jnp.concatenate([cosine, sine], axis=1).astype(BF16)
    folded = FINE // PH * (k % (LANES // 2)) + k // (LANES // 2)
    back = jnp.concatenate(cos_sin(n * folded, LANES), axis=0).astype(BF16)
    turn_cos, turn_sin = cos_sin(iota((PH, LANES), 0) * iota((PH, LANES), 1), length)
    for p in range(PH):
        y_ref[p] = dot(x_ref[p], table)
    lane = iota((8, LANES), 1)

    def forward(i, _):
        at = pl.ds(pl.multiple_of(i * 8, 8), 8)
        v = []
        for p in range(PH):
            y = y_ref[p, at, :LANES], y_ref[p, at, LANES:]
            v.append(times(y, (turn_cos[p : p + 1], turn_sin[p : p + 1])) if p else y)
        out, last = forward_sixteen(v)
        total = None
        for j, (re, im) in enumerate(out):
            if j == 0:
                mag = jnp.where(lane == 0, jnp.abs(re), jnp.sqrt(re * re + im * im))
                im = jnp.where(lane == 0, last, im)
                total = jnp.where(lane == 0, 0.5 * (jnp.abs(re) + jnp.abs(im)), mag)
            else:
                mag = jnp.sqrt(re * re + im * im)
                total = total + mag
            f_ref[j, at, :] = re
            f_ref[half + j, at, :] = im
            f_ref[2 * half + j, at, :] = mag
        sum_ref[at, :] = total
        return 0

    lax.fori_loop(0, rows // 8, forward, 0, unroll=4)
    amp = 2.0 * jnp.sum(seg_total(sum_ref[...], segs), axis=1, keepdims=True)
    level = WATER * amp / window + EPSILON
    sum_ref[...] = jnp.concatenate(
        [jnp.broadcast_to(level, (rows // segs, LANES))] * segs, axis=0
    )

    def inverse(i, _):
        at = pl.ds(pl.multiple_of(i * 8, 8), 8)
        level = sum_ref[at, :]
        f = []
        for j in range(half):
            re, im, mag = f_ref[j, at, :], f_ref[half + j, at, :], f_ref[2 * half + j, at, :]
            if j == 0:
                edge = im / (jnp.abs(im) + level)
                share = 2.0 / (mag + level)
                f.append(
                    (
                        jnp.where(lane == 0, 0.5, 1.0) * (re * share),
                        jnp.where(lane == 0, 0.0, im * share),
                    )
                )
                edge = jnp.where(lane == 0, edge, 0.0)
            else:
                share = 2.0 / (mag + level)
                f.append((re * share, im * share))
        for p, z in enumerate(inverse_sixteen(f)):
            if p:
                z = times(z, (turn_cos[p : p + 1], -turn_sin[p : p + 1]))
            y_ref[p, at, :LANES] = z[0] - edge if p % 2 else z[0] + edge
            y_ref[p, at, LANES:] = z[1]
        return 0

    lax.fori_loop(0, rows // 8, inverse, 0, unroll=4)
    energy = jnp.zeros((rows, LANES), F32)
    for p in range(PH):
        trace = dot(y_ref[p].astype(BF16), back) * (1.0 / length)
        energy = energy + trace * trace
        trace_ref[p] = trace
    energy = jnp.sum(seg_total(energy, segs), axis=1, keepdims=True)
    return lax.rsqrt(energy / window + EPSILON)


def whiten_scratch(rows):
    return [
        pltpu.VMEM((PH, rows, LANES), BF16),
        pltpu.VMEM((PH, rows, 2 * LANES), F32),
        pltpu.VMEM((3 * PH // 2, rows, LANES), F32),
        pltpu.VMEM((rows, LANES), F32),
        pltpu.VMEM((PH, rows, LANES), F32),
    ]


def own_kernel(segs, me_ref, *refs):
    pairs, refs = refs[: segs // CORES], refs[segs // CORES :]
    white_ref, phase_ref, x_ref, y_ref, f_ref, sum_ref, trace_ref = refs
    rows, length = x_ref.shape[1], PH * LANES
    stations = rows // segs
    per_tile = LANES // PH
    me, chips = me_ref[0], segs // CORES
    for i, ref in enumerate(pairs):
        chip = (lax.div(me, CORES) + chips - STEPS[i]) & (chips - 1)
        for j in range(CORES):
            core = (me + j) & (CORES - 1)
            at = pl.ds(pl.multiple_of((chip * CORES + core) * stations, stations), stations)
            for p in range(PH):
                x_ref[p, at, :] = ref[
                    j * stations : (j + 1) * stations, p * LANES : (p + 1) * LANES
                ]
    scale = whiten(x_ref, y_ref, f_ref, sum_ref, trace_ref, segs)
    def put(p, s, tile):
        phase_ref[s, (FINE - 1 - p) * stations : (FINE - p) * stations, :] = tile.astype(F32)

    fold(trace_ref, scale, segs, put)
    mine = pl.ds(pl.multiple_of(me * stations, stations), stations)
    for p in range(PH):
        white_ref[:, p * LANES : (p + 1) * LANES] = (trace_ref[p, mine, :] * scale).astype(BF16)


def order_kernel(phased_ref, white_ref):
    stations, length = phased_ref.shape
    per_tile = LANES // PH
    tiles = [phased_ref[:, p * LANES : (p + 1) * LANES].astype(F32) for p in range(PH)]
    moved = []
    for t in range(length // LANES):
        turn = (LANES - per_tile // 2 * t) % LANES
        moved.append(
            jnp.concatenate(
                [(pltpu.roll(x, turn, 1) if turn else x).astype(BF16) for x in tiles], axis=1
            )
        )
    natural = dot_t(jnp.concatenate(moved, axis=0), gather_back()).astype(BF16)
    for t in range(length // LANES):
        white_ref[:, t * LANES : (t + 1) * LANES] = natural[t * stations : (t + 1) * stations]


def in_sample_order(phased):
    return pl.pallas_call(
        order_kernel,
        out_shape=jax.ShapeDtypeStruct(phased.shape, BF16),
        in_specs=[pl.BlockSpec(memory_space=pltpu.VMEM)],
        out_specs=pl.BlockSpec(memory_space=pltpu.VMEM),
        compiler_params=pltpu.CompilerParams(vmem_limit_bytes=8 * MIB),
        cost_estimate=pl.CostEstimate(flops=1000 * MIB, bytes_accessed=MIB, transcendentals=0),
        name="order",
    )(phased)


def pack_kernel(me_ref, *refs):
    near, out_ref = refs[:-1], refs[-1]
    other = 1 - (me_ref[0] & (CORES - 1))
    chip = lax.div(me_ref[0], CORES)
    for i, ref in enumerate(near):
        out_ref[i] = ref[(chip * CORES if i == 0 else 0) + other]


def pack(me, near):
    return pl.pallas_call(
        pack_kernel,
        out_shape=jax.ShapeDtypeStruct((len(near), *near[0].shape[1:]), BF16),
        in_specs=[
            pl.BlockSpec(memory_space=pltpu.SMEM),
            *[pl.BlockSpec(memory_space=pltpu.VMEM)] * len(near),
        ],
        out_specs=pl.BlockSpec(memory_space=pltpu.VMEM),
        compiler_params=pltpu.CompilerParams(vmem_limit_bytes=8 * MIB),
        cost_estimate=pl.CostEstimate(flops=0, bytes_accessed=MIB, transcendentals=0),
        name="pack",
    )(me, *near)


def own_part(me, pairs, segs):
    rows, length = len(pairs) * pairs[0].shape[0], pairs[0].shape[1]
    stations = rows // segs
    return pl.pallas_call(
        lambda *refs: own_kernel(segs, *refs),
        out_shape=(
            jax.ShapeDtypeStruct((stations, length), BF16),
            jax.ShapeDtypeStruct((segs // 2, FINE * stations, LANES), F32),
        ),
        in_specs=[
            pl.BlockSpec(memory_space=pltpu.SMEM),
            *[pl.BlockSpec(memory_space=pltpu.VMEM)] * len(pairs),
        ],
        out_specs=[pl.BlockSpec(memory_space=pltpu.VMEM)] * 2,
        scratch_shapes=whiten_scratch(rows),
        compiler_params=pltpu.CompilerParams(vmem_limit_bytes=32 * MIB),
        cost_estimate=pl.CostEstimate(
            flops=2000 * MIB, bytes_accessed=4 * MIB, transcendentals=0
        ),
        name="own",
    )(me, *pairs)


def shift_kernel(stations, phase_ref, shifted_hbm, extra_hbm, shifted_ref, extra_ref, sems):
    count = LAGS // FINE
    tiles = phase_ref.shape[0]
    lane = iota((FINE, LANES), 1)

    def copies(a):
        to = shifted_hbm.at[pl.ds(pl.multiple_of(a * LAGS, LAGS), LAGS), :]
        to_extra = extra_hbm.at[pl.ds(pl.multiple_of(a * FINE, FINE), FINE), :]
        return (
            pltpu.make_async_copy(shifted_ref.at[a], to, sems.at[0, a]),
            pltpu.make_async_copy(extra_ref.at[a], to_extra, sems.at[1, a]),
        )

    def body(a, _):
        block = [phase_ref[s, pl.ds(a, FINE, stride=stations), :] for s in range(tiles)]
        zero = jnp.zeros((FINE, LANES), F32)
        for i in range(-1, count):
            m = i + 1 - count // 2
            turned = [pltpu.roll(tile, m % LANES, 1) if m else tile for tile in block]
            for t in range(tiles):
                if m > 0:
                    moved = jnp.where(lane >= m, turned[t], turned[t - 1] if t else zero)
                elif m < 0:
                    later = turned[t + 1] if t + 1 < tiles else zero
                    moved = jnp.where(lane < LANES + m, turned[t], later)
                else:
                    moved = turned[t]
                cols = slice(t * LANES, (t + 1) * LANES)
                if i < 0:
                    extra_ref[a, :, cols] = moved.astype(BF16)
                else:
                    shifted_ref[a, i * FINE : (i + 1) * FINE, cols] = moved.astype(BF16)
        for copy in copies(a):
            copy.start()
        return 0

    lax.fori_loop(0, stations, body, 0, unroll=4)

    def finish(a, _):
        for copy in copies(a):
            copy.wait()
        return 0

    lax.fori_loop(0, stations, finish, 0)


def shift(phases):
    stations = phases.shape[1] // FINE
    total = phases.shape[0] * LANES
    return pl.pallas_call(
        lambda *refs: shift_kernel(stations, *refs),
        out_shape=(
            pltpu.HBM((stations * LAGS, total), BF16),
            pltpu.HBM((stations * FINE, total), BF16),
        ),
        in_specs=[pl.BlockSpec(memory_space=pltpu.VMEM)],
        out_specs=[pl.BlockSpec(memory_space=pltpu.HBM)] * 2,
        scratch_shapes=[
            pltpu.VMEM((stations, LAGS, total), BF16),
            pltpu.VMEM((stations, FINE, total), BF16),
            pltpu.SemaphoreType.DMA((2, stations)),
        ],
        compiler_params=pltpu.CompilerParams(vmem_limit_bytes=16 * MIB),
        cost_estimate=pl.CostEstimate(
            flops=1, bytes_accessed=9 * MIB, transcendentals=0
        ),
        name="shift",
    )(phases)


def correlate_kernel(segs, me_ref, *refs):
    chips = segs // CORES
    near, (far_ref, shifted_hbm, extra_hbm, out_ref), refs = (
        refs[:chips],
        refs[chips : chips + 4],
        refs[chips + 4 :],
    )
    x_ref, y_ref, f_ref, sum_ref, trace_ref, phase_ref, edge_ref, total_ref = refs[:8]
    shifted_ref, extra_ref, even_ref, odd_ref, sems = refs[8:]
    rows = x_ref.shape[1]
    received = rows // segs
    stations = shifted_ref.shape[0]
    copies = [pltpu.make_async_copy(extra_hbm, extra_ref, sems.at[stations])]
    for a in range(stations):
        block = shifted_hbm.at[pl.ds(a * LAGS, LAGS), :]
        copies.append(pltpu.make_async_copy(block, shifted_ref.at[a], sems.at[a]))
    for copy in copies:
        copy.start()
    high, unit_rows = PH // GROUP, SLOTS * BS
    per_seg = high * received
    to, at_row = iota((per_seg, per_seg), 0), iota((per_seg, per_seg), 1)
    wanted = (
        to % received // unit_rows * (high * unit_rows) + to // received * unit_rows
    ) + to % unit_rows
    order = jnp.where(at_row == wanted, 1.0, 0.0).astype(BF16)
    me = me_ref[0]
    mine = me & (CORES - 1)
    for s in range(segs):
        i = s // CORES
        chip = (lax.div(me, CORES) + chips - STEPS[i]) & (chips - 1)
        if s % CORES:
            source, seg = far_ref[i], chip * CORES + 1 - mine
        else:
            source = near[i][(chip * CORES if i == 0 else 0) + mine]
            seg = chip * CORES + mine
        block = dot(order, source).astype(BF16)
        at = pl.ds(pl.multiple_of(seg * received, received), received)
        for p in range(PH):
            x_ref[p, at, :] = block[
                p // GROUP * received : (p // GROUP + 1) * received,
                p % GROUP * LANES : (p % GROUP + 1) * LANES,
            ]
    scale = whiten(x_ref, y_ref, f_ref, sum_ref, trace_ref, segs)

    def put(p, s, tile):
        phase_ref[p * received : (p + 1) * received, s * LANES : (s + 1) * LANES] = tile

    fold(trace_ref, scale, segs, put)
    for copy in copies:
        copy.wait()
    edge = dot_t(phase_ref[...], extra_ref[...])
    width = stations * FINE
    lag = iota((received, width), 1) % FINE
    sums = jnp.zeros((received, width), F32)
    for p in range(FINE):
        block = edge[p * received : (p + 1) * received]
        turn = (p + 1 - FINE) % width
        block = pltpu.roll(block, turn, 1) if turn else block
        sums = sums + jnp.where(lag <= p, block, 0.0)
    edge_ref[...] = sums
    lane = iota((received, LAGS), 1)
    norm = 1.0 / math.sqrt(segs * PH * LANES)

    def multiply(a):
        return dot_t(phase_ref[...], shifted_ref[a])

    def combine(a, product_ref):
        first = pltpu.roll(edge_ref[...], (stations - a) * FINE, 1)
        sums = jnp.where(lane < FINE, first[:, :LAGS], 0.0)
        for p in range(FINE):
            block = pltpu.roll(product_ref[p * received : (p + 1) * received], p + 1, 1)
            sums = sums + jnp.where(lane > p, block, 0.0)
        sums = sums * norm
        for c in range(LAGS // LANES):
            total_ref[c, pl.ds(a, received, stride=stations), :] = sums[
                :, c * LANES : (c + 1) * LANES
            ]

    even_ref[...] = multiply(0)

    def body(i, _):
        odd_ref[...] = multiply(2 * i + 1)
        combine(2 * i, even_ref)
        even_ref[...] = multiply(2 * i + 2)
        combine(2 * i + 1, odd_ref)
        return 0

    lax.fori_loop(0, stations // 2 - 1, body, 0, unroll=7)
    odd_ref[...] = multiply(stations - 1)
    combine(stations - 2, even_ref)
    combine(stations - 1, odd_ref)
    for c in range(LAGS // LANES):
        out_ref[:, c * LANES : (c + 1) * LANES] = total_ref[c].astype(BF16)


def correlate(me, near, far, shifted, extra, segs):
    rows = segs * far.shape[1] // (PH // GROUP)
    count = rows // segs
    stations = shifted.shape[0] // LAGS
    total = shifted.shape[1]
    return pl.pallas_call(
        lambda *refs: correlate_kernel(segs, *refs),
        out_shape=jax.ShapeDtypeStruct((count * stations, LAGS), BF16),
        in_specs=[
            pl.BlockSpec(memory_space=pltpu.SMEM),
            *[pl.BlockSpec(memory_space=pltpu.VMEM)] * (len(near) + 1),
            pl.BlockSpec(memory_space=pltpu.HBM),
            pl.BlockSpec(memory_space=pltpu.HBM),
        ],
        out_specs=pl.BlockSpec(memory_space=pltpu.VMEM),
        scratch_shapes=[
            *whiten_scratch(rows),
            pltpu.VMEM((count * FINE, total), BF16),
            pltpu.VMEM((count, stations * FINE), F32),
            pltpu.VMEM((LAGS // LANES, count * stations, LANES), F32),
            pltpu.VMEM((stations, LAGS, total), BF16),
            pltpu.VMEM((stations * FINE, total), BF16),
            pltpu.VMEM((count * FINE, LAGS), F32),
            pltpu.VMEM((count * FINE, LAGS), F32),
            pltpu.SemaphoreType.DMA((stations + 1,)),
        ],
        compiler_params=pltpu.CompilerParams(vmem_limit_bytes=48 * MIB),
        cost_estimate=pl.CostEstimate(
            flops=6000 * MIB, bytes_accessed=20 * MIB, transcendentals=0
        ),
        name="correlate",
    )(
        me,
        *near,
        far,
        in_hbm(shifted),
        in_hbm(extra),
    )


def on_device(records, owners):
    stations, length = records.shape
    segs, sources = lax.axis_size("seg"), lax.axis_size("sta")
    chips = segs // CORES
    me = lax.axis_index("seg")
    chip = lax.div(me, jnp.int32(CORES))
    along_x = [[(i, (i + k * CORES) % segs) for i in range(segs)] for k in range(chips)]
    across = [(i, i ^ 1) for i in range(segs)]
    phased, slots = prepare(records, owners.T, sources)
    slots = slots.reshape(sources, -1, GROUP * LANES)
    passing = lax.all_to_all(slots, "sta", 0, 0, tiled=True)
    passing = passing.reshape(segs, -1, GROUP * LANES)
    other = lax.ppermute(phased, "seg", across)
    pair = jnp.concatenate([phased, other], axis=0)
    pairs = [pair] + [lax.ppermute(pair, "seg", along_x[k]) for k in STEPS[1:]]
    mine, phases = own_part(me.reshape(1), pairs, segs)
    passing, phases = lax.optimization_barrier((passing, phases))
    shifted, extra = shift(phases)
    near = [passing]
    for k in STEPS[1:]:
        at = ((chip + k) & (chips - 1)) * CORES
        block = lax.dynamic_slice_in_dim(passing, at, CORES, 0)
        near.append(lax.ppermute(block, "seg", along_x[k]))
    near, shifted, extra, mine = lax.optimization_barrier((near, shifted, extra, mine))
    far = lax.ppermute(pack(me.reshape(1), near), "seg", across)
    whitened = in_sample_order(mine)
    result = correlate(me.reshape(1), near, far, shifted, extra, segs)
    return whitened, result.reshape(-1, stations, LAGS)


def solution(mesh):
    return jax.shard_map(
        on_device,
        mesh=mesh,
        in_specs=(P("sta", "seg"), P("sta", None)),
        out_specs=(P("sta", "seg"), P("seg", "sta", None)),
        check_vma=False,
    )
```
